32 devices in a mesh: dp: 16 (over z, y, x), tensor: 2 (over core).
Axes of the slice: x: 2, y: 2, z: 4, core: 2. Of those that a mesh axis runs over, the one named last changes fastest.
Arguments:
- inputs: bfloat16 [8192, 1024], P(('dp', 'tensor')), may hold values from -6 to 6
- segment_ids: int32 [8192], P('dp'), may hold values from 0 to 3, as said below
- positions: int32 [8192], P('dp'), may hold values from 0 to 2047, as said below
- first_gain: float32 [1024], replicated, may hold values from 0.1 to 1.9
- first_shift: float32 [1024], replicated, may hold values from -1.75 to 1.75
- second_gain: float32 [1024], replicated, may hold values from 0.1 to 1.9
- second_shift: float32 [1024], replicated, may hold values from -1.75 to 1.75
- attend_weight: bfloat16 [1024, 3072], P('dp', 'tensor'), may hold values from -0.1875 to 0.1875
- attend_bias: float32 [3072], P('tensor'), may hold values from -1.5 to 1.5
- project_weight: bfloat16 [1024, 1024], P('tensor', 'dp'), may hold values from -0.75 to 0.75
- project_bias: float32 [1024], replicated, may hold values from -1.75 to 1.75
- expand_weight: bfloat16 [1024, 4096], P('dp', 'tensor'), may hold values from -0.1875 to 0.1875
- expand_bias: float32 [4096], P('tensor'), may hold values from -3 to 3
- shrink_weight: bfloat16 [4096, 1024], P('tensor', 'dp'), may hold values from -0.09375 to 0.09375
- shrink_bias: float32 [1024], replicated, may hold values from -1.75 to 1.75
- output_grad: bfloat16 [8192, 1024], P(('dp', 'tensor')), may hold values from -6 to 6
Outputs:
- outputs: bfloat16 [8192, 1024], P(('dp', 'tensor'))
- grad_inputs: bfloat16 [8192, 1024], P(('dp', 'tensor'))
- grad_first_gain: float32 [1024], replicated
- grad_first_shift: float32 [1024], replicated
- grad_second_gain: float32 [1024], replicated
- grad_second_shift: float32 [1024], replicated
- grad_attend_weight: float32 [1024, 3072], P('dp', 'tensor')
- grad_attend_bias: float32 [3072], replicated
- grad_project_weight: float32 [1024, 1024], P('tensor', 'dp')
- grad_project_bias: float32 [1024], replicated
- grad_expand_weight: float32 [1024, 4096], P('dp', 'tensor')
- grad_expand_bias: float32 [4096], replicated
- grad_shrink_weight: float32 [4096, 1024], P('tensor', 'dp')
- grad_shrink_bias: float32 [1024], replicated
The draws below stay inside these ranges and needn't reach their ends.
Inputs may be any that keep to these rules, and one draw needn't show every extreme that they name: `segment_ids`: each sequence, the rows of one index of dp, holds exactly 4 segments numbered 0 to 3 in order, each of one token or more. Within a segment positions rise by one from token to token; in each sequence the first segment starts at position 0 and the last ends at 2047.
All inputs are finite; a program needn't handle non-finite values.
Results may differ from the reference program's by a relative error of at most 0.01.
Values may be sent and summed in bfloat16 or wider, within the bound.
No kernel may reach another device: no remote copies, remote signals or barrier semaphores. Data moves between devices by JAX's collectives and lax.ppermute only.
A program may use at most 128 MiB of HBM per device.

```python
import math
import jax
import jax.numpy as jnp
from jax import lax

D = 1024
HEADS = 16
HD = 64
ROT = 16
FF = 4096
CTX = 2048
SEQ = 512
SEGS = 4
TOKENS = 8192
N_DP = 16


def segment_layout(key):
    sequence_keys = jax.random.split(key, TOKENS // SEQ)

    def one_sequence(seq_key):
        cut_key, offset_key = jax.random.split(seq_key)
        shuffled = jax.random.permutation(cut_key, SEQ - 1) + 1
        cut_points = jnp.sort(shuffled[:SEGS - 1]).astype(jnp.int32)
        starts = jnp.concatenate([jnp.zeros((1,), jnp.int32), cut_points])
        finishes = jnp.concatenate([cut_points, jnp.full((1,), SEQ, jnp.int32)])
        extents = finishes - starts
        offsets = jax.random.randint(offset_key, (SEGS,), 0, CTX - extents + 1).astype(jnp.int32)
        offsets = offsets.at[0].set(0)
        offsets = offsets.at[SEGS - 1].set(CTX - extents[SEGS - 1])
        places = jnp.arange(SEQ, dtype=jnp.int32)
        segment = jnp.sum((cut_points[None, :] <= places[:, None]).astype(jnp.int32), axis=1)
        member = (segment[:, None] == jnp.arange(SEGS, dtype=jnp.int32)[None, :]).astype(jnp.int32)
        position = places + jnp.sum(member * (offsets - starts)[None, :], axis=1)
        return (segment.astype(jnp.int32), position.astype(jnp.int32))
    return jax.vmap(one_sequence)(sequence_keys)


def draw_segment_ids(key, part):
    return segment_layout(jax.random.fold_in(key, 7))[0].reshape(TOKENS)


def draw_positions(key, part):
    return segment_layout(jax.random.fold_in(key, 7))[1].reshape(TOKENS)


def draw_attend_bias(key, part):
    base_key = jax.random.fold_in(key, 13)
    return jnp.clip(0.3 * jax.random.normal(base_key, (3 * D,), jnp.float32), -1.5, 1.5)


def strengthened(array, key, source, target, shards_of, factor):
    owner, partner = [(jnp.arange(array.shape[dim]) // (array.shape[dim] // shards_of)).reshape([-1 if axis == dim else 1 for axis in range(array.ndim)]) for dim in (source, target)]
    chosen = jax.random.permutation(key, shards_of)[partner]
    strong = (owner == chosen) | (owner == (partner + shards_of // 2) % shards_of)
    return jnp.where(strong, factor * array, array)


def level_of(own_key, shape, shards, smallest, largest):
    factor_of, own = 1.0, jax.random.fold_in(own_key, 6)
    for dim, shards_of in shards:
        heights = jnp.exp(jax.random.uniform(jax.random.fold_in(own, dim), (shards_of,), jnp.float32, smallest / len(shards), largest / len(shards)))
        factor_of = factor_of * jnp.repeat(heights, shape[dim] // shards_of).reshape([-1 if axis == dim else 1 for axis in range(len(shape))])
    return factor_of


def gaussian(stream_key, shape, deviation, limit, cuts=(), kind=jnp.bfloat16):
    drawn = jax.random.normal(stream_key, shape, jnp.float32) * deviation
    if len(cuts) > 0:
        drawn = level_of(stream_key, shape, cuts, -0.22, 0.18) * drawn
    return jnp.clip(drawn, min=-limit, max=limit).astype(kind)


def bell_draw_with(stream_key, shape, deviation, bound, shards, heavy, kind=jnp.bfloat16):
    array = deviation * jax.random.normal(stream_key, shape, jnp.float32)
    if shards:
        array = array * level_of(stream_key, shape, shards, -0.22, 0.18)
    return jnp.clip(strengthened(array, jax.random.fold_in(stream_key, 3), *heavy), -bound, bound).astype(kind)


def setup_inputs(seed: int = 0) -> dict:
    seeds = jax.random.split(jax.random.key(seed), 17)
    return {
        "inputs": bell_draw_with(seeds[0], (TOKENS, D), 1.0, 6.0, ((0, 32),), (0, 1, 32, 2.75)),
        "segment_ids": draw_segment_ids(jax.random.fold_in(seeds[16], 71), 0),
        "positions": draw_positions(jax.random.fold_in(seeds[16], 71), 0),
        "first_gain": jnp.clip(1.0 + 0.18 * jax.random.normal(seeds[3], (D,), jnp.float32), 0.1, 1.9),
        "first_shift": gaussian(seeds[4], (D,), 0.3, 1.75, (), jnp.float32),
        "second_gain": jnp.clip(1.0 + 0.18 * jax.random.normal(seeds[5], (D,), jnp.float32), 0.1, 1.9),
        "second_shift": gaussian(seeds[6], (D,), 0.3, 1.75, (), jnp.float32),
        "attend_weight": gaussian(seeds[7], (D, 3 * D), D ** -0.5, 0.1875, ((0, 16), (1, 2))),
        "attend_bias": draw_attend_bias(jax.random.fold_in(seeds[16], 71), 0),
        "project_weight": gaussian(seeds[9], (D, D), (D // 16) ** -0.5, 0.75, ((0, 2), (1, 16))),
        "project_bias": gaussian(seeds[10], (D,), 0.3, 1.75, (), jnp.float32),
        "expand_weight": gaussian(seeds[11], (D, FF), D ** -0.5, 0.1875, ((0, 16), (1, 2))),
        "expand_bias": gaussian(seeds[12], (FF,), 0.5, 3.0, ((0, 2),), jnp.float32),
        "shrink_weight": gaussian(seeds[13], (FF, D), FF ** -0.5, 0.09375, ((0, 2), (1, 16))),
        "shrink_bias": gaussian(seeds[14], (D,), 0.3, 1.75, (), jnp.float32),
        "output_grad": bell_draw_with(seeds[15], (TOKENS, D), 1.0, 6.0, ((0, 32),), (0, 1, 32, 2.75)),
    }


@jax.custom_vjp
def low(v):
    return lax.optimization_barrier(v.astype(jnp.bfloat16)).astype(jnp.float32)

@jax.custom_vjp
def low_back(v):
    return v

def low_keep(v):
    return (low(v), None)

def low_pass(kept, grad):
    return (grad,)

def back_keep(v):
    return (v, None)

def back_low(kept, grad):
    return (low(grad),)
low.defvjp(low_keep, low_pass)
low_back.defvjp(back_keep, back_low)
EPSILON = 1e-05
NEGATIVE = -1e+30
HIGHEST = lax.Precision.HIGHEST

def layer_norm(tokens, gain_vector, shift_vector):
    average = lax.optimization_barrier(jnp.mean(tokens, axis=-1, keepdims=True))
    centred = tokens - average
    variance = lax.optimization_barrier(jnp.mean(centred * centred, axis=-1, keepdims=True))
    return centred * lax.rsqrt(variance + EPSILON) * gain_vector + shift_vector

def rotary_tables(positions, rotated):
    halfway = rotated // 2
    frequency = 1.0 / 10000.0 ** (jnp.arange(halfway, dtype=jnp.float32) * (2.0 / rotated))
    angles = positions.astype(jnp.float32)[:, None] * frequency[None, :]
    return (jnp.cos(angles), jnp.sin(angles))

def rotate(tokens, cosine, sine_table):
    halfway = cosine.shape[-1]
    leading = tokens[..., :halfway]
    trailing = tokens[..., halfway:2 * halfway]
    remainder = tokens[..., 2 * halfway:]
    cos_heads = cosine[:, None, :]
    sin_heads = sine_table[:, None, :]
    return jnp.concatenate([leading * cos_heads - trailing * sin_heads, trailing * cos_heads + leading * sin_heads, remainder], axis=-1)

def attend_group(blocks):
    queries, key_rows, values, segments = blocks
    length = queries.shape[1]
    places = jnp.arange(length)
    products = low_back(jnp.einsum('bqhd,bkhd->bhqk', queries, key_rows, precision=HIGHEST))
    allowed = (places[None, :] <= places[:, None])[None] & (segments[:, :, None] == segments[:, None, :])
    scores = jnp.where(allowed[:, None], products * HD ** (-0.5), NEGATIVE)
    highest = lax.optimization_barrier(jnp.max(scores, axis=-1, keepdims=True))
    numerators = jnp.exp(scores - highest)
    weights = low(numerators / lax.optimization_barrier(jnp.sum(numerators, axis=-1, keepdims=True)))
    return jnp.einsum('bhqk,bkhd->bqhd', weights, values, precision=HIGHEST)

def reference(inputs, segment_ids, positions, first_gain, first_shift, second_gain, second_shift, attend_weight, attend_bias, project_weight, project_bias, expand_weight, expand_bias, shrink_weight, shrink_bias, output_grad):
    per_group = math.gcd(N_DP, max(1, 4096 // SEQ))
    cosine, sine_table = rotary_tables(positions, ROT)
    segments = segment_ids.reshape(N_DP // per_group, per_group, SEQ)
    block_shape = (N_DP // per_group, per_group, SEQ, HEADS, HD)

    def forward(tokens, gain_one, shift_one, gain_two, shift_two, w_attend, b_attend, w_project, b_project, w_expand, b_expand, w_shrink, b_shrink):
        normed_one = low(layer_norm(tokens, gain_one, shift_one))
        normed_two = low(layer_norm(tokens, gain_two, shift_two))
        projected = low_back(jnp.dot(normed_one, w_attend, precision=HIGHEST) + b_attend)
        projected = projected.reshape(TOKENS, HEADS, 3, HD)
        queries = low(rotate(projected[:, :, 0], cosine, sine_table))
        key_rows = low(rotate(projected[:, :, 1], cosine, sine_table))
        values = low(projected[:, :, 2])
        context = lax.map(jax.checkpoint(attend_group), (queries.reshape(block_shape), key_rows.reshape(block_shape), values.reshape(block_shape), segments))
        context = low(low_back(context.reshape(TOKENS, D)))
        hidden = low_back(jnp.dot(normed_two, w_expand, precision=HIGHEST) + b_expand)
        activated = low(jax.nn.gelu(hidden, approximate=False))
        attended = jnp.dot(context, w_project, precision=HIGHEST)
        shrunk = jnp.dot(activated, w_shrink, precision=HIGHEST)
        return tokens + attended + shrunk + b_project + b_shrink
    floats = (inputs.astype(jnp.float32), first_gain, first_shift, second_gain, second_shift, attend_weight.astype(jnp.float32), attend_bias, project_weight.astype(jnp.float32), project_bias, expand_weight.astype(jnp.float32), expand_bias, shrink_weight.astype(jnp.float32), shrink_bias)
    result, pullback = jax.vjp(forward, *floats)
    gradients = pullback(output_grad.astype(jnp.float32))
    return (result.astype(jnp.bfloat16), gradients[0].astype(jnp.bfloat16), gradients[1], gradients[2], gradients[3], gradients[4], gradients[5], gradients[6], gradients[7], gradients[8], gradients[9], gradients[10], gradients[11], gradients[12])
```

```python
import jax
import jax.numpy as jnp
import numpy as np
from jax import lax
from jax.experimental import pallas as pl
from jax.experimental.pallas import tpu as pltpu
from jax.sharding import PartitionSpec as P

HD = 64
ROT = 16
QUAD = 4
EPSILON = 1e-05
NEGATIVE = -1e30
QUERY_BLOCK = 128
ROW_CHUNK = 128
ATTEND_GROUPS = ((0,), (1, 2), (3,))
MLP_GROUPS = ((3, 1), (2, 0))
F32 = jnp.float32
BF16 = jnp.bfloat16


ANY = pl.BlockSpec(memory_space=pl.ANY)
VMEM = pl.BlockSpec(memory_space=pltpu.VMEM)
SMEM = pl.BlockSpec(memory_space=pltpu.SMEM)


def dot_nn(left, right):
    return lax.dot_general(left, right, (((1,), (0,)), ((), ())), preferred_element_type=F32)


def dot_nt(left, right):
    return lax.dot_general(left, right, (((1,), (1,)), ((), ())), preferred_element_type=F32)


def dot_tn(left, right):
    return lax.dot_general(left, right, (((0,), (0,)), ((), ())), preferred_element_type=F32)


def after(value, *others):
    return lax.optimization_barrier((value, others))[0]


def ring_order(count):
    return [0, 1, 3, 2] if count == 4 else list(range(count))


def position_table(n_dp):
    count = n_dp // QUAD
    order = ring_order(count)
    rows = []
    for index in range(n_dp):
        at = order.index(index // QUAD)
        sources = [order[(at - k) % count] for k in range(count)]
        blocks = [order[(at - 1 - k) % count] for k in range(count)]
        rows.append([index % QUAD] + sources + blocks)
    return np.array(rows, np.int32)


def ring_pairs(n_dp):
    count = n_dp // QUAD
    order = ring_order(count)
    pairs = []
    for index in range(n_dp):
        at = order.index(index // QUAD)
        pairs.append((index, order[(at + 1) % count] * QUAD + index % QUAD))
    return pairs


def xor_pairs(n_dp, bits):
    return [(index, index ^ bits) for index in range(n_dp)]


def swap_cores(value):
    return lax.ppermute(value, "tensor", [(0, 1), (1, 0)])


def pack_body(meta, attend, project, expand, shrink, first, second):
    quarter = meta[1]
    heads = attend.shape[1] // QUAD
    context = project.shape[1] // QUAD
    hidden = expand.shape[1] // QUAD
    for j in range(QUAD):
        at = quarter ^ j
        first[j, :, :heads] = attend[:, pl.ds(pl.multiple_of(at * heads, 128), heads)]
        first[j, :, heads:] = project[:, pl.ds(pl.multiple_of(at * context, 128), context)]
        second[j, 0] = expand[:, pl.ds(pl.multiple_of(at * hidden, 128), hidden)]
        second[j, 1] = shrink[:, pl.ds(pl.multiple_of(at * hidden, 128), hidden)]


def pack_weights(meta, attend, project, expand, shrink):
    rows = attend.shape[0]
    width = (attend.shape[1] + project.shape[1]) // QUAD
    hidden = expand.shape[1] // QUAD
    return pl.pallas_call(
        pack_body,
        in_specs=[SMEM] + [VMEM] * 4,
        out_specs=[VMEM] * 2,
        out_shape=[
            jax.ShapeDtypeStruct((QUAD, rows, width), BF16),
            jax.ShapeDtypeStruct((QUAD, 2, rows, hidden), BF16),
        ],
        name="pack_weights",
    )(meta, attend, project, expand, shrink)


def unpack_attend_body(meta, own, *refs):
    received, (attend, project) = refs[:3], refs[3:]
    quarter = meta[1]
    heads = attend.shape[1] // QUAD
    context = project.shape[1] // QUAD
    for j in range(QUAD):
        piece = own[...] if j == 0 else received[j - 1][...].astype(F32)
        at = quarter ^ j
        attend[:, pl.ds(pl.multiple_of(at * heads, 128), heads)] = piece[:, :heads]
        project[:, pl.ds(pl.multiple_of(at * context, 128), context)] = piece[:, heads:]


def unpack_attend(meta, own, received, attend_cols, project_cols):
    rows = own.shape[0]
    return pl.pallas_call(
        unpack_attend_body,
        in_specs=[SMEM] + [VMEM] * 4,
        out_specs=[VMEM] * 2,
        out_shape=[
            jax.ShapeDtypeStruct((rows, attend_cols), F32),
            jax.ShapeDtypeStruct((rows, project_cols), F32),
        ],
        name="unpack_attend",
    )(meta, own, *received)


def unpack_mlp_body(meta, own, *refs):
    received, (expand, shrink) = refs[:3], refs[3:]
    quarter = meta[1]
    hidden = expand.shape[1] // QUAD
    for j in range(QUAD):
        piece = own if j == 0 else received[j - 1]
        lanes = pl.ds(pl.multiple_of((quarter ^ j) * hidden, 128), hidden)
        expand[:, lanes] = piece[0].astype(F32)
        shrink[:, lanes] = piece[1].astype(F32)


def unpack_mlp(meta, own, received, hidden_cols):
    rows = own.shape[1]
    return pl.pallas_call(
        unpack_mlp_body,
        in_specs=[SMEM] + [VMEM] * 4,
        out_specs=[VMEM] * 2,
        out_shape=[jax.ShapeDtypeStruct((rows, hidden_cols), F32)] * 2,
        name="unpack_mlp",
    )(meta, own, *received)


def normalize_rows(tokens, gain, shift):
    average = jnp.mean(tokens, axis=-1, keepdims=True)
    centred = tokens - average
    variance = jnp.mean(centred * centred, axis=-1, keepdims=True)
    scaled = centred * lax.rsqrt(variance + EPSILON)
    return scaled, scaled * gain + shift


def start_tokens(meta, sources, target, sems, slot, half):
    mine = pl.multiple_of(meta[0] * half, half)
    other = pl.multiple_of((1 - meta[0]) * half, half)
    for number, (source, place) in enumerate(zip(sources, (mine, other))):
        pltpu.make_async_copy(
            source, target.at[slot, pl.ds(place, half)], sems.at[number]
        ).start()


def wait_tokens(target, sems, slot, half):
    for number in range(2):
        view = target.at[slot, pl.ds(0, half)]
        pltpu.make_async_copy(view, view, sems.at[number]).wait()


def weight_copies(meta, count, blocks, pick, target, sems):
    rows = blocks[0].shape[-2]
    copies = []
    for k in range(count):
        for j in range(QUAD):
            source = blocks[k].at[j] if pick is None else blocks[k].at[j, pick]
            place = meta[2 + k] * (QUAD * rows) + (meta[1] ^ j) * rows
            copies.append(
                pltpu.make_async_copy(
                    source, target.at[pl.ds(pl.multiple_of(place, rows), rows)], sems.at[k, j]
                )
            )
    return copies


def store_blocks(meta, count, turned, first, rest, pick):
    rows = first.shape[-2]
    for k in range(count):
        for j in range(QUAD):
            place = meta[2 + count + k] * (QUAD * rows) + (meta[1] ^ j) * rows
            piece = turned[pl.ds(pl.multiple_of(place, rows), rows), :]
            at = (j,) if pick is None else (j, pick)
            if k == 0:
                first[at] = piece.astype(BF16)
            else:
                rest[(k - 1,) + at] = piece


def rotate_tile(tile, cosine, sine, lane):
    partner = jnp.where(lane % ROT < ROT // 2, pltpu.roll(tile, 120, 1), pltpu.roll(tile, 8, 1))
    return tile * cosine + partner * sine


def attend_body(n_seq, count, is_first, is_last, *refs):
    refs = list(refs)
    take = lambda number: [refs.pop(0) for _ in range(number)]
    (meta, gain, shift, bias) = take(4)
    tables = take(n_seq)
    tokens = [take(2) for _ in range(n_seq)]
    cotangents = [take(2) for _ in range(n_seq)]
    blocks = take(count)
    carried = [] if is_first else take(2)
    out_hbm, grad_hbm, sums = take(3)
    if is_last:
        grad_first, grad_rest = take(2)
    else:
        (total_hbm,) = take(1)
    x_s, d_s, w_s, total, tab_s = take(5)
    cos_s, sin_s, seg_s, norm_s, hat_s = take(5)
    q_s, k_s, v_s, dctx_s, ctx_s = take(5)
    dq_s, dk_s, dv_s, gm_s, grad_s = take(5)
    out_st, grad_st = take(2)
    turned = take(1)[0] if is_last else None
    token_sem, weight_sem, table_sem, out_sem, total_sem = take(5)

    length = x_s.shape[1]
    half = length // 2
    features = x_s.shape[2]
    heads = gm_s.shape[1]
    scale = HD ** (-0.5)

    copies = weight_copies(meta, count, blocks, None, w_s, weight_sem)
    for i in range(n_seq):
        start_tokens(meta, tokens[i], x_s, token_sem.at[i, 0], i, half)
        start_tokens(meta, cotangents[i], d_s, token_sem.at[i, 1], i, half)
        pltpu.make_async_copy(tables[i], tab_s.at[i], table_sem.at[i]).start()
        if i == 0:
            for copy in copies:
                copy.start()
    if is_first:
        total[...] = jnp.zeros_like(total)
        sums[...] = jnp.zeros_like(sums)
    else:
        load = pltpu.make_async_copy(carried[0], total, total_sem.at[0])
        load.start()
        sums[...] = carried[1][...]

    def one_sequence(i, carry):
        wait_tokens(x_s, token_sem.at[i, 0], i, half)
        pltpu.make_async_copy(tab_s.at[i], tab_s.at[i], table_sem.at[i]).wait()
        for c in range(length // ROW_CHUNK):
            rows = slice(c * ROW_CHUNK, (c + 1) * ROW_CHUNK)
            scaled, normed = normalize_rows(x_s[i, rows, :].astype(F32), gain[...], shift[...])
            hat_s[rows, :] = scaled
            norm_s[rows, :] = normed.astype(BF16)
        cos_t = tab_s[i, 0:8, :]
        sin_t = tab_s[i, 8:16, :]
        plain = jnp.ones((HD - ROT, length), F32)
        nothing = jnp.zeros((HD - ROT, length), F32)
        cos_s[...] = jnp.concatenate([cos_t, cos_t, plain] * 2, axis=0).T
        sin_s[...] = jnp.concatenate([-sin_t, sin_t, nothing] * 2, axis=0).T
        seg_s[...] = jnp.broadcast_to(tab_s[i, 16:17, :], (128, length)).T
        wait_tokens(d_s, token_sem.at[i, 1], i, half)

        @pl.when(i == 0)
        def _():
            for copy in copies:
                copy.wait()

        projected = dot_nn(norm_s[...], w_s[:, :heads]) + bias[...]
        dctx_s[...] = dot_nn(d_s[i], w_s[:, heads:]).astype(BF16)
        lane = lax.broadcasted_iota(jnp.int32, (length, 128), 1)
        low = lane < HD
        cosine, sine = cos_s[...], sin_s[...]
        tiles = [projected[:, k * 128 : (k + 1) * 128] for k in range(3)]
        turned_tiles = [rotate_tile(tile, cosine, sine, lane) for tile in tiles]
        t0 = turned_tiles[0]
        t1 = jnp.where(low, tiles[1], turned_tiles[1])
        t2 = jnp.where(low, turned_tiles[2], tiles[2])
        q_s[0] = t0[:, :HD].astype(BF16)
        k_s[0] = t0[:, HD:].astype(BF16)
        v_s[0] = t1[:, :HD].astype(BF16)
        q_s[1] = t1[:, HD:].astype(BF16)
        k_s[1] = t2[:, :HD].astype(BF16)
        v_s[1] = t2[:, HD:].astype(BF16)

        for h in range(2):
            lanes = slice(h * HD, (h + 1) * HD)
            for block in reversed(range(length // QUERY_BLOCK)):
                rows = slice(block * QUERY_BLOCK, (block + 1) * QUERY_BLOCK)
                width = (block + 1) * QUERY_BLOCK
                query = q_s[h, rows, :]
                key = k_s[h, :width, :]
                value = v_s[h, :width, :]
                dctx = dctx_s[rows, lanes]
                products = dot_nt(query, key) * scale
                at_row = lax.broadcasted_iota(jnp.int32, (QUERY_BLOCK, width), 0)
                at_col = lax.broadcasted_iota(jnp.int32, (QUERY_BLOCK, width), 1)
                own_seg = jnp.concatenate([seg_s[rows, :]] * (width // 128), axis=1)
                allowed = (at_col <= at_row + block * QUERY_BLOCK) & (
                    own_seg == tab_s[i, 16:17, :width]
                )
                scores = jnp.where(allowed, products, NEGATIVE)
                highest = jnp.max(scores, axis=-1, keepdims=True)
                numerators = jnp.exp(scores - highest)
                weights = numerators * (1.0 / jnp.sum(numerators, axis=-1, keepdims=True))
                weights_low = weights.astype(BF16)
                ctx_s[rows, lanes] = dot_nn(weights_low, value).astype(BF16)
                grad_probs = dot_nt(dctx, value)
                centre = jnp.sum(grad_probs * weights, axis=-1, keepdims=True)
                grad_products = (weights * (grad_probs - centre) * scale).astype(BF16)
                dq_s[h, rows, :] = dot_nn(grad_products, key)
                grad_key = dot_tn(grad_products, query)
                grad_value = dot_tn(weights_low, dctx)
                if width == length:
                    dk_s[h, :, :] = grad_key
                    dv_s[h, :, :] = grad_value
                else:
                    dk_s[h, :width, :] += grad_key
                    dv_s[h, :width, :] += grad_value

        tiles = [
            jnp.concatenate([dq_s[0], dk_s[0]], axis=1),
            jnp.concatenate([dv_s[0], dq_s[1]], axis=1),
            jnp.concatenate([dk_s[1], dv_s[1]], axis=1),
        ]
        cosine, sine = cos_s[...], -sin_s[...]
        back = [rotate_tile(tile, cosine, sine, lane) for tile in tiles]
        mixed = [
            back[0],
            jnp.where(low, tiles[1], back[1]),
            jnp.where(low, back[2], tiles[2]),
        ]
        for k in range(3):
            piece = mixed[k].astype(BF16)
            gm_s[:, k * 128 : (k + 1) * 128] = piece
            sums[2:3, k * 128 : (k + 1) * 128] += jnp.sum(
                piece.astype(F32), axis=0, keepdims=True
            )
        out_st[i] = dot_nt(ctx_s[...], w_s[:, heads:]).astype(BF16)
        pltpu.make_async_copy(out_st.at[i], out_hbm.at[i], out_sem.at[i, 0]).start()
        grad_s[...] = dot_nt(gm_s[...], w_s[:, :heads])
        for c in range(length // ROW_CHUNK):
            rows = slice(c * ROW_CHUNK, (c + 1) * ROW_CHUNK)
            grad = grad_s[rows, :]
            sums[0:1, :] += jnp.sum(grad * hat_s[rows, :], axis=0, keepdims=True)
            sums[1:2, :] += jnp.sum(grad, axis=0, keepdims=True)
            grad_st[i, rows, :] = (grad * gain[...]).astype(BF16)
        pltpu.make_async_copy(grad_st.at[i], grad_hbm.at[i], out_sem.at[i, 1]).start()
        if not is_first:

            @pl.when(i == 0)
            def _():
                load.wait()

        total[:heads, :] += dot_tn(gm_s[...], norm_s[...])
        total[heads:, :] += dot_tn(ctx_s[...], d_s[i])
        return carry

    lax.fori_loop(0, n_seq, one_sequence, 0)
    if is_last:
        for c in range(features // 256):
            cols = slice(c * 256, (c + 1) * 256)
            turned[cols, :] = total[:, cols].T
        store_blocks(meta, count, turned, grad_first, grad_rest, None)
    else:
        save = pltpu.make_async_copy(total, total_hbm, total_sem.at[1])
        save.start()
        save.wait()
    for i in range(n_seq):
        pltpu.make_async_copy(out_st.at[i], out_hbm.at[i], out_sem.at[i, 0]).wait()
        pltpu.make_async_copy(grad_st.at[i], grad_hbm.at[i], out_sem.at[i, 1]).wait()


def attend_branch(meta, gain, shift, bias, tables, tokens, cotangents, blocks, carried, is_last):
    n_seq, count, is_first = len(tokens), len(blocks), carried is None
    half, features = tokens[0][0].shape
    length = 2 * half
    rows, width = blocks[0].shape[1:]
    heads = bias.shape[1]
    operands = [meta, gain, shift, bias, *tables]
    specs = [SMEM] + [VMEM] * 3 + [ANY] * n_seq
    for pair in list(tokens) + list(cotangents):
        operands += list(pair)
        specs += [ANY] * 2
    operands += list(blocks)
    specs += [ANY] * count
    if not is_first:
        operands += list(carried)
        specs += [ANY, VMEM]
    whole = jax.ShapeDtypeStruct((n_seq, length, features), BF16)
    shapes = [whole, whole, jax.ShapeDtypeStruct((8, features), F32)]
    out_specs = [ANY, ANY, VMEM]
    if is_last:
        shapes += [
            jax.ShapeDtypeStruct((QUAD, rows, width), BF16),
            jax.ShapeDtypeStruct((count - 1, QUAD, rows, width), F32),
        ]
        out_specs += [VMEM] * 2
    else:
        shapes += [jax.ShapeDtypeStruct((width, features), F32)]
        out_specs += [ANY]
    scratch = [
        pltpu.VMEM((n_seq, length, features), BF16),
        pltpu.VMEM((n_seq, length, features), BF16),
        pltpu.VMEM((features, width), BF16),
        pltpu.VMEM((width, features), F32),
        pltpu.VMEM((n_seq,) + tables[0].shape, F32),
        pltpu.VMEM((length, 128), F32),
        pltpu.VMEM((length, 128), F32),
        pltpu.VMEM((length, 128), F32),
        pltpu.VMEM((length, features), BF16),
        pltpu.VMEM((length, features), F32),
        pltpu.VMEM((2, length, HD), BF16),
        pltpu.VMEM((2, length, HD), BF16),
        pltpu.VMEM((2, length, HD), BF16),
        pltpu.VMEM((length, 2 * HD), BF16),
        pltpu.VMEM((length, 2 * HD), BF16),
        pltpu.VMEM((2, length, HD), F32),
        pltpu.VMEM((2, length, HD), F32),
        pltpu.VMEM((2, length, HD), F32),
        pltpu.VMEM((length, heads), BF16),
        pltpu.VMEM((length, features), F32),
        pltpu.VMEM((n_seq, length, features), BF16),
        pltpu.VMEM((n_seq, length, features), BF16),
    ]
    if is_last:
        scratch += [pltpu.VMEM((features, width), F32)]
    scratch += [
        pltpu.SemaphoreType.DMA((n_seq, 2, 2)),
        pltpu.SemaphoreType.DMA((count, QUAD)),
        pltpu.SemaphoreType.DMA((n_seq,)),
        pltpu.SemaphoreType.DMA((n_seq, 2)),
        pltpu.SemaphoreType.DMA((2,)),
    ]
    flops = n_seq * (6 * length * features * width + 14 * length * length * 2 * HD)
    return pl.pallas_call(
        lambda *refs: attend_body(n_seq, count, is_first, is_last, *refs),
        in_specs=specs,
        out_specs=out_specs,
        out_shape=shapes,
        scratch_shapes=scratch,
        compiler_params=pltpu.CompilerParams(vmem_limit_bytes=40 << 20),
        cost_estimate=pl.CostEstimate(
            flops=flops,
            bytes_accessed=n_seq * 8 * length * features + 10 * width * features,
            transcendentals=n_seq * 2 * length * length,
        ),
        name="attend_branch",
    )(*operands)


def mlp_body(n_seq, count, is_first, is_last, places, *refs):
    refs = list(refs)
    take = lambda number: [refs.pop(0) for _ in range(number)]
    (meta, gain, shift, bias) = take(4)
    tokens = [take(2) for _ in range(n_seq)]
    cotangents = [take(2) for _ in range(n_seq)]
    partials = [take(2) for _ in range(n_seq)]
    blocks = take(count)
    carried = [] if is_first else take(2)
    mine_hbm, other_hbm, sums = take(3)
    if is_last:
        grad_first, grad_rest = take(2)
    else:
        (total_hbm,) = take(1)
    x_s, d_s, w_s, total = take(4)
    norm_s, hat_s, hid_s, act_s, dh_s, grad_s = take(6)
    out_st, grad_st = take(2)
    turned = take(1)[0] if is_last else None
    token_sem, weight_sem, part_sem, out_sem, total_sem = take(5)

    length = x_s.shape[1]
    half = length // 2
    features = x_s.shape[2]
    hidden = w_s.shape[2]

    copies = []
    for pick in range(2):
        copies += weight_copies(meta, count, blocks, pick, w_s.at[pick], weight_sem.at[pick])
    for i in range(n_seq):
        start_tokens(meta, tokens[i], x_s, token_sem.at[i, 0], i, half)
        start_tokens(meta, cotangents[i], d_s, token_sem.at[i, 1], i, half)
        if i == 0:
            for copy in copies:
                copy.start()
        out_part = partials[i][0].at[places[i]]
        grad_part = partials[i][1].at[places[i]]
        pltpu.make_async_copy(out_part, out_st.at[i], part_sem.at[i, 0]).start()
        pltpu.make_async_copy(grad_part, grad_st.at[i], part_sem.at[i, 1]).start()
    if is_first:
        total[...] = jnp.zeros_like(total)
        sums[...] = jnp.zeros_like(sums)
    else:
        load = pltpu.make_async_copy(carried[0], total, total_sem.at[0])
        load.start()
        sums[...] = carried[1][...]

    def send_halves(stage, i, which):
        mine = pl.multiple_of(meta[0] * half, half)
        other = pl.multiple_of((1 - meta[0]) * half, half)
        return [
            pltpu.make_async_copy(
                stage.at[i, pl.ds(mine, half)], mine_hbm.at[i, which], out_sem.at[i, which, 0]
            ),
            pltpu.make_async_copy(
                stage.at[i, pl.ds(other, half)], other_hbm.at[i, which], out_sem.at[i, which, 1]
            ),
        ]

    def one_sequence(i, carry):
        wait_tokens(x_s, token_sem.at[i, 0], i, half)
        for c in range(length // ROW_CHUNK):
            rows = slice(c * ROW_CHUNK, (c + 1) * ROW_CHUNK)
            scaled, normed = normalize_rows(x_s[i, rows, :].astype(F32), gain[...], shift[...])
            hat_s[rows, :] = scaled
            norm_s[rows, :] = normed.astype(BF16)
        wait_tokens(d_s, token_sem.at[i, 1], i, half)

        @pl.when(i == 0)
        def _():
            for copy in copies:
                copy.wait()

        hid_s[0] = dot_nn(norm_s[...], w_s[0]) + bias[...]
        hid_s[1] = dot_nn(d_s[i], w_s[1])
        for c in range(length // ROW_CHUNK):
            rows = slice(c * ROW_CHUNK, (c + 1) * ROW_CHUNK)
            hid = hid_s[0, rows, :]
            below = 0.5 + 0.5 * lax.erf(hid * np.float32(0.5**0.5))
            slope = below + hid * jnp.exp(-0.5 * (hid * hid)) * np.float32((2 * np.pi) ** -0.5)
            act_s[rows, :] = (hid * below).astype(BF16)
            grad_hid = (slope * hid_s[1, rows, :]).astype(BF16)
            dh_s[rows, :] = grad_hid
            sums[2:3, :hidden] += jnp.sum(grad_hid.astype(F32), axis=0, keepdims=True)
        view = out_st.at[i]
        pltpu.make_async_copy(view, view, part_sem.at[i, 0]).wait()
        out_st[i] = (dot_nt(act_s[...], w_s[1]) + out_st[i].astype(F32)).astype(BF16)
        for copy in send_halves(out_st, i, 0):
            copy.start()
        grad_s[...] = dot_nt(dh_s[...], w_s[0])
        view = grad_st.at[i]
        pltpu.make_async_copy(view, view, part_sem.at[i, 1]).wait()
        for c in range(length // ROW_CHUNK):
            rows = slice(c * ROW_CHUNK, (c + 1) * ROW_CHUNK)
            grad = grad_s[rows, :]
            sums[0:1, :] += jnp.sum(grad * hat_s[rows, :], axis=0, keepdims=True)
            sums[1:2, :] += jnp.sum(grad, axis=0, keepdims=True)
            whole = grad * gain[...] + grad_st[i, rows, :].astype(F32)
            grad_st[i, rows, :] = whole.astype(BF16)
        for copy in send_halves(grad_st, i, 1):
            copy.start()
        if not is_first:

            @pl.when(i == 0)
            def _():
                load.wait()

        total[0] += dot_tn(dh_s[...], norm_s[...])
        total[1] += dot_tn(act_s[...], d_s[i])
        return carry

    lax.fori_loop(0, n_seq, one_sequence, 0)
    if is_last:
        for pick in range(2):
            for c in range(features // 256):
                cols = slice(c * 256, (c + 1) * 256)
                turned[cols, :] = total[pick, :, cols].T
            store_blocks(meta, count, turned, grad_first, grad_rest, pick)
    else:
        save = pltpu.make_async_copy(total, total_hbm, total_sem.at[1])
        save.start()
        save.wait()
    for i in range(n_seq):
        for copy in send_halves(out_st, i, 0) + send_halves(grad_st, i, 1):
            copy.wait()


def mlp_branch(meta, gain, shift, bias, tokens, cotangents, partials, blocks, carried, is_last):
    n_seq, count, is_first = len(tokens), len(blocks), carried is None
    half, features = tokens[0][0].shape
    length = 2 * half
    rows, hidden = blocks[0].shape[2:]
    operands = [meta, gain, shift, bias]
    specs = [SMEM] + [VMEM] * 3
    for pair in list(tokens) + list(cotangents) + [part[:2] for part in partials]:
        operands += list(pair)
        specs += [ANY] * 2
    places = [part[2] for part in partials]
    operands += list(blocks)
    specs += [ANY] * count
    if not is_first:
        operands += list(carried)
        specs += [ANY, VMEM]
    split = jax.ShapeDtypeStruct((n_seq, 2, half, features), BF16)
    shapes = [split, split, jax.ShapeDtypeStruct((8, features), F32)]
    out_specs = [ANY, ANY, VMEM]
    if is_last:
        shapes += [
            jax.ShapeDtypeStruct((QUAD, 2, rows, hidden), BF16),
            jax.ShapeDtypeStruct((count - 1, QUAD, 2, rows, hidden), F32),
        ]
        out_specs += [VMEM] * 2
    else:
        shapes += [jax.ShapeDtypeStruct((2, hidden, features), F32)]
        out_specs += [ANY]
    scratch = [
        pltpu.VMEM((n_seq, length, features), BF16),
        pltpu.VMEM((n_seq, length, features), BF16),
        pltpu.VMEM((2, features, hidden), BF16),
        pltpu.VMEM((2, hidden, features), F32),
        pltpu.VMEM((length, features), BF16),
        pltpu.VMEM((length, features), F32),
        pltpu.VMEM((2, length, hidden), F32),
        pltpu.VMEM((length, hidden), BF16),
        pltpu.VMEM((length, hidden), BF16),
        pltpu.VMEM((length, features), F32),
        pltpu.VMEM((n_seq, length, features), BF16),
        pltpu.VMEM((n_seq, length, features), BF16),
    ]
    if is_last:
        scratch += [pltpu.VMEM((features, hidden), F32)]
    scratch += [
        pltpu.SemaphoreType.DMA((n_seq, 2, 2)),
        pltpu.SemaphoreType.DMA((2, count, QUAD)),
        pltpu.SemaphoreType.DMA((n_seq, 2)),
        pltpu.SemaphoreType.DMA((n_seq, 2, 2)),
        pltpu.SemaphoreType.DMA((2,)),
    ]
    return pl.pallas_call(
        lambda *refs: mlp_body(n_seq, count, is_first, is_last, places, *refs),
        in_specs=specs,
        out_specs=out_specs,
        out_shape=shapes,
        scratch_shapes=scratch,
        compiler_params=pltpu.CompilerParams(vmem_limit_bytes=44 << 20),
        cost_estimate=pl.CostEstimate(
            flops=n_seq * 12 * length * features * hidden,
            bytes_accessed=n_seq * 12 * length * features + 20 * hidden * features,
            transcendentals=n_seq * 2 * length * hidden,
        ),
        name="mlp_branch",
    )(*operands)


def finish_body(x, d, own, p1, p2, p3, first_bias, second_bias, out, grad):
    tokens = x[...].astype(F32)
    branches = own[0].astype(F32) + p1[0].astype(F32) + p2[0].astype(F32) + p3[0].astype(F32)
    out[...] = (tokens + branches + first_bias[...] + second_bias[...]).astype(BF16)
    back = own[1].astype(F32) + p1[1].astype(F32) + p2[1].astype(F32) + p3[1].astype(F32)
    average = jnp.mean(tokens, axis=-1, keepdims=True)
    centred = tokens - average
    inverse = lax.rsqrt(jnp.mean(centred * centred, axis=-1, keepdims=True) + EPSILON)
    scaled = centred * inverse
    level = jnp.mean(back, axis=-1, keepdims=True)
    along = jnp.mean(back * scaled, axis=-1, keepdims=True)
    grad[...] = (d[...].astype(F32) + (back - level - scaled * along) * inverse).astype(BF16)


def finish(x, d, own, parts, first_bias, second_bias):
    rows, features = x.shape
    block = min(rows, 64)
    flat = pl.BlockSpec((block, features), lambda i: (i, 0))
    pair = pl.BlockSpec((2, block, features), lambda i: (0, i, 0))
    row = pl.BlockSpec((1, features), lambda i: (0, 0))
    return pl.pallas_call(
        finish_body,
        grid=(rows // block,),
        in_specs=[flat, flat, pair, pair, pair, pair, row, row],
        out_specs=[flat, flat],
        out_shape=[jax.ShapeDtypeStruct((rows, features), BF16)] * 2,
        name="finish",
    )(x, d, own, *parts, first_bias, second_bias)


def on_device(
    n_dp,
    inputs,
    segment_ids,
    positions,
    first_gain,
    first_shift,
    second_gain,
    second_shift,
    attend_weight,
    attend_bias,
    project_weight,
    project_bias,
    expand_weight,
    expand_bias,
    shrink_weight,
    shrink_bias,
    output_grad,
):
    count = n_dp // QUAD
    features = inputs.shape[1]
    attend_cols, hidden_cols = attend_weight.shape[1], expand_weight.shape[1]
    project_cols = project_weight.shape[0]
    core = lax.axis_index("tensor")
    dp_at = lax.axis_index("dp")
    table = lax.dynamic_slice_in_dim(jnp.asarray(position_table(n_dp)), dp_at, 1, 0)[0]
    meta = jnp.concatenate([core.astype(jnp.int32)[None], table])
    quarter = meta[1]
    along = ring_pairs(n_dp)
    hop = [xor_pairs(n_dp, bits) for bits in range(QUAD)]

    def to_quad(value, j):
        return lax.ppermute(value, "dp", hop[j])

    first_pack, second_pack = pack_weights(
        meta, attend_weight, project_weight.T, expand_weight, shrink_weight.T
    )
    first_parts = [first_pack[0]] + [to_quad(first_pack[j], j) for j in range(1, QUAD)]
    first_blocks = [jnp.stack(first_parts)]
    second_pack = after(second_pack, *first_parts)
    second_parts = [second_pack[0]] + [to_quad(second_pack[j], j) for j in range(1, QUAD)]
    for _ in range(1, count):
        first_blocks.append(lax.ppermute(first_blocks[-1], "dp", along))
    second_blocks = [after(jnp.stack(second_parts), first_blocks[-1])]
    for _ in range(1, count):
        second_blocks.append(lax.ppermute(second_blocks[-1], "dp", along))

    halfway = ROT // 2
    frequency = 1.0 / 10000.0 ** (jnp.arange(halfway, dtype=F32) * (2.0 / ROT))
    angles = frequency[:, None] * positions.astype(F32)[None, :]
    segments = jnp.broadcast_to(segment_ids.astype(F32)[None], angles.shape)
    tables = [jnp.concatenate([jnp.cos(angles), jnp.sin(angles), segments], axis=0)]
    tables += [to_quad(tables[0], j) for j in range(1, QUAD)]

    early_x, early_d = after((inputs, output_grad), *second_parts)
    rows_x = [inputs, to_quad(early_x, 1), to_quad(early_x, 2)]
    rows_d = [output_grad, to_quad(early_d, 1), to_quad(early_d, 2)]
    late_x, late_d = after((inputs, output_grad), *rows_x[1:], *rows_d[1:])
    rows_x.append(to_quad(late_x, 3))
    rows_d.append(to_quad(late_d, 3))
    tokens = [(value, swap_cores(value)) for value in rows_x]
    cotangents = [(value, swap_cores(value)) for value in rows_d]

    one_row = lambda vector: vector[None, :]
    bias_part = lax.dynamic_index_in_dim(
        attend_bias.reshape(QUAD, attend_cols // QUAD), quarter, 0, True
    )
    hidden_part = lax.dynamic_index_in_dim(
        expand_bias.reshape(QUAD, hidden_cols // QUAD), quarter, 0, True
    )

    carried, partials = None, {}
    for group in ATTEND_GROUPS:
        is_last = group is ATTEND_GROUPS[-1]
        results = attend_branch(
            meta,
            one_row(first_gain),
            one_row(first_shift),
            bias_part,
            [tables[s] for s in group],
            [tokens[s] for s in group],
            [cotangents[s] for s in group],
            first_blocks,
            carried,
            is_last,
        )
        for place, s in enumerate(group):
            partials[s] = (results[0], results[1], place)
        attend_sums = results[2]
        carried = (results[3], attend_sums)
    attend_first, attend_rest = results[3:]

    carried, sums_of = None, {}
    for group in MLP_GROUPS:
        is_last = group is MLP_GROUPS[-1]
        results = mlp_branch(
            meta,
            one_row(second_gain),
            one_row(second_shift),
            hidden_part,
            [tokens[s] for s in group],
            [cotangents[s] for s in group],
            [partials[s] for s in group],
            second_blocks,
            carried,
            is_last,
        )
        mine, other = results[:2]
        other = swap_cores(other)
        for place, s in enumerate(group):
            both = mine[place].astype(F32) + other[place].astype(F32)
            sums_of[s] = both.astype(BF16)
        mlp_sums = results[2]
        carried = (results[3], mlp_sums)
    mlp_first, mlp_rest = results[3:]

    parts = [to_quad(sums_of[j], j) for j in range(1, QUAD)]
    outputs, grad_inputs = finish(
        inputs, output_grad, sums_of[0], parts, one_row(project_bias), one_row(shrink_bias)
    )

    def reduce_ring(first, rest):
        running = first
        for k in range(count - 1):
            total = lax.ppermute(running, "dp", along).astype(F32) + rest[k]
            running = total.astype(BF16)
        return total[0], [to_quad(running[j], j) for j in range(1, QUAD)]

    own, received = reduce_ring(attend_first, attend_rest)
    grad_attend, grad_project = unpack_attend(meta, own, received, attend_cols, project_cols)
    own, received = reduce_ring(mlp_first, mlp_rest)
    grad_expand, grad_shrink = unpack_mlp(meta, own, received, hidden_cols)

    place = core * QUAD + quarter
    attend_full = lax.dynamic_update_slice_in_dim(
        jnp.zeros((2 * attend_cols,), F32),
        attend_sums[2, : attend_cols // QUAD],
        place * (attend_cols // QUAD),
        0,
    )
    hidden_full = lax.dynamic_update_slice_in_dim(
        jnp.zeros((2 * hidden_cols,), F32),
        mlp_sums[2, : hidden_cols // QUAD],
        place * (hidden_cols // QUAD),
        0,
    )
    vector = jnp.concatenate(
        [
            attend_sums[:2].reshape(-1),
            mlp_sums[:2].reshape(-1),
            jnp.sum(output_grad.astype(F32), axis=0),
            attend_full,
            hidden_full,
        ]
    ).reshape(-1, 128)
    vector = vector + swap_cores(vector)
    bit = 1
    while bit < n_dp:
        vector = vector + lax.ppermute(vector, "dp", xor_pairs(n_dp, bit))
        bit *= 2
    vector = vector.reshape(-1)
    pieces, at = [], 0
    for size in [features] * 5 + [2 * attend_cols, 2 * hidden_cols]:
        pieces.append(vector[at : at + size])
        at += size
    return (
        outputs,
        grad_inputs,
        pieces[0],
        pieces[1],
        pieces[2],
        pieces[3],
        grad_attend,
        pieces[5],
        grad_project.T,
        pieces[4],
        grad_expand,
        pieces[6],
        grad_shrink.T,
        pieces[4],
    )


def solution(mesh):
    n_dp = mesh.shape["dp"]
    assert mesh.shape["tensor"] == 2 and n_dp % QUAD == 0 and n_dp & (n_dp - 1) == 0
    rows = P(("dp", "tensor"), None)
    in_specs = (
        rows,
        P("dp"),
        P("dp"),
        P(),
        P(),
        P(),
        P(),
        P("dp", "tensor"),
        P("tensor"),
        P("tensor", "dp"),
        P(),
        P("dp", "tensor"),
        P("tensor"),
        P("tensor", "dp"),
        P(),
        rows,
    )
    out_specs = (
        rows,
        rows,
        P(),
        P(),
        P(),
        P(),
        P("dp", "tensor"),
        P(),
        P("tensor", "dp"),
        P(),
        P("dp", "tensor"),
        P(),
        P("tensor", "dp"),
        P(),
    )
    return jax.shard_map(
        lambda *args: on_device(n_dp, *args),
        mesh=mesh,
        in_specs=in_specs,
        out_specs=out_specs,
        check_vma=False,
    )
```

```python
import jax
import jax.numpy as jnp
import numpy as np
from jax import lax
from jax.experimental import pallas as pl
from jax.experimental.pallas import tpu as pltpu
from jax.sharding import PartitionSpec as P


HD = 64
ROT = 16
QUAD = 4
TABLE_ROWS = 32
EPSILON = 1e-05
NEGATIVE = -1e30
QUERY_BLOCK = 256
ROW_CHUNK = 32
ATTEND_GROUPS = ((0,), (1, 2), (3,))
MLP_GROUPS = ((3,), (1,), (2, 0))
F32 = jnp.float32
BF16 = jnp.bfloat16


HBM = pl.BlockSpec(memory_space=pltpu.HBM)
VMEM = pl.BlockSpec(memory_space=pltpu.VMEM)
SMEM = pl.BlockSpec(memory_space=pltpu.SMEM)


def dot_nn(left, right):
    return lax.dot_general(left, right, (((1,), (0,)), ((), ())), preferred_element_type=F32)


def dot_nt(left, right):
    return lax.dot_general(left, right, (((1,), (1,)), ((), ())), preferred_element_type=F32)


def dot_tn(left, right):
    return lax.dot_general(left, right, (((0,), (0,)), ((), ())), preferred_element_type=F32)


def xor_pairs(n_dp, bits):
    return [(index, index ^ bits) for index in range(n_dp)]


def swap_cores(value):
    return lax.ppermute(value, "tensor", [(0, 1), (1, 0)])


def low_parts(value, number):
    parts = []
    for _ in range(number):
        part = lax.reduce_precision(value, 8, 7)
        parts.append(part.astype(BF16))
        value = value - part
    return parts


def pack_body(meta, attend, project, expand, shrink, *outs):
    first, second = outs[:QUAD], outs[QUAD:]
    quarter = meta[1]
    heads = attend.shape[1] // QUAD
    context = project.shape[1] // QUAD
    hidden = expand.shape[1] // QUAD
    for j in range(QUAD):
        at = quarter ^ j
        first[j][:, :heads] = attend[:, pl.ds(pl.multiple_of(at * heads, 128), heads)]
        first[j][:, heads:] = project[:, pl.ds(pl.multiple_of(at * context, 128), context)]
        second[j][0] = expand[:, pl.ds(pl.multiple_of(at * hidden, 128), hidden)]
        second[j][1] = shrink[:, pl.ds(pl.multiple_of(at * hidden, 128), hidden)]


def pack_weights(meta, attend, project, expand, shrink):
    rows = attend.shape[0]
    width = (attend.shape[1] + project.shape[1]) // QUAD
    hidden = expand.shape[1] // QUAD
    parts = pl.pallas_call(
        pack_body,
        in_specs=[SMEM] + [VMEM] * 4,
        out_specs=[VMEM] * (2 * QUAD),
        out_shape=[jax.ShapeDtypeStruct((rows, width), BF16)] * QUAD
        + [jax.ShapeDtypeStruct((2, rows, hidden), BF16)] * QUAD,
        name="pack_weights",
    )(meta, attend, project, expand, shrink)
    return parts[:QUAD], parts[QUAD:]


def join_body(*refs):
    parts, message = refs[:-1], refs[-1]
    at = 0
    for part in parts:
        message[at : at + part.shape[0]] = part[...]
        at += part.shape[0]


def join_message(*parts):
    rows = sum(part.shape[0] for part in parts)
    return pl.pallas_call(
        join_body,
        in_specs=[VMEM] * len(parts),
        out_specs=VMEM,
        out_shape=jax.ShapeDtypeStruct((rows, parts[0].shape[1]), BF16),
        name="join_message",
    )(*parts)


def unpack_attend_body(meta, own, *refs):
    received, (attend, project) = refs[:3], refs[3:]
    quarter = meta[1]
    heads = attend.shape[1] // QUAD
    context = project.shape[1] // QUAD
    for j in range(QUAD):
        piece = own[...] if j == 0 else received[j - 1][...].astype(F32)
        at = quarter ^ j
        attend[:, pl.ds(pl.multiple_of(at * heads, 128), heads)] = piece[:, :heads]
        project[:, pl.ds(pl.multiple_of(at * context, 128), context)] = piece[:, heads:]


def unpack_attend(meta, own, received, attend_cols, project_cols):
    rows = own.shape[0]
    return pl.pallas_call(
        unpack_attend_body,
        in_specs=[SMEM] + [VMEM] * 4,
        out_specs=[VMEM] * 2,
        out_shape=[
            jax.ShapeDtypeStruct((rows, attend_cols), F32),
            jax.ShapeDtypeStruct((rows, project_cols), F32),
        ],
        name="unpack_attend",
    )(meta, own, *received)


def unpack_mlp_body(meta, own, *refs):
    received, (expand, shrink) = refs[:3], refs[3:]
    quarter = meta[1]
    hidden = expand.shape[1] // QUAD
    for j in range(QUAD):
        piece = own if j == 0 else received[j - 1]
        lanes = pl.ds(pl.multiple_of((quarter ^ j) * hidden, 128), hidden)
        expand[:, lanes] = piece[0].astype(F32)
        shrink[:, lanes] = piece[1].astype(F32)


def unpack_mlp(meta, own, received, hidden_cols):
    rows = own.shape[1]
    return pl.pallas_call(
        unpack_mlp_body,
        in_specs=[SMEM] + [VMEM] * 4,
        out_specs=[VMEM] * 2,
        out_shape=[jax.ShapeDtypeStruct((rows, hidden_cols), F32)] * 2,
        name="unpack_mlp",
    )(meta, own, *received)


def row_chunks(length):
    return [slice(c * ROW_CHUNK, (c + 1) * ROW_CHUNK) for c in range(length // ROW_CHUNK)]


def column_chunks(features):
    return [slice(c * 256, (c + 1) * 256) for c in range(features // 256)]


def wait_bytes(view, sem):
    pltpu.make_async_copy(view, view, sem).wait()


def widen(tile, features):
    return jnp.concatenate([tile] * (features // 128), axis=1)


def fold_rows(value):
    return jnp.sum(value.reshape(value.shape[0] // 8, 8, value.shape[1]), axis=0)


def fold_lanes(value):
    tiles = [value[:, k * 128 : (k + 1) * 128] for k in range(value.shape[1] // 128)]
    while len(tiles) > 1:
        tiles = [sum(tiles[k : k + 2]) for k in range(0, len(tiles), 2)]
    return tiles[0]


def normalize(x, gain, shift, norm_s, hat_s):
    length, features = x.shape
    share = np.float32(1.0 / features)

    def some_rows(number, carry):
        for part in range(4):
            at = pl.multiple_of((number * 4 + part) * ROW_CHUNK, ROW_CHUNK)
            rows = pl.ds(at, ROW_CHUNK)
            tokens = x[rows, :].astype(F32)
            centred = tokens - jnp.sum(fold_lanes(tokens), axis=-1, keepdims=True) * share
            variance = jnp.sum(fold_lanes(centred * centred), axis=-1, keepdims=True) * share
            scaled = centred * lax.rsqrt(variance + EPSILON)
            hat_s[rows, :] = scaled
            norm_s[rows, :] = (scaled * gain[...] + shift[...]).astype(BF16)
        return carry

    lax.fori_loop(0, length // (4 * ROW_CHUNK), some_rows, 0)


def rotate_rows(part, cosine, sine):
    half = ROT // 2
    lead, trail = part[:half], part[half:ROT]
    return jnp.concatenate(
        [lead * cosine - trail * sine, trail * cosine + lead * sine, part[ROT:]], axis=0
    )


class Attend:
    picks = (None,)
    turns = True

    @staticmethod
    def scratch(length, features, width):
        return {
            "mask": pltpu.VMEM((length // QUERY_BLOCK, length, QUERY_BLOCK), F32),
            "q": pltpu.VMEM((2, 2 * HD, length), BF16),
            "d": pltpu.VMEM((2, 2 * HD, length), BF16),
            "kv": pltpu.VMEM((2, length, 2 * HD), BF16),
            "kvt": pltpu.VMEM((2, 2 * HD, length), BF16),
            "dq": pltpu.VMEM((2, HD, length), F32),
            "dk": pltpu.VMEM((2, HD, length), F32),
            "dv": pltpu.VMEM((2, HD, length), F32),
            "ctxt": pltpu.VMEM((2 * HD, length), BF16),
            "ctx": pltpu.VMEM((length, 2 * HD), BF16),
            "gmt": pltpu.VMEM((6 * HD, length), BF16),
            "gm": pltpu.VMEM((length, 6 * HD), BF16),
        }

    @staticmethod
    def bias_shape(width):
        return (6 * HD, 128)

    @staticmethod
    def cost(length, features, width):
        return 6 * length * features * width + 14 * length * length * 2 * HD, 2 * length**2

    @staticmethod
    def compute(m, norm, cot, w, bias, bias_sums, table):
        length = norm.shape[0]
        heads = 6 * HD
        scale = np.float32(HD ** (-0.5))
        values = sum(table[k * 8 : (k + 1) * 8, :].astype(F32) for k in range(3))
        cosine, sine = values[:, :length], values[:, length:]
        start = table[24:25, :length].astype(F32) * 256.0 + table[24:25, length:].astype(F32)
        for block in range(length // QUERY_BLOCK):
            width = (block + 1) * QUERY_BLOCK
            lanes = slice(block * QUERY_BLOCK, width)
            key_at = lax.broadcasted_iota(jnp.int32, (width, QUERY_BLOCK), 0)
            query_at = lax.broadcasted_iota(jnp.int32, (width, QUERY_BLOCK), 1)
            first = start[:, lanes].astype(jnp.int32)
            allowed = (key_at >= first) & (key_at <= query_at + block * QUERY_BLOCK)
            m["mask"][block, :width, :] = jnp.where(allowed, 0.0, NEGATIVE)

        projected = dot_nt(w[:heads, :], norm[...]) + widen(bias[...], length)
        grad_context = dot_nt(w[heads:, :], cot[...]).astype(BF16)
        nothing = jnp.zeros((HD, length), BF16)
        for h in range(2):
            query, key, value = [
                projected[(3 * h + k) * HD : (3 * h + k + 1) * HD] for k in range(3)
            ]
            m["q"][h, :HD, :] = (rotate_rows(query, cosine, sine) * scale).astype(BF16)
            m["q"][h, HD:, :] = nothing
            m["d"][h, :HD, :] = nothing
            m["d"][h, HD:, :] = grad_context[h * HD : (h + 1) * HD]
            both = jnp.concatenate([rotate_rows(key, cosine, sine), value], axis=0).astype(BF16)
            m["kvt"][h] = both
            m["kv"][h] = both.T

        for block in reversed(range(length // QUERY_BLOCK)):
            width = (block + 1) * QUERY_BLOCK
            lanes = slice(block * QUERY_BLOCK, width)
            for h in range(2):
                key_value = m["kv"][h, :width, :]
                scores = dot_nn(key_value, m["q"][h, :, lanes]) + m["mask"][block, :width, :]
                highest = jnp.max(scores, axis=0, keepdims=True)
                numerators = jnp.exp(scores - highest)
                weights = numerators * (1.0 / jnp.sum(numerators, axis=0, keepdims=True))
                weights_low = weights.astype(BF16)
                context = dot_nn(m["kvt"][h, HD:, :width], weights_low)
                m["ctxt"][h * HD : (h + 1) * HD, lanes] = context.astype(BF16)
                grad_probs = dot_nn(key_value, m["d"][h, :, lanes])
                centre = jnp.sum(grad_probs * weights, axis=0, keepdims=True)
                grad_products = (weights * (grad_probs - centre)).astype(BF16)
                grad_query = dot_nn(m["kvt"][h, :HD, :width], grad_products)
                m["dq"][h, :, lanes] = grad_query * scale
                grad_key = dot_nt(m["q"][h, :HD, lanes], grad_products)
                grad_value = dot_nt(m["d"][h, HD:, lanes], weights_low)
                if width == length:
                    m["dk"][h] = grad_key
                    m["dv"][h] = grad_value
                else:
                    m["dk"][h, :, :width] += grad_key
                    m["dv"][h, :, :width] += grad_value

        for h in range(2):
            parts = [
                rotate_rows(m["dq"][h], cosine, -sine),
                rotate_rows(m["dk"][h], cosine, -sine),
                m["dv"][h],
            ]
            for k, part in enumerate(parts):
                rows = slice((3 * h + k) * HD, (3 * h + k + 1) * HD)
                low = part.astype(BF16)
                m["gmt"][rows, :] = low
                bias_sums[rows, :] += fold_lanes(low.astype(F32))
        m["gm"][...] = m["gmt"][...].T
        m["ctx"][...] = m["ctxt"][...].T

    @staticmethod
    def accumulate(m, norm, cot, total):
        heads = 6 * HD
        total[0, :heads, :] += dot_nn(m["gmt"][...], norm[...])
        total[0, heads:, :] += dot_nn(m["ctxt"][...], cot[...])

    @staticmethod
    def forward_out(m, w, cols):
        return dot_nn(m["ctx"][...], w[6 * HD :, cols])

    @staticmethod
    def backward_out(m, w, cols):
        return dot_nn(m["gm"][...], w[: 6 * HD, cols])


class Mlp:
    picks = (0, 1)
    turns = False

    @staticmethod
    def scratch(length, features, width):
        return {
            "hid": pltpu.VMEM((2, length, width), F32),
            "act": pltpu.VMEM((length, width), BF16),
            "dh": pltpu.VMEM((length, width), BF16),
        }

    @staticmethod
    def bias_shape(width):
        return (8, width)

    @staticmethod
    def cost(length, features, width):
        return 12 * length * features * width, 2 * length * width

    @staticmethod
    def compute(m, norm, cot, w, bias, bias_sums, table):
        m["hid"][0] = dot_nn(norm[...], w[0]) + bias[...]
        m["hid"][1] = dot_nn(cot[...], w[1])
        for rows in row_chunks(norm.shape[0]):
            hid = m["hid"][0, rows, :]
            below = 0.5 + 0.5 * lax.erf(hid * np.float32(0.5**0.5))
            slope = below + hid * jnp.exp(-0.5 * (hid * hid)) * np.float32((2 * np.pi) ** -0.5)
            m["act"][rows, :] = (hid * below).astype(BF16)
            grad_hid = (slope * m["hid"][1, rows, :]).astype(BF16)
            m["dh"][rows, :] = grad_hid
            bias_sums[...] += fold_rows(grad_hid.astype(F32))

    @staticmethod
    def accumulate(m, norm, cot, total):
        total[0] += dot_tn(m["dh"][...], norm[...])
        total[1] += dot_tn(m["act"][...], cot[...])

    @staticmethod
    def forward_out(m, w, cols):
        return dot_nt(m["act"][...], w[1, cols, :])

    @staticmethod
    def backward_out(m, w, cols):
        return dot_nt(m["dh"][...], w[0, cols, :])


def branch_body(kind, names, n_seq, count, is_first, is_last, places, *refs):
    refs = list(refs)
    take = lambda number: [refs.pop(0) for _ in range(number)]
    (meta, gain, shift, bias) = take(4)
    messages = [take(2) for _ in range(n_seq)]
    partials = [take(2) for _ in places or ()]
    reads_turned = kind.turns and not is_first
    blocks = take(1 if reads_turned else count)
    carried = [] if is_first else take(3)
    out_hbm, grad_hbm, sums, bias_sums = take(4)
    if is_last:
        grad_send, grad_keep = take(2)
    else:
        (total_hbm,) = take(1)
        if kind.turns:
            (turned_hbm,) = take(1) if is_first else (None,)
    x_s, d_s, tab_s, w_s, total, norm_s, hat_s, out_st, grad_st = take(9)
    wt_s = take(1)[0] if kind.turns else None
    turned = take(1)[0] if is_last else None
    m = dict(zip(names, take(len(names))))
    token_sem, table_sem, weight_sem, part_sem, out_sem, total_sem = take(6)

    length, features = x_s.shape[1:]
    half = length // 2
    mine = pl.multiple_of(meta[0] * half, half)
    other = pl.multiple_of((1 - meta[0]) * half, half)
    rows = features // (QUAD * count)

    weight_copies = []
    if reads_turned:
        weight_copies.append(pltpu.make_async_copy(blocks[0], wt_s, weight_sem.at[0, 0, 0]))
    else:
        for k in range(count):
            for j in range(QUAD):
                place = (meta[2] ^ k) * (QUAD * rows) + (meta[1] ^ j) * rows
                for number, pick in enumerate(kind.picks):
                    source = blocks[k].at[j] if pick is None else blocks[k].at[j, pick]
                    target = w_s.at[number, pl.ds(pl.multiple_of(place, rows), rows)]
                    weight_copies.append(
                        pltpu.make_async_copy(source, target, weight_sem.at[number, k, j])
                    )
    for i in range(n_seq):
        for target, first, which in ((x_s, 0, 0), (d_s, half, 1)):
            for number, place in enumerate((mine, other)):
                pltpu.make_async_copy(
                    messages[i][number].at[pl.ds(first, half)],
                    target.at[i, pl.ds(place, half)],
                    token_sem.at[i, which, number],
                ).start()
        if kind.turns:
            pltpu.make_async_copy(
                messages[i][0].at[pl.ds(2 * half, TABLE_ROWS)], tab_s.at[i], table_sem.at[i]
            ).start()
        if i == 0:
            for copy in weight_copies:
                copy.start()
        if places:
            for number, stage in enumerate((out_st, grad_st)):
                pltpu.make_async_copy(
                    partials[i][number].at[places[i]], stage.at[i], part_sem.at[i, number]
                ).start()
    if is_first:
        total[...] = jnp.zeros_like(total)
        sums[...] = jnp.zeros_like(sums)
        bias_sums[...] = jnp.zeros_like(bias_sums)
    else:
        load = pltpu.make_async_copy(carried[0], total, total_sem.at[0])
        load.start()
        sums[...] = carried[1][...]
        bias_sums[...] = carried[2][...]
    saves = []
    if not is_last:
        saves.append(pltpu.make_async_copy(total, total_hbm, total_sem.at[1]))
        if kind.turns and is_first:
            keep = pltpu.make_async_copy(wt_s, turned_hbm, total_sem.at[2])

    def stores(stage, i, which):
        if not places:
            target = (out_hbm, grad_hbm)[which]
            return [pltpu.make_async_copy(stage.at[i], target.at[i], out_sem.at[i, which, 0])]
        return [
            pltpu.make_async_copy(
                stage.at[i, pl.ds(place, half)], target.at[i, which], out_sem.at[i, which, number]
            )
            for number, (place, target) in enumerate(((mine, out_hbm), (other, grad_hbm)))
        ]

    def one_sequence(i, carry):
        for number in range(2):
            wait_bytes(x_s.at[i, pl.ds(0, half)], token_sem.at[i, 0, number])
        normalize(x_s.at[i], gain, shift, norm_s, hat_s)
        if kind.turns:
            wait_bytes(tab_s.at[i], table_sem.at[i])
        for number in range(2):
            wait_bytes(d_s.at[i, pl.ds(0, half)], token_sem.at[i, 1, number])

        @pl.when(i == 0)
        def _():
            for copy in weight_copies:
                copy.wait()
            if kind.turns and is_first:
                for cols in column_chunks(features):
                    wt_s[:, cols] = w_s[0, cols, :].T
                if not is_last:
                    keep.start()

        cot = d_s.at[i]
        w = wt_s if kind.turns else w_s
        kind.compute(m, norm_s, cot, w, bias, bias_sums, tab_s.at[i])
        if not is_first:

            @pl.when(i == 0)
            def _():
                load.wait()

        kind.accumulate(m, norm_s, cot, total)
        if not is_last:

            @pl.when(i == n_seq - 1)
            def _():
                for copy in saves:
                    copy.start()

        if places:
            wait_bytes(out_st.at[i], part_sem.at[i, 0])
            wait_bytes(grad_st.at[i], part_sem.at[i, 1])
        for cols in column_chunks(features):
            out = kind.forward_out(m, w, cols)
            if places:
                out = out + out_st[i, :, cols].astype(F32)
            out_st[i, :, cols] = out.astype(BF16)
        for copy in stores(out_st, i, 0):
            copy.start()
        for cols in column_chunks(features):
            grad = kind.backward_out(m, w, cols)
            sums[0:8, cols] += fold_rows(grad * hat_s[:, cols])
            sums[8:16, cols] += fold_rows(grad)
            whole = grad * gain[:, cols]
            if places:
                whole = whole + grad_st[i, :, cols].astype(F32)
            grad_st[i, :, cols] = whole.astype(BF16)
        for copy in stores(grad_st, i, 1):
            copy.start()
        return carry

    if n_seq == 1:
        one_sequence(0, 0)
    else:
        lax.fori_loop(0, n_seq, one_sequence, 0)
    if is_last:
        for number, pick in enumerate(kind.picks):
            for cols in column_chunks(features):
                turned[cols, :] = total[number, :, cols].T
            for k in range(count):
                for j in range(QUAD):
                    place = (meta[2] ^ k) * (QUAD * rows) + (meta[1] ^ j) * rows
                    piece = turned[pl.ds(pl.multiple_of(place, rows), rows), :]
                    at = (k // 2, j) if pick is None else (k // 2, j, pick)
                    if k % 2:
                        grad_send[at] = piece.astype(BF16)
                    else:
                        grad_keep[at] = piece
    for copy in saves:
        copy.wait()
    if kind.turns and is_first and not is_last:
        keep.wait()
    for i in range(n_seq):
        for copy in stores(out_st, i, 0) + stores(grad_st, i, 1):
            copy.wait()


def branch(kind, meta, gain, shift, bias, messages, partials, blocks, carried, is_last):
    n_seq, count, is_first = len(messages), len(blocks), carried is None
    half = (messages[0][0].shape[0] - TABLE_ROWS) // 2
    features = messages[0][0].shape[1]
    length = 2 * half
    width = blocks[0].shape[-1]
    n_pick = len(kind.picks)
    operands = [meta, gain, shift, bias]
    specs = [SMEM] + [VMEM] * 3
    for pair in list(messages) + [part[:2] for part in partials]:
        operands += list(pair)
        specs += [HBM] * 2
    places = [part[2] for part in partials]
    if kind.turns and not is_first:
        operands += [carried[3]]
        specs += [HBM]
    else:
        operands += list(blocks)
        specs += [HBM] * count
    if not is_first:
        operands += list(carried[:3])
        specs += [HBM, VMEM, VMEM]
    if places:
        shapes = [jax.ShapeDtypeStruct((n_seq, 2, half, features), BF16)] * 2
    else:
        shapes = [jax.ShapeDtypeStruct((n_seq, length, features), BF16)] * 2
    shapes += [
        jax.ShapeDtypeStruct((16, features), F32),
        jax.ShapeDtypeStruct(kind.bias_shape(width), F32),
    ]
    out_specs = [HBM, HBM, VMEM, VMEM]
    if is_last:
        piece = (count // 2,) + blocks[0].shape
        shapes += [jax.ShapeDtypeStruct(piece, BF16), jax.ShapeDtypeStruct(piece, F32)]
        out_specs += [VMEM] * 2
    else:
        shapes += [jax.ShapeDtypeStruct((n_pick, width, features), F32)]
        out_specs += [HBM]
        if kind.turns and is_first:
            shapes += [jax.ShapeDtypeStruct((width, features), BF16)]
            out_specs += [HBM]
    scratch = [
        pltpu.VMEM((n_seq, length, features), BF16),
        pltpu.VMEM((n_seq, length, features), BF16),
        pltpu.VMEM((n_seq, TABLE_ROWS, features), BF16),
        pltpu.VMEM((n_pick, features, width), BF16),
        pltpu.VMEM((n_pick, width, features), F32),
        pltpu.VMEM((length, features), BF16),
        pltpu.VMEM((length, features), F32),
        pltpu.VMEM((n_seq, length, features), BF16),
        pltpu.VMEM((n_seq, length, features), BF16),
    ]
    if kind.turns:
        scratch += [pltpu.VMEM((width, features), BF16)]
    if is_last:
        scratch += [pltpu.VMEM((features, width), F32)]
    named = kind.scratch(length, features, width)
    scratch += list(named.values())
    scratch += [
        pltpu.SemaphoreType.DMA((n_seq, 2, 2)),
        pltpu.SemaphoreType.DMA((n_seq,)),
        pltpu.SemaphoreType.DMA((n_pick, count, QUAD)),
        pltpu.SemaphoreType.DMA((n_seq, 2)),
        pltpu.SemaphoreType.DMA((n_seq, 2, 2)),
        pltpu.SemaphoreType.DMA((3,)),
    ]
    flops, transcendentals = kind.cost(length, features, width)
    names = tuple(named)

    def body(*refs):
        branch_body(kind, names, n_seq, count, is_first, is_last, places, *refs)

    call = pl.pallas_call(
        body,
        in_specs=specs,
        out_specs=out_specs,
        out_shape=shapes,
        scratch_shapes=scratch,
        cost_estimate=pl.CostEstimate(
            flops=n_seq * flops,
            bytes_accessed=n_seq * 8 * length * features + 10 * n_pick * width * features,
            transcendentals=n_seq * transcendentals,
        ),
    )
    results = call(*operands)
    sums = results[2:4]
    if is_last:
        return results[:2], sums, results[4:]
    turned = () if not kind.turns else (results[5] if is_first else carried[3],)
    return results[:2], sums, (results[4], *sums, *turned)


def finish_body(x, d, own, p1, p2, p3, first_bias, second_bias, out, grad):
    tokens = x[...].astype(F32)
    branches = own[0].astype(F32) + p1[0].astype(F32) + p2[0].astype(F32) + p3[0].astype(F32)
    out[...] = (tokens + branches + first_bias[...] + second_bias[...]).astype(BF16)
    back = own[1].astype(F32) + p1[1].astype(F32) + p2[1].astype(F32) + p3[1].astype(F32)
    average = jnp.mean(tokens, axis=-1, keepdims=True)
    centred = tokens - average
    inverse = lax.rsqrt(jnp.mean(centred * centred, axis=-1, keepdims=True) + EPSILON)
    scaled = centred * inverse
    level = jnp.mean(back, axis=-1, keepdims=True)
    along = jnp.mean(back * scaled, axis=-1, keepdims=True)
    grad[...] = (d[...].astype(F32) + (back - level - scaled * along) * inverse).astype(BF16)


def finish(x, d, own, parts, first_bias, second_bias):
    rows, features = x.shape
    block = min(rows, 64)
    flat = pl.BlockSpec((block, features), lambda i: (i, 0))
    pair = pl.BlockSpec((2, block, features), lambda i: (0, i, 0))
    row = pl.BlockSpec((1, features), lambda i: (0, 0))
    return pl.pallas_call(
        finish_body,
        grid=(rows // block,),
        in_specs=[flat, flat, pair, pair, pair, pair, row, row],
        out_specs=[flat, flat],
        out_shape=[jax.ShapeDtypeStruct((rows, features), BF16)] * 2,
        name="finish",
    )(x, d, own, *parts, first_bias, second_bias)


def on_device(
    n_dp,
    inputs,
    segment_ids,
    positions,
    first_gain,
    first_shift,
    second_gain,
    second_shift,
    attend_weight,
    attend_bias,
    project_weight,
    project_bias,
    expand_weight,
    expand_bias,
    shrink_weight,
    shrink_bias,
    output_grad,
):
    count = n_dp // QUAD
    features = inputs.shape[1]
    attend_cols, hidden_cols = attend_weight.shape[1], expand_weight.shape[1]
    project_cols = project_weight.shape[0]
    core = lax.axis_index("tensor").astype(jnp.int32)
    dp_at = lax.axis_index("dp").astype(jnp.int32)
    quarter = dp_at % QUAD
    meta = jnp.stack([core, quarter, dp_at // QUAD])

    def to_quad(value, j):
        return lax.ppermute(value, "dp", xor_pairs(n_dp, j))

    def to_layer(value, bits):
        return lax.ppermute(value, "dp", xor_pairs(n_dp, bits * QUAD))

    def gather_layers(block):
        blocks = {0: block}
        bit = count // 2
        while bit:
            for k in sorted(blocks):
                blocks[k | bit] = to_layer(blocks[k], bit)
            bit //= 2
        return [blocks[k] for k in range(count)]

    halfway = ROT // 2
    frequency = 1.0 / 10000.0 ** (jnp.arange(halfway, dtype=F32) * (2.0 / ROT))
    angles = frequency[:, None] * positions.astype(F32)[None, :]
    earlier = segment_ids[None, :] < segment_ids[:, None]
    start = jnp.sum(earlier.astype(jnp.int32), axis=1)
    start = jnp.concatenate([start // 256, start % 256]).astype(BF16)
    turns = jnp.concatenate([jnp.cos(angles), jnp.sin(angles)], axis=1)
    message = join_message(
        inputs, output_grad, *low_parts(turns, 3), jnp.broadcast_to(start[None], turns.shape)
    )

    first_pack, second_pack = pack_weights(
        meta, attend_weight, project_weight.T, expand_weight, shrink_weight.T
    )
    second_parts = [second_pack[0]]
    second_parts += [to_quad(second_pack[j], j) for j in range(1, QUAD)]
    second_blocks = gather_layers(jnp.stack(second_parts))
    first_parts = [first_pack[0]] + [to_quad(first_pack[j], j) for j in range(1, QUAD)]
    first_blocks = gather_layers(jnp.stack(first_parts))

    whole = [message] + [to_quad(message, j) for j in range(1, QUAD)]
    messages = [(value, swap_cores(value)) for value in whole]

    one_row = lambda vector: vector[None, :]
    bias_part = lax.dynamic_index_in_dim(
        attend_bias.reshape(QUAD, attend_cols // QUAD), quarter, 0, False
    )
    bias_part = jnp.broadcast_to(bias_part[:, None], (attend_cols // QUAD, 128))
    hidden_part = lax.dynamic_index_in_dim(
        expand_bias.reshape(QUAD, hidden_cols // QUAD), quarter, 0, True
    )

    carried, partials = None, {}
    for group in ATTEND_GROUPS:
        results = branch(
            Attend,
            meta,
            one_row(first_gain),
            one_row(first_shift),
            bias_part,
            [messages[s] for s in group],
            [],
            first_blocks,
            carried,
            group is ATTEND_GROUPS[-1],
        )
        (out_part, grad_part), attend_sums, carried = results
        for place, s in enumerate(group):
            partials[s] = (out_part, grad_part, place)
    attend_send, attend_keep = carried

    carried, sums_of = None, {}
    for group in MLP_GROUPS:
        results = branch(
            Mlp,
            meta,
            one_row(second_gain),
            one_row(second_shift),
            hidden_part,
            [messages[s] for s in group],
            [partials[s] for s in group],
            second_blocks,
            carried,
            group is MLP_GROUPS[-1],
        )
        (mine, other), mlp_sums, carried = results
        other = swap_cores(other)
        for place, s in enumerate(group):
            both = mine[place].astype(F32) + other[place].astype(F32)
            sums_of[s] = both.astype(BF16)
    mlp_send, mlp_keep = carried

    parts = [to_quad(sums_of[j], j) for j in range(1, QUAD)]
    outputs, grad_inputs = finish(
        inputs, output_grad, sums_of[0], parts, one_row(project_bias), one_row(shrink_bias)
    )

    def reduce_layers(send, keep):
        bit = 1
        while True:
            total = to_layer(send, bit).astype(F32) + keep
            if total.shape[0] == 1:
                break
            send, keep = total[1::2].astype(BF16), total[0::2]
            bit *= 2
        parts = [to_quad(total[0, j].astype(BF16), j) for j in range(1, QUAD)]
        return total[0, 0], parts

    own, received = reduce_layers(mlp_send, mlp_keep)
    grad_expand, grad_shrink = unpack_mlp(meta, own, received, hidden_cols)
    own, received = reduce_layers(attend_send, attend_keep)
    grad_attend, grad_project = unpack_attend(meta, own, received, attend_cols, project_cols)

    place = core * QUAD + quarter
    attend_full = lax.dynamic_update_slice_in_dim(
        jnp.zeros((2 * attend_cols,), F32),
        jnp.sum(attend_sums[1], axis=1),
        place * (attend_cols // QUAD),
        0,
    )
    hidden_full = lax.dynamic_update_slice_in_dim(
        jnp.zeros((2 * hidden_cols,), F32),
        jnp.sum(mlp_sums[1], axis=0),
        place * (hidden_cols // QUAD),
        0,
    )
    vector = jnp.concatenate(
        [
            jnp.sum(attend_sums[0].reshape(2, 8, features), axis=1).reshape(-1),
            jnp.sum(mlp_sums[0].reshape(2, 8, features), axis=1).reshape(-1),
            jnp.sum(output_grad.astype(F32), axis=0),
            attend_full,
            hidden_full,
        ]
    ).reshape(-1, 128)
    vector = vector + swap_cores(vector)
    bit = 1
    while bit < n_dp:
        vector = vector + lax.ppermute(vector, "dp", xor_pairs(n_dp, bit))
        bit *= 2
    vector = vector.reshape(-1)
    pieces, at = [], 0
    for size in [features] * 5 + [2 * attend_cols, 2 * hidden_cols]:
        pieces.append(vector[at : at + size])
        at += size
    return (
        outputs,
        grad_inputs,
        pieces[0],
        pieces[1],
        pieces[2],
        pieces[3],
        grad_attend,
        pieces[5],
        grad_project.T,
        pieces[4],
        grad_expand,
        pieces[6],
        grad_shrink.T,
        pieces[4],
    )


def solution(mesh):
    n_dp = mesh.shape["dp"]
    assert mesh.shape["tensor"] == 2 and n_dp % QUAD == 0 and n_dp & (n_dp - 1) == 0
    rows = P(("dp", "tensor"), None)
    in_specs = (
        rows,
        P("dp"),
        P("dp"),
        P(),
        P(),
        P(),
        P(),
        P("dp", "tensor"),
        P("tensor"),
        P("tensor", "dp"),
        P(),
        P("dp", "tensor"),
        P("tensor"),
        P("tensor", "dp"),
        P(),
        rows,
    )
    out_specs = (
        rows,
        rows,
        P(),
        P(),
        P(),
        P(),
        P("dp", "tensor"),
        P(),
        P("tensor", "dp"),
        P(),
        P("dp", "tensor"),
        P(),
        P("tensor", "dp"),
        P(),
    )

    def program(*args):
        return on_device(n_dp, *args)

    return jax.shard_map(
        program, mesh=mesh, in_specs=in_specs, out_specs=out_specs, check_vma=False
    )
```

```python
import jax
import jax.numpy as jnp
import numpy as np
from jax import lax
from jax.experimental import pallas as pl
from jax.experimental.pallas import tpu as pltpu
from jax.sharding import PartitionSpec as P


HD = 64
ROT = 16
QUAD = 4
TABLE_ROWS = 32
EPSILON = 1e-05
NEGATIVE = -1e30
QUERY_BLOCK = 256
ROW_CHUNK = 32
ATTEND_GROUPS = ((0,), (1, 2), (3,))
MLP_GROUPS = ((3,), (1, 2), (0,))
F32 = jnp.float32
BF16 = jnp.bfloat16


HBM = pl.BlockSpec(memory_space=pltpu.HBM)
VMEM = pl.BlockSpec(memory_space=pltpu.VMEM)
SMEM = pl.BlockSpec(memory_space=pltpu.SMEM)


def dot_nn(left, right):
    return lax.dot_general(left, right, (((1,), (0,)), ((), ())), preferred_element_type=F32)


def dot_nt(left, right):
    return lax.dot_general(left, right, (((1,), (1,)), ((), ())), preferred_element_type=F32)


def dot_tn(left, right):
    return lax.dot_general(left, right, (((0,), (0,)), ((), ())), preferred_element_type=F32)


def xor_pairs(n_dp, bits):
    return [(index, index ^ bits) for index in range(n_dp)]


def swap_cores(value):
    return lax.ppermute(value, "tensor", [(0, 1), (1, 0)])


def low_parts(value, number):
    parts = []
    for _ in range(number):
        part = lax.reduce_precision(value, 8, 7)
        parts.append(part.astype(BF16))
        value = value - part
    return parts


def pack_body(meta, attend, project, expand, shrink, *outs):
    first, second = outs[:QUAD], outs[QUAD:]
    quarter = meta[1]
    heads = attend.shape[1] // QUAD
    context = project.shape[1] // QUAD
    hidden = expand.shape[1] // QUAD
    for j in range(QUAD):
        at = quarter ^ j
        first[j][:, :heads] = attend[:, pl.ds(pl.multiple_of(at * heads, 128), heads)]
        first[j][:, heads:] = project[:, pl.ds(pl.multiple_of(at * context, 128), context)]
        second[j][0] = expand[:, pl.ds(pl.multiple_of(at * hidden, 128), hidden)]
        second[j][1] = shrink[:, pl.ds(pl.multiple_of(at * hidden, 128), hidden)]


def pack_weights(meta, attend, project, expand, shrink):
    rows = attend.shape[0]
    width = (attend.shape[1] + project.shape[1]) // QUAD
    hidden = expand.shape[1] // QUAD
    parts = pl.pallas_call(
        pack_body,
        in_specs=[SMEM] + [VMEM] * 4,
        out_specs=[VMEM] * (2 * QUAD),
        out_shape=[jax.ShapeDtypeStruct((rows, width), BF16)] * QUAD
        + [jax.ShapeDtypeStruct((2, rows, hidden), BF16)] * QUAD,
        name="pack_weights",
    )(meta, attend, project, expand, shrink)
    return parts[:QUAD], parts[QUAD:]


def join_body(*refs):
    parts, message = refs[:-1], refs[-1]
    at = 0
    for part in parts:
        message[at : at + part.shape[0]] = part[...]
        at += part.shape[0]


def join_message(*parts):
    rows = sum(part.shape[0] for part in parts)
    return pl.pallas_call(
        join_body,
        in_specs=[VMEM] * len(parts),
        out_specs=VMEM,
        out_shape=jax.ShapeDtypeStruct((rows, parts[0].shape[1]), BF16),
        name="join_message",
    )(*parts)


def sum_layers_body(keep, *refs):
    received, outs = refs[:-QUAD], refs[-QUAD:]
    for j in range(QUAD):
        total = keep[j]
        for part in received:
            total = total + part[j].astype(F32)
        outs[j][...] = total.astype(outs[j].dtype)


def sum_layers(keep, received):
    shape = keep.shape[1:]
    return pl.pallas_call(
        sum_layers_body,
        in_specs=[VMEM] * (1 + len(received)),
        out_specs=[VMEM] * QUAD,
        out_shape=[jax.ShapeDtypeStruct(shape, BF16 if j else F32) for j in range(QUAD)],
        name="sum_layers",
    )(keep, *received)


def add_body(place, mine, other, out, mine_s, other_s, out_s, sems):
    def copies(which):
        pairs = ((mine, mine_s), (other, other_s))
        return [
            pltpu.make_async_copy(source.at[place, which], target.at[which], sems.at[which, n])
            for n, (source, target) in enumerate(pairs)
        ]

    saves = [
        pltpu.make_async_copy(out_s.at[which], out.at[which], sems.at[which, 2]) for which in (0, 1)
    ]
    for which in (0, 1):
        for copy in copies(which):
            copy.start()
    for which in (0, 1):
        for copy in copies(which):
            copy.wait()
        out_s[which] = (mine_s[which].astype(F32) + other_s[which].astype(F32)).astype(BF16)
        saves[which].start()
    for save in saves:
        save.wait()


def add_halves(mine, other, place):
    shape = mine.shape[1:]
    return pl.pallas_call(
        lambda *refs: add_body(place, *refs),
        in_specs=[HBM] * 2,
        out_specs=HBM,
        out_shape=jax.ShapeDtypeStruct(shape, BF16),
        scratch_shapes=[pltpu.VMEM(shape, BF16)] * 3 + [pltpu.SemaphoreType.DMA((2, 3))],
        name="add_halves",
    )(mine, other)


def split_body(*refs):
    count = len(refs) - 8
    totals = [ref[...] for ref in refs[:count]]
    while len(totals) > 1:
        totals = [first + second for first, second in zip(totals[::2], totals[1::2])]
    at = 0
    for number, out in enumerate(refs[count:]):
        at -= out.shape[0] if number == 5 else 0
        out[...] = totals[0][at : at + out.shape[0]]
        at += out.shape[0]


def split_vector(vectors, sizes):
    pieces = pl.pallas_call(
        split_body,
        in_specs=[VMEM] * len(vectors),
        out_specs=[VMEM] * len(sizes),
        out_shape=[jax.ShapeDtypeStruct((size // 128, 128), F32) for size in sizes],
        name="split_vector",
    )(*vectors)
    return [piece.reshape(-1) for piece in pieces]


def unpack_attend_body(meta, own, *refs):
    received, (attend, project) = refs[:3], refs[3:]
    quarter = meta[1]
    heads = attend.shape[1] // QUAD
    context = project.shape[1] // QUAD
    for j in range(QUAD):
        piece = own[...] if j == 0 else received[j - 1][...].astype(F32)
        at = quarter ^ j
        attend[:, pl.ds(pl.multiple_of(at * heads, 128), heads)] = piece[:, :heads]
        project[:, pl.ds(pl.multiple_of(at * context, 128), context)] = piece[:, heads:]


def unpack_attend(meta, own, received, attend_cols, project_cols):
    rows = own.shape[0]
    return pl.pallas_call(
        unpack_attend_body,
        in_specs=[SMEM] + [VMEM] * 4,
        out_specs=[VMEM] * 2,
        out_shape=[
            jax.ShapeDtypeStruct((rows, attend_cols), F32),
            jax.ShapeDtypeStruct((rows, project_cols), F32),
        ],
        name="unpack_attend",
    )(meta, own, *received)


def unpack_mlp_body(meta, own, *refs):
    received, (expand, shrink) = refs[:3], refs[3:]
    quarter = meta[1]
    hidden = expand.shape[1] // QUAD
    for j in range(QUAD):
        piece = own if j == 0 else received[j - 1]
        lanes = pl.ds(pl.multiple_of((quarter ^ j) * hidden, 128), hidden)
        expand[:, lanes] = piece[0].astype(F32)
        shrink[:, lanes] = piece[1].astype(F32)


def unpack_mlp(meta, own, received, hidden_cols):
    rows = own.shape[1]
    return pl.pallas_call(
        unpack_mlp_body,
        in_specs=[SMEM] + [VMEM] * 4,
        out_specs=[VMEM] * 2,
        out_shape=[jax.ShapeDtypeStruct((rows, hidden_cols), F32)] * 2,
        name="unpack_mlp",
    )(meta, own, *received)


def row_chunks(length):
    return [slice(c * ROW_CHUNK, (c + 1) * ROW_CHUNK) for c in range(length // ROW_CHUNK)]


def column_chunks(features):
    return [slice(c * 256, (c + 1) * 256) for c in range(features // 256)]


def wait_bytes(view, sem):
    pltpu.make_async_copy(view, view, sem).wait()


def widen(tile, features):
    return jnp.concatenate([tile] * (features // 128), axis=1)


def fold_rows(value):
    return jnp.sum(value.reshape(value.shape[0] // 8, 8, value.shape[1]), axis=0)


def fold_lanes(value):
    tiles = [value[:, k * 128 : (k + 1) * 128] for k in range(value.shape[1] // 128)]
    while len(tiles) > 1:
        tiles = [sum(tiles[k : k + 2]) for k in range(0, len(tiles), 2)]
    return tiles[0]


def normalize(x, gain, shift, norm_s, hat_s):
    length, features = x.shape
    share = np.float32(1.0 / features)

    def some_rows(number, carry):
        for part in range(4):
            at = pl.multiple_of((number * 4 + part) * ROW_CHUNK, ROW_CHUNK)
            rows = pl.ds(at, ROW_CHUNK)
            tokens = x[rows, :].astype(F32)
            centred = tokens - jnp.sum(fold_lanes(tokens), axis=-1, keepdims=True) * share
            variance = jnp.sum(fold_lanes(centred * centred), axis=-1, keepdims=True) * share
            scaled = centred * lax.rsqrt(variance + EPSILON)
            hat_s[rows, :] = scaled
            norm_s[rows, :] = (scaled * gain[...] + shift[...]).astype(BF16)
        return carry

    lax.fori_loop(0, length // (4 * ROW_CHUNK), some_rows, 0)


def rotate_rows(part, cosine, sine):
    half = ROT // 2
    lead, trail = part[:half], part[half:ROT]
    return jnp.concatenate(
        [lead * cosine - trail * sine, trail * cosine + lead * sine, part[ROT:]], axis=0
    )


class Attend:
    picks = (None,)
    turns = True

    @staticmethod
    def scratch(length, features, width):
        return {
            "mask": pltpu.VMEM((length // QUERY_BLOCK, length, QUERY_BLOCK), F32),
            "q": pltpu.VMEM((2, 2 * HD, length), BF16),
            "d": pltpu.VMEM((2, 2 * HD, length), BF16),
            "kv": pltpu.VMEM((2, length, 2 * HD), BF16),
            "kvt": pltpu.VMEM((2, 2 * HD, length), BF16),
            "score": pltpu.VMEM((2, length, QUERY_BLOCK), F32),
            "gprob": pltpu.VMEM((2, length, QUERY_BLOCK), F32),
            "weight": pltpu.VMEM((2, length, QUERY_BLOCK), BF16),
            "gprod": pltpu.VMEM((2, length, QUERY_BLOCK), BF16),
            "dq": pltpu.VMEM((2, HD, length), F32),
            "dk": pltpu.VMEM((2, HD, length), F32),
            "dv": pltpu.VMEM((2, HD, length), F32),
            "ctxt": pltpu.VMEM((2 * HD, length), BF16),
            "ctx": pltpu.VMEM((length, 2 * HD), BF16),
            "gmt": pltpu.VMEM((6 * HD, length), BF16),
            "gm": pltpu.VMEM((length, 6 * HD), BF16),
        }

    @staticmethod
    def bias_shape(width):
        return (6 * HD, 128)

    @staticmethod
    def cost(length, features, width):
        return 6 * length * features * width + 14 * length * length * 2 * HD, 2 * length**2

    @staticmethod
    def compute(m, norm, cot, w, bias, bias_sums, table):
        length = norm.shape[0]
        heads = 6 * HD
        scale = np.float32(HD ** (-0.5))
        values = sum(table[k * 8 : (k + 1) * 8, :].astype(F32) for k in range(3))
        cosine, sine = values[:, :length], values[:, length:]
        start = table[24:25, :length].astype(F32) * 256.0 + table[24:25, length:].astype(F32)
        for block in range(length // QUERY_BLOCK):
            width = (block + 1) * QUERY_BLOCK
            lanes = slice(block * QUERY_BLOCK, width)
            key_at = lax.broadcasted_iota(jnp.int32, (width, QUERY_BLOCK), 0)
            query_at = lax.broadcasted_iota(jnp.int32, (width, QUERY_BLOCK), 1)
            first = start[:, lanes].astype(jnp.int32)
            allowed = (key_at >= first) & (key_at <= query_at + block * QUERY_BLOCK)
            m["mask"][block, :width, :] = jnp.where(allowed, 0.0, NEGATIVE)

        projected = dot_nt(w[:heads, :], norm[...]) + widen(bias[...], length)
        grad_context = dot_nt(w[heads:, :], cot[...]).astype(BF16)
        nothing = jnp.zeros((HD, length), BF16)
        for h in range(2):
            query, key, value = [
                projected[(3 * h + k) * HD : (3 * h + k + 1) * HD] for k in range(3)
            ]
            m["q"][h, :HD, :] = (rotate_rows(query, cosine, sine) * scale).astype(BF16)
            m["q"][h, HD:, :] = nothing
            m["d"][h, :HD, :] = nothing
            m["d"][h, HD:, :] = grad_context[h * HD : (h + 1) * HD]
            both = jnp.concatenate([rotate_rows(key, cosine, sine), value], axis=0).astype(BF16)
            m["kvt"][h] = both
            m["kv"][h] = both.T

        items = [
            (block, h) for block in reversed(range(length // QUERY_BLOCK)) for h in range(2)
        ]

        def place(item):
            block = items[item][0]
            width = (block + 1) * QUERY_BLOCK
            return *items[item], width, slice(block * QUERY_BLOCK, width)

        def products(item):
            _, h, width, lanes = place(item)
            key_value = m["kv"][h, :width, :]
            m["score"][item % 2, :width, :] = dot_nn(key_value, m["q"][h, :, lanes])
            m["gprob"][item % 2, :width, :] = dot_nn(key_value, m["d"][h, :, lanes])

        def softmax(item):
            block, _, width, _ = place(item)
            scores = m["score"][item % 2, :width, :] + m["mask"][block, :width, :]
            highest = jnp.max(scores, axis=0, keepdims=True)
            numerators = jnp.exp(scores - highest)
            weights = numerators * (1.0 / jnp.sum(numerators, axis=0, keepdims=True))
            grad_probs = m["gprob"][item % 2, :width, :]
            centre = jnp.sum(grad_probs * weights, axis=0, keepdims=True)
            m["weight"][item % 2, :width, :] = weights.astype(BF16)
            m["gprod"][item % 2, :width, :] = (weights * (grad_probs - centre)).astype(BF16)

        def results(item):
            _, h, width, lanes = place(item)
            weights_low = m["weight"][item % 2, :width, :]
            grad_products = m["gprod"][item % 2, :width, :]
            context = dot_nn(m["kvt"][h, HD:, :width], weights_low)
            m["ctxt"][h * HD : (h + 1) * HD, lanes] = context.astype(BF16)
            grad_query = dot_nn(m["kvt"][h, :HD, :width], grad_products)
            m["dq"][h, :, lanes] = grad_query * scale
            grad_key = dot_nt(m["q"][h, :HD, lanes], grad_products)
            grad_value = dot_nt(m["d"][h, HD:, lanes], weights_low)
            if width == length:
                m["dk"][h] = grad_key
                m["dv"][h] = grad_value
            else:
                m["dk"][h, :, :width] += grad_key
                m["dv"][h, :, :width] += grad_value

        products(0)
        for item in range(len(items)):
            if item + 1 < len(items):
                products(item + 1)
            if item:
                results(item - 1)
            softmax(item)
        results(len(items) - 1)

        for h in range(2):
            parts = [
                rotate_rows(m["dq"][h], cosine, -sine),
                rotate_rows(m["dk"][h], cosine, -sine),
                m["dv"][h],
            ]
            for k, part in enumerate(parts):
                rows = slice((3 * h + k) * HD, (3 * h + k + 1) * HD)
                low = part.astype(BF16)
                m["gmt"][rows, :] = low
                bias_sums[rows, :] += fold_lanes(low.astype(F32))
        m["gm"][...] = m["gmt"][...].T
        m["ctx"][...] = m["ctxt"][...].T

    @staticmethod
    def accumulate(m, norm, cot, total):
        heads = 6 * HD
        total[0, :heads, :] += dot_nn(m["gmt"][...], norm[...])
        total[0, heads:, :] += dot_nn(m["ctxt"][...], cot[...])

    @staticmethod
    def forward_out(m, w, cols):
        return dot_nn(m["ctx"][...], w[6 * HD :, cols])

    @staticmethod
    def backward_out(m, w, cols):
        return dot_nn(m["gm"][...], w[: 6 * HD, cols])


class Mlp:
    picks = (0, 1)
    turns = False

    @staticmethod
    def scratch(length, features, width):
        return {
            "hid": pltpu.VMEM((2, length, width), F32),
            "act": pltpu.VMEM((length, width), BF16),
            "dh": pltpu.VMEM((length, width), BF16),
        }

    @staticmethod
    def bias_shape(width):
        return (8, width)

    @staticmethod
    def cost(length, features, width):
        return 12 * length * features * width, 2 * length * width

    @staticmethod
    def compute(m, norm, cot, w, bias, bias_sums, table):
        m["hid"][0] = dot_nn(norm[...], w[0]) + bias[...]
        m["hid"][1] = dot_nn(cot[...], w[1])
        for rows in row_chunks(norm.shape[0]):
            hid = m["hid"][0, rows, :]
            below = 0.5 + 0.5 * lax.erf(hid * np.float32(0.5**0.5))
            slope = below + hid * jnp.exp(-0.5 * (hid * hid)) * np.float32((2 * np.pi) ** -0.5)
            m["act"][rows, :] = (hid * below).astype(BF16)
            grad_hid = (slope * m["hid"][1, rows, :]).astype(BF16)
            m["dh"][rows, :] = grad_hid
            bias_sums[...] += fold_rows(grad_hid.astype(F32))

    @staticmethod
    def accumulate(m, norm, cot, total):
        total[0] += dot_tn(m["dh"][...], norm[...])
        total[1] += dot_tn(m["act"][...], cot[...])

    @staticmethod
    def forward_out(m, w, cols):
        return dot_nt(m["act"][...], w[1, cols, :])

    @staticmethod
    def backward_out(m, w, cols):
        return dot_nt(m["dh"][...], w[0, cols, :])


def branch_body(kind, names, n_seq, count, is_first, is_last, places, *refs):
    refs = list(refs)
    take = lambda number: [refs.pop(0) for _ in range(number)]
    (meta, gain, shift, bias) = take(4)
    messages = [take(2) for _ in range(n_seq)]
    partials = [take(2) for _ in places or ()]
    reads_turned = kind.turns and not is_first
    blocks = take(1 if reads_turned else count)
    carried = [] if is_first else take(3)
    out_hbm, grad_hbm, sums, bias_sums = take(4)
    if is_last:
        grads = take(count)
    else:
        (total_hbm,) = take(1)
        if kind.turns:
            (turned_hbm,) = take(1) if is_first else (None,)
    x_s, d_s, tab_s, w_s, total, norm_s, hat_s, out_st, grad_st = take(9)
    wt_s = take(1)[0] if kind.turns else None
    turned = take(1)[0] if is_last else None
    m = dict(zip(names, take(len(names))))
    token_sem, table_sem, weight_sem, part_sem, out_sem, total_sem = take(6)

    length, features = x_s.shape[1:]
    half = length // 2
    mine = pl.multiple_of(meta[0] * half, half)
    other = pl.multiple_of((1 - meta[0]) * half, half)
    rows = features // (QUAD * count)

    weight_copies = []
    if reads_turned:
        weight_copies.append(pltpu.make_async_copy(blocks[0], wt_s, weight_sem.at[0, 0, 0]))
    else:
        for k in range(count):
            for j in range(QUAD):
                place = (meta[2] ^ k) * (QUAD * rows) + (meta[1] ^ j) * rows
                for number, pick in enumerate(kind.picks):
                    source = blocks[k].at[j] if pick is None else blocks[k].at[j, pick]
                    target = w_s.at[number, pl.ds(pl.multiple_of(place, rows), rows)]
                    weight_copies.append(
                        pltpu.make_async_copy(source, target, weight_sem.at[number, k, j])
                    )

    def start_message(i, target, first, which):
        for number, place in enumerate((mine, other)):
            pltpu.make_async_copy(
                messages[i][number].at[pl.ds(first, half)],
                target.at[i, pl.ds(place, half)],
                token_sem.at[i, which, number],
            ).start()

    def start_rest(i):
        start_message(i, d_s, half, 1)
        if kind.turns:
            pltpu.make_async_copy(
                messages[i][0].at[pl.ds(2 * half, TABLE_ROWS)], tab_s.at[i], table_sem.at[i]
            ).start()
        if i == 0:
            for copy in weight_copies:
                copy.start()

    def start_partials(i):
        if places:
            for number, stage in enumerate((out_st, grad_st)):
                pltpu.make_async_copy(
                    partials[i][number].at[places[i]], stage.at[i], part_sem.at[i, number]
                ).start()

    start_message(0, x_s, 0, 0)
    if is_first:
        total[...] = jnp.zeros_like(total)
        sums[...] = jnp.zeros_like(sums)
        bias_sums[...] = jnp.zeros_like(bias_sums)
    else:
        load = pltpu.make_async_copy(carried[0], total, total_sem.at[0])
        sums[...] = carried[1][...]
        bias_sums[...] = carried[2][...]
    saves = []
    if not is_last:
        saves.append(pltpu.make_async_copy(total, total_hbm, total_sem.at[1]))
        if kind.turns and is_first:
            keep = pltpu.make_async_copy(wt_s, turned_hbm, total_sem.at[2])

    def stores(stage, i, which):
        if not places:
            target = (out_hbm, grad_hbm)[which]
            return [pltpu.make_async_copy(stage.at[i], target.at[i], out_sem.at[i, which, 0])]
        return [
            pltpu.make_async_copy(
                stage.at[i, pl.ds(place, half)], target.at[i, which], out_sem.at[i, which, number]
            )
            for number, (place, target) in enumerate(((mine, out_hbm), (other, grad_hbm)))
        ]

    def one_sequence(i, carry):
        for number in range(2):
            wait_bytes(x_s.at[i, pl.ds(0, half)], token_sem.at[i, 0, number])

        @pl.when(i == 0)
        def _():
            start_rest(0)

        normalize(x_s.at[i], gain, shift, norm_s, hat_s)
        if kind.turns:
            wait_bytes(tab_s.at[i], table_sem.at[i])
        for number in range(2):
            wait_bytes(d_s.at[i, pl.ds(0, half)], token_sem.at[i, 1, number])

        @pl.when(i == 0)
        def _():
            for copy in weight_copies:
                copy.wait()
            if not is_first:
                load.start()
            for later in range(1, n_seq):
                start_message(later, x_s, 0, 0)
                start_rest(later)
            for later in range(n_seq):
                start_partials(later)
            if kind.turns and is_first:
                for cols in column_chunks(features):
                    wt_s[:, cols] = w_s[0, cols, :].T
                if not is_last:
                    keep.start()

        cot = d_s.at[i]
        w = wt_s if kind.turns else w_s
        kind.compute(m, norm_s, cot, w, bias, bias_sums, tab_s.at[i])
        if not is_first:

            @pl.when(i == 0)
            def _():
                load.wait()

        kind.accumulate(m, norm_s, cot, total)
        if not is_last:

            @pl.when(i == n_seq - 1)
            def _():
                for copy in saves:
                    copy.start()

        if places:
            wait_bytes(out_st.at[i], part_sem.at[i, 0])
            wait_bytes(grad_st.at[i], part_sem.at[i, 1])
        for cols in column_chunks(features):
            out = kind.forward_out(m, w, cols)
            if places:
                out = out + out_st[i, :, cols].astype(F32)
            out_st[i, :, cols] = out.astype(BF16)
        for copy in stores(out_st, i, 0):
            copy.start()
        for cols in column_chunks(features):
            grad = kind.backward_out(m, w, cols)
            sums[0:8, cols] += fold_rows(grad * hat_s[:, cols])
            sums[8:16, cols] += fold_rows(grad)
            whole = grad * gain[:, cols]
            if places:
                whole = whole + grad_st[i, :, cols].astype(F32)
            grad_st[i, :, cols] = whole.astype(BF16)
        for copy in stores(grad_st, i, 1):
            copy.start()
        return carry

    if n_seq == 1:
        one_sequence(0, 0)
    else:
        lax.fori_loop(0, n_seq, one_sequence, 0)
    if is_last:
        for number, pick in enumerate(kind.picks):
            for cols in column_chunks(features):
                turned[cols, :] = total[number, :, cols].T
            for k in range(count):
                for j in range(QUAD):
                    place = (meta[2] ^ k) * (QUAD * rows) + (meta[1] ^ j) * rows
                    piece = turned[pl.ds(pl.multiple_of(place, rows), rows), :]
                    at = (j,) if pick is None else (j, pick)
                    grads[k][at] = piece.astype(grads[k].dtype)
    for copy in saves:
        copy.wait()
    if kind.turns and is_first and not is_last:
        keep.wait()
    for i in range(n_seq):
        for copy in stores(out_st, i, 0) + stores(grad_st, i, 1):
            copy.wait()


def branch(kind, meta, gain, shift, bias, messages, partials, blocks, carried, is_last):
    n_seq, count, is_first = len(messages), len(blocks), carried is None
    half = (messages[0][0].shape[0] - TABLE_ROWS) // 2
    features = messages[0][0].shape[1]
    length = 2 * half
    width = blocks[0].shape[-1]
    n_pick = len(kind.picks)
    operands = [meta, gain, shift, bias]
    specs = [SMEM] + [VMEM] * 3
    for pair in list(messages) + [part[:2] for part in partials]:
        operands += list(pair)
        specs += [HBM] * 2
    places = [part[2] for part in partials]
    if kind.turns and not is_first:
        operands += [carried[3]]
        specs += [HBM]
    else:
        operands += list(blocks)
        specs += [HBM] * count
    if not is_first:
        operands += list(carried[:3])
        specs += [HBM, VMEM, VMEM]
    if places:
        shapes = [jax.ShapeDtypeStruct((n_seq, 2, half, features), BF16)] * 2
    else:
        shapes = [jax.ShapeDtypeStruct((n_seq, length, features), BF16)] * 2
    shapes += [
        jax.ShapeDtypeStruct((16, features), F32),
        jax.ShapeDtypeStruct(kind.bias_shape(width), F32),
    ]
    out_specs = [HBM, HBM, VMEM, VMEM]
    if is_last:
        shape = blocks[0].shape
        shapes += [jax.ShapeDtypeStruct(shape, BF16 if k else F32) for k in range(count)]
        out_specs += [VMEM] * count
    else:
        shapes += [jax.ShapeDtypeStruct((n_pick, width, features), F32)]
        out_specs += [HBM]
        if kind.turns and is_first:
            shapes += [jax.ShapeDtypeStruct((width, features), BF16)]
            out_specs += [HBM]
    scratch = [
        pltpu.VMEM((n_seq, length, features), BF16),
        pltpu.VMEM((n_seq, length, features), BF16),
        pltpu.VMEM((n_seq, TABLE_ROWS, features), BF16),
        pltpu.VMEM((n_pick, features, width), BF16),
        pltpu.VMEM((n_pick, width, features), F32),
        pltpu.VMEM((length, features), BF16),
        pltpu.VMEM((length, features), F32),
        pltpu.VMEM((n_seq, length, features), BF16),
        pltpu.VMEM((n_seq, length, features), BF16),
    ]
    if kind.turns:
        scratch += [pltpu.VMEM((width, features), BF16)]
    if is_last:
        scratch += [pltpu.VMEM((features, width), F32)]
    named = kind.scratch(length, features, width)
    scratch += list(named.values())
    scratch += [
        pltpu.SemaphoreType.DMA((n_seq, 2, 2)),
        pltpu.SemaphoreType.DMA((n_seq,)),
        pltpu.SemaphoreType.DMA((n_pick, count, QUAD)),
        pltpu.SemaphoreType.DMA((n_seq, 2)),
        pltpu.SemaphoreType.DMA((n_seq, 2, 2)),
        pltpu.SemaphoreType.DMA((3,)),
    ]
    flops, transcendentals = kind.cost(length, features, width)
    names = tuple(named)

    def body(*refs):
        branch_body(kind, names, n_seq, count, is_first, is_last, places, *refs)

    call = pl.pallas_call(
        body,
        in_specs=specs,
        out_specs=out_specs,
        out_shape=shapes,
        scratch_shapes=scratch,
        cost_estimate=pl.CostEstimate(
            flops=n_seq * flops,
            bytes_accessed=n_seq * 8 * length * features + 10 * n_pick * width * features,
            transcendentals=n_seq * transcendentals,
        ),
    )
    results = call(*operands)
    sums = results[2:4]
    if is_last:
        return results[:2], sums, results[4:]
    turned = () if not kind.turns else (results[5] if is_first else carried[3],)
    return results[:2], sums, (results[4], *sums, *turned)


def finish_body(x, d, mine, other, p1, p2, p3, first_bias, second_bias, out, grad):
    def total(which):
        own = mine[0, which].astype(F32) + other[0, which].astype(F32)
        return own + p1[which].astype(F32) + (p2[which].astype(F32) + p3[which].astype(F32))

    tokens = x[...].astype(F32)
    out[...] = (tokens + total(0) + first_bias[...] + second_bias[...]).astype(BF16)
    back = total(1)
    average = jnp.mean(tokens, axis=-1, keepdims=True)
    centred = tokens - average
    inverse = lax.rsqrt(jnp.mean(centred * centred, axis=-1, keepdims=True) + EPSILON)
    scaled = centred * inverse
    level = jnp.mean(back, axis=-1, keepdims=True)
    along = jnp.mean(back * scaled, axis=-1, keepdims=True)
    grad[...] = (d[...].astype(F32) + (back - level - scaled * along) * inverse).astype(BF16)


def finish(x, d, own, parts, first_bias, second_bias):
    rows, features = x.shape
    block = min(rows, 128)
    mine, other, place = own
    flat = pl.BlockSpec((block, features), lambda i: (i, 0))
    half = pl.BlockSpec((1, 2, block, features), lambda i: (place, 0, i, 0))
    pair = pl.BlockSpec((2, block, features), lambda i: (0, i, 0))
    row = pl.BlockSpec((1, features), lambda i: (0, 0))
    return pl.pallas_call(
        finish_body,
        grid=(rows // block,),
        in_specs=[flat, flat, half, half, pair, pair, pair, row, row],
        out_specs=[flat, flat],
        out_shape=[jax.ShapeDtypeStruct((rows, features), BF16)] * 2,
        name="finish",
    )(x, d, mine, other, *parts, first_bias, second_bias)


def on_device(
    n_dp,
    inputs,
    segment_ids,
    positions,
    first_gain,
    first_shift,
    second_gain,
    second_shift,
    attend_weight,
    attend_bias,
    project_weight,
    project_bias,
    expand_weight,
    expand_bias,
    shrink_weight,
    shrink_bias,
    output_grad,
):
    count = n_dp // QUAD
    features = inputs.shape[1]
    attend_cols, hidden_cols = attend_weight.shape[1], expand_weight.shape[1]
    project_cols = project_weight.shape[0]
    core = lax.axis_index("tensor").astype(jnp.int32)
    dp_at = lax.axis_index("dp").astype(jnp.int32)
    quarter = dp_at % QUAD
    meta = jnp.stack([core, quarter, dp_at // QUAD])

    def to_quad(value, j):
        return lax.ppermute(value, "dp", xor_pairs(n_dp, j))

    def to_layer(value, bits):
        return lax.ppermute(value, "dp", xor_pairs(n_dp, bits * QUAD))

    def gather_layers(block):
        blocks = {0: block}
        bit = count // 2
        while bit:
            for k in sorted(blocks):
                blocks[k | bit] = to_layer(blocks[k], bit)
            bit //= 2
        return [blocks[k] for k in range(count)]

    def gather_direct(block):
        return [block] + [to_layer(block, k) for k in range(1, count)]

    halfway = ROT // 2
    frequency = 1.0 / 10000.0 ** (jnp.arange(halfway, dtype=F32) * (2.0 / ROT))
    angles = frequency[:, None] * positions.astype(F32)[None, :]
    earlier = segment_ids[None, :] < segment_ids[:, None]
    start = jnp.sum(earlier.astype(jnp.int32), axis=1)
    start = jnp.concatenate([start // 256, start % 256]).astype(BF16)
    turns = jnp.concatenate([jnp.cos(angles), jnp.sin(angles)], axis=1)
    message = join_message(
        inputs, output_grad, *low_parts(turns, 3), jnp.broadcast_to(start[None], turns.shape)
    )

    first_pack, second_pack = pack_weights(
        meta, attend_weight, project_weight.T, expand_weight, shrink_weight.T
    )
    second_parts = [second_pack[0]]
    second_parts += [to_quad(second_pack[j], j) for j in range(1, QUAD)]
    second_blocks = gather_direct(jnp.stack(second_parts))
    first_parts = [first_pack[0]] + [to_quad(first_pack[j], j) for j in range(1, QUAD)]
    first_blocks = gather_layers(jnp.stack(first_parts))

    whole = [message] + [to_quad(message, j) for j in range(1, QUAD)]
    messages = [(value, swap_cores(value)) for value in whole]

    one_row = lambda vector: vector[None, :]
    bias_part = lax.dynamic_index_in_dim(
        attend_bias.reshape(QUAD, attend_cols // QUAD), quarter, 0, False
    )
    bias_part = jnp.broadcast_to(bias_part[:, None], (attend_cols // QUAD, 128))
    hidden_part = lax.dynamic_index_in_dim(
        expand_bias.reshape(QUAD, hidden_cols // QUAD), quarter, 0, True
    )

    carried, partials = None, {}
    for group in ATTEND_GROUPS:
        results = branch(
            Attend,
            meta,
            one_row(first_gain),
            one_row(first_shift),
            bias_part,
            [messages[s] for s in group],
            [],
            first_blocks,
            carried,
            group is ATTEND_GROUPS[-1],
        )
        (out_part, grad_part), attend_sums, carried = results
        for place, s in enumerate(group):
            partials[s] = (out_part, grad_part, place)
    attend_grads = carried

    carried, sums_of = None, {}
    for group in MLP_GROUPS:
        results = branch(
            Mlp,
            meta,
            one_row(second_gain),
            one_row(second_shift),
            hidden_part,
            [messages[s] for s in group],
            [partials[s] for s in group],
            second_blocks,
            carried,
            group is MLP_GROUPS[-1],
        )
        (mine, other), mlp_sums, carried = results
        other = swap_cores(other)
        for place, s in enumerate(group):
            if s == 0:
                own_halves = mine, other, place
                continue
            sums_of[s] = add_halves(mine, other, place)
    mlp_grads = carried

    parts = [to_quad(sums_of[j], j) for j in range(1, QUAD)]
    outputs, grad_inputs = finish(
        inputs, output_grad, own_halves, parts, one_row(project_bias), one_row(shrink_bias)
    )

    def reduce_layers(grads):
        received = [to_layer(grads[k], k) for k in range(1, count)]
        parts = sum_layers(grads[0], received)
        return parts[0], [to_quad(parts[j], j) for j in range(1, QUAD)]

    own, received = reduce_layers(attend_grads)
    grad_attend, grad_project = unpack_attend(meta, own, received, attend_cols, project_cols)
    own, received = reduce_layers(mlp_grads)
    grad_expand, grad_shrink = unpack_mlp(meta, own, received, hidden_cols)

    place = core * QUAD + quarter
    attend_full = lax.dynamic_update_slice_in_dim(
        jnp.zeros((2 * attend_cols,), F32),
        jnp.sum(attend_sums[1], axis=1),
        place * (attend_cols // QUAD),
        0,
    )
    hidden_full = lax.dynamic_update_slice_in_dim(
        jnp.zeros((2 * hidden_cols,), F32),
        jnp.sum(mlp_sums[1], axis=0),
        place * (hidden_cols // QUAD),
        0,
    )
    vector = jnp.concatenate(
        [
            jnp.sum(attend_sums[0].reshape(2, 8, features), axis=1).reshape(-1),
            jnp.sum(mlp_sums[0].reshape(2, 8, features), axis=1).reshape(-1),
            jnp.sum(output_grad.astype(F32), axis=0),
            attend_full,
            hidden_full,
        ]
    ).reshape(-1, 128)
    vector = vector + swap_cores(vector)
    for bit in (1, 2):
        vector = vector + lax.ppermute(vector, "dp", xor_pairs(n_dp, bit))
    vectors = [vector] + [to_layer(vector, k) for k in range(1, count)]
    sizes = [features] * 4 + [features] * 2 + [2 * attend_cols, 2 * hidden_cols]
    pieces = split_vector(vectors, sizes)
    return (
        outputs,
        grad_inputs,
        *pieces[:4],
        grad_attend,
        pieces[6],
        grad_project.T,
        pieces[4],
        grad_expand,
        pieces[7],
        grad_shrink.T,
        pieces[5],
    )


def solution(mesh):
    n_dp = mesh.shape["dp"]
    assert mesh.shape["tensor"] == 2 and n_dp % QUAD == 0 and n_dp & (n_dp - 1) == 0
    rows = P(("dp", "tensor"), None)
    in_specs = (
        rows,
        P("dp"),
        P("dp"),
        P(),
        P(),
        P(),
        P(),
        P("dp", "tensor"),
        P("tensor"),
        P("tensor", "dp"),
        P(),
        P("dp", "tensor"),
        P("tensor"),
        P("tensor", "dp"),
        P(),
        rows,
    )
    out_specs = (
        rows,
        rows,
        P(),
        P(),
        P(),
        P(),
        P("dp", "tensor"),
        P(),
        P("tensor", "dp"),
        P(),
        P("dp", "tensor"),
        P(),
        P("tensor", "dp"),
        P(),
    )

    def program(*args):
        return on_device(n_dp, *args)

    return jax.shard_map(
        program, mesh=mesh, in_specs=in_specs, out_specs=out_specs, check_vma=False
    )
```

```python
from types import SimpleNamespace

import jax
import jax.numpy as jnp
import numpy as np
from jax import lax
from jax.experimental import pallas as pl
from jax.experimental.pallas import tpu as pltpu
from jax.sharding import PartitionSpec as P


HD = 64
ROT = 16
QUAD = 4
TABLE_ROWS = 32
EPSILON = 1e-05
NEGATIVE = -1e30
QUERY_BLOCK = 256
SMALL_VMEM = 12 << 20
ROW_CHUNK = 32
ATTEND_GROUPS = ((0,), (1, 2), (3,))
MLP_GROUPS = ((3,), (1, 2, 0))
F32 = jnp.float32
BF16 = jnp.bfloat16


HBM = pl.BlockSpec(memory_space=pltpu.HBM)
ANY = pl.BlockSpec(memory_space=pl.ANY)
VMEM = pl.BlockSpec(memory_space=pltpu.VMEM)
SMEM = pl.BlockSpec(memory_space=pltpu.SMEM)


def dot_nn(left, right):
    return lax.dot_general(left, right, (((1,), (0,)), ((), ())), preferred_element_type=F32)


def dot_nt(left, right):
    return lax.dot_general(left, right, (((1,), (1,)), ((), ())), preferred_element_type=F32)


def dot_tn(left, right):
    return lax.dot_general(left, right, (((0,), (0,)), ((), ())), preferred_element_type=F32)


def xor_pairs(n_dp, bits):
    return [(index, index ^ bits) for index in range(n_dp)]


def swap_cores(value):
    return lax.ppermute(value, "tensor", [(0, 1), (1, 0)])


def low_parts(value, number):
    parts = []
    for _ in range(number):
        part = lax.reduce_precision(value, 8, 7)
        parts.append(part.astype(BF16))
        value = value - part
    return parts


def staged_call(body, scalars, arrays, shapes):
    count = len(arrays)

    def whole(*refs):
        at = len(scalars)
        given, sources = refs[:at], refs[at : at + count]
        outs = refs[at + count : at + count + len(shapes)]
        targets, sems = refs[at + count + len(shapes) : -1], refs[-1]
        copies = [
            pltpu.make_async_copy(source, target, sems.at[k])
            for k, (source, target) in enumerate(zip(sources, targets))
        ]
        for copy in copies:
            copy.start()
        for copy in copies:
            copy.wait()
        body(*given, *targets, *outs)

    return pl.pallas_call(
        whole,
        in_specs=[SMEM] * len(scalars) + [ANY] * count,
        out_specs=[VMEM] * len(shapes),
        out_shape=shapes,
        scratch_shapes=[pltpu.VMEM(array.shape, array.dtype) for array in arrays]
        + [pltpu.SemaphoreType.DMA((count,))],
        compiler_params=pltpu.CompilerParams(vmem_limit_bytes=SMALL_VMEM),
    )(*scalars, *arrays)


def pack_body(meta, attend, project, expand, shrink, *outs):
    first, second = outs[:QUAD], outs[QUAD:]
    quarter = meta[1]
    heads = attend.shape[1] // QUAD
    context = project.shape[1] // QUAD
    hidden = expand.shape[1] // QUAD
    for j in range(QUAD):
        at = quarter ^ j
        first[j][:, :heads] = attend[:, pl.ds(pl.multiple_of(at * heads, 128), heads)]
        first[j][:, heads:] = project[:, pl.ds(pl.multiple_of(at * context, 128), context)]
        second[j][0] = expand[:, pl.ds(pl.multiple_of(at * hidden, 128), hidden)]
        second[j][1] = shrink[:, pl.ds(pl.multiple_of(at * hidden, 128), hidden)]


def pack_weights(meta, attend, project, expand, shrink):
    rows = attend.shape[0]
    width = (attend.shape[1] + project.shape[1]) // QUAD
    hidden = expand.shape[1] // QUAD
    parts = pl.pallas_call(
        pack_body,
        in_specs=[SMEM] + [VMEM] * 4,
        out_specs=[VMEM] * (2 * QUAD),
        out_shape=[jax.ShapeDtypeStruct((rows, width), BF16)] * QUAD
        + [jax.ShapeDtypeStruct((2, rows, hidden), BF16)] * QUAD,
    )(meta, attend, project, expand, shrink)
    return parts[:QUAD], parts[QUAD:]


def join_body(*refs):
    parts, message, column_sums = refs[:-2], refs[-2], refs[-1]
    total = fold_rows(parts[1][...].astype(F32))
    column_sums[...] = jnp.sum(total, axis=0, keepdims=True)
    at = 0
    for part in parts:
        message[at : at + part.shape[0]] = part[...]
        at += part.shape[0]


def join_message(*parts):
    rows = sum(part.shape[0] for part in parts)
    return pl.pallas_call(
        join_body,
        in_specs=[VMEM] * len(parts),
        out_specs=[VMEM] * 2,
        out_shape=[
            jax.ShapeDtypeStruct((rows, parts[0].shape[1]), BF16),
            jax.ShapeDtypeStruct((1, parts[0].shape[1]), F32),
        ],
    )(*parts)


def sum_layers_body(keep, *refs):
    received, outs = refs[:-QUAD], refs[-QUAD:]
    for j in range(QUAD):
        total = keep[j]
        for part in received:
            total = total + part[j].astype(F32)
        outs[j][...] = total.astype(outs[j].dtype)


def sum_layers(keep, received):
    shape = keep.shape[1:]
    shapes = [jax.ShapeDtypeStruct(shape, BF16 if j else F32) for j in range(QUAD)]
    return staged_call(sum_layers_body, [], [keep, *received], shapes)


def add_body(mine, other, out, mine_s, other_s, out_s, sems):
    def copies(which):
        pairs = ((mine, mine_s), (other, other_s))
        return [
            pltpu.make_async_copy(source.at[which], target.at[which], sems.at[which, n])
            for n, (source, target) in enumerate(pairs)
        ]

    saves = [
        pltpu.make_async_copy(out_s.at[which], out.at[which], sems.at[which, 2]) for which in (0, 1)
    ]
    for which in (0, 1):
        for copy in copies(which):
            copy.start()
    for which in (0, 1):
        for copy in copies(which):
            copy.wait()
        out_s[which] = (mine_s[which].astype(F32) + other_s[which].astype(F32)).astype(BF16)
        saves[which].start()
    for save in saves:
        save.wait()


def add_halves(mine, other):
    shape = mine.shape
    return pl.pallas_call(
        add_body,
        in_specs=[ANY] * 2,
        out_specs=ANY,
        out_shape=jax.ShapeDtypeStruct(shape, BF16),
        scratch_shapes=[pltpu.VMEM(shape, BF16)] * 3 + [pltpu.SemaphoreType.DMA((2, 3))],
        compiler_params=pltpu.CompilerParams(vmem_limit_bytes=SMALL_VMEM),
    )(mine, other)


def join_vector_body(meta, first, first_bias, second, second_bias, cotangent, out):
    out[...] = jnp.zeros_like(out)
    tiles = first.shape[1] // 128

    def put(at, row):
        for k in range(row.shape[1] // 128):
            out[pl.ds(at + k, 1), :] = row[:, k * 128 : (k + 1) * 128]

    at = 0
    for sums in (first, second):
        for part in (sums[:8], sums[8:]):
            put(at, jnp.sum(part, axis=0, keepdims=True))
            at += tiles
    put(at, cotangent[...])
    at += tiles
    place = meta[0] * QUAD + meta[1]
    row = jnp.sum(first_bias[...].T, axis=0, keepdims=True)
    put(at + place * (row.shape[1] // 128), row)
    at += 2 * QUAD * (row.shape[1] // 128)
    row = jnp.sum(second_bias[...], axis=0, keepdims=True)
    put(at + place * (row.shape[1] // 128), row)


def join_vector(meta, first, first_bias, second, second_bias, cotangent, sizes):
    rows = (sum(sizes) - cotangent.shape[1]) // 128
    return pl.pallas_call(
        join_vector_body,
        in_specs=[SMEM] + [VMEM] * 5,
        out_specs=VMEM,
        out_shape=jax.ShapeDtypeStruct((rows, 128), F32),
    )(meta, first, first_bias, second, second_bias, cotangent)


def split_body(*refs):
    count = len(refs) - 8
    totals = [ref[...] for ref in refs[:count]]
    while len(totals) > 1:
        totals = [first + second for first, second in zip(totals[::2], totals[1::2])]
    at = 0
    for number, out in enumerate(refs[count:]):
        at -= out.shape[0] if number == 5 else 0
        out[...] = totals[0][at : at + out.shape[0]]
        at += out.shape[0]


def split_vector(vectors, sizes):
    shapes = [jax.ShapeDtypeStruct((size // 128, 128), F32) for size in sizes]
    pieces = staged_call(split_body, [], vectors, shapes)
    return [piece.reshape(-1) for piece in pieces]


def unpack_attend_body(meta, own, *refs):
    received, (attend, project) = refs[:3], refs[3:]
    quarter = meta[1]
    heads = attend.shape[1] // QUAD
    context = project.shape[1] // QUAD
    for j in range(QUAD):
        piece = own[...] if j == 0 else received[j - 1][...].astype(F32)
        at = quarter ^ j
        attend[:, pl.ds(pl.multiple_of(at * heads, 128), heads)] = piece[:, :heads]
        project[:, pl.ds(pl.multiple_of(at * context, 128), context)] = piece[:, heads:]


def unpack_attend(meta, own, received, attend_cols, project_cols):
    rows = own.shape[0]
    shapes = [jax.ShapeDtypeStruct((rows, cols), F32) for cols in (attend_cols, project_cols)]
    return staged_call(unpack_attend_body, [meta], [own, *received], shapes)


def unpack_mlp_body(meta, own, *refs):
    received, (expand, shrink) = refs[:3], refs[3:]
    quarter = meta[1]
    hidden = expand.shape[1] // QUAD
    for j in range(QUAD):
        piece = own if j == 0 else received[j - 1]
        lanes = pl.ds(pl.multiple_of((quarter ^ j) * hidden, 128), hidden)
        expand[:, lanes] = piece[0].astype(F32)
        shrink[:, lanes] = piece[1].astype(F32)


def unpack_mlp(meta, own, received, hidden_cols):
    rows = own.shape[1]
    shapes = [jax.ShapeDtypeStruct((rows, hidden_cols), F32)] * 2
    return staged_call(unpack_mlp_body, [meta], [own, *received], shapes)


def row_chunks(length):
    return [slice(c * ROW_CHUNK, (c + 1) * ROW_CHUNK) for c in range(length // ROW_CHUNK)]


def column_chunks(features):
    return [slice(c * 256, (c + 1) * 256) for c in range(features // 256)]


def wait_bytes(view, sem):
    pltpu.make_async_copy(view, view, sem).wait()


def widen(tile, features):
    return jnp.concatenate([tile] * (features // 128), axis=1)


def fold_rows(value):
    return jnp.sum(value.reshape(value.shape[0] // 8, 8, value.shape[1]), axis=0)


def fold_lanes(value):
    tiles = [value[:, k * 128 : (k + 1) * 128] for k in range(value.shape[1] // 128)]
    while len(tiles) > 1:
        tiles = [sum(tiles[k : k + 2]) for k in range(0, len(tiles), 2)]
    return tiles[0]


def normalize(x, gain, shift, norm_s, hat_s):
    length, features = x.shape
    share = np.float32(1.0 / features)

    def some_rows(number, carry):
        for part in range(4):
            at = pl.multiple_of((number * 4 + part) * ROW_CHUNK, ROW_CHUNK)
            rows = pl.ds(at, ROW_CHUNK)
            tokens = x[rows, :].astype(F32)
            centred = tokens - jnp.sum(fold_lanes(tokens), axis=-1, keepdims=True) * share
            variance = jnp.sum(fold_lanes(centred * centred), axis=-1, keepdims=True) * share
            scaled = centred * lax.rsqrt(variance + EPSILON)
            hat_s[rows, :] = scaled
            norm_s[rows, :] = (scaled * gain[...] + shift[...]).astype(BF16)
        return carry

    lax.fori_loop(0, length // (4 * ROW_CHUNK), some_rows, 0)


def rotate_rows(part, cosine, sine):
    half = ROT // 2
    lead, trail = part[:half], part[half:ROT]
    return jnp.concatenate(
        [lead * cosine - trail * sine, trail * cosine + lead * sine, part[ROT:]], axis=0
    )


class Attend:
    picks = (None,)
    turns = True

    @staticmethod
    def scratch(length, features, width):
        return dict(
            mask=pltpu.VMEM((length // QUERY_BLOCK, length, QUERY_BLOCK), F32),
            q=pltpu.VMEM((2, 2 * HD, length), BF16),
            d=pltpu.VMEM((2, 2 * HD, length), BF16),
            kv=pltpu.VMEM((2, length, 2 * HD), BF16),
            kvt=pltpu.VMEM((2, 2 * HD, length), BF16),
            score=pltpu.VMEM((2, length, QUERY_BLOCK), F32),
            gprob=pltpu.VMEM((2, length, QUERY_BLOCK), F32),
            weight=pltpu.VMEM((2, length, QUERY_BLOCK), BF16),
            gprod=pltpu.VMEM((2, length, QUERY_BLOCK), BF16),
            dq=pltpu.VMEM((2, HD, length), F32),
            dk=pltpu.VMEM((2, HD, length), F32),
            dv=pltpu.VMEM((2, HD, length), F32),
            ctxt=pltpu.VMEM((2 * HD, length), BF16),
            ctx=pltpu.VMEM((length, 2 * HD), BF16),
            gmt=pltpu.VMEM((6 * HD, length), BF16),
            gm=pltpu.VMEM((length, 6 * HD), BF16),
        )

    @staticmethod
    def bias_shape(width):
        return (6 * HD, 128)

    @staticmethod
    def cost(length, features, width):
        return 6 * length * features * width + 14 * length * length * 2 * HD, 2 * length**2

    @staticmethod
    def compute(m, norm, cot, w, bias, bias_sums, table):
        length = norm.shape[0]
        heads = 6 * HD
        scale = np.float32(HD ** (-0.5))
        values = sum(table[k * 8 : (k + 1) * 8, :].astype(F32) for k in range(3))
        cosine, sine = values[:, :length], values[:, length:]
        start = table[24:25, :length].astype(F32) * 256.0 + table[24:25, length:].astype(F32)
        for block in range(length // QUERY_BLOCK):
            width = (block + 1) * QUERY_BLOCK
            lanes = slice(block * QUERY_BLOCK, width)
            key_at = lax.broadcasted_iota(jnp.int32, (width, QUERY_BLOCK), 0)
            query_at = lax.broadcasted_iota(jnp.int32, (width, QUERY_BLOCK), 1)
            first = start[:, lanes].astype(jnp.int32)
            allowed = (key_at >= first) & (key_at <= query_at + block * QUERY_BLOCK)
            m.mask[block, :width, :] = jnp.where(allowed, 0.0, NEGATIVE)

        projected = dot_nt(w[:heads, :], norm[...]) + widen(bias[...], length)
        grad_context = dot_nt(w[heads:, :], cot[...]).astype(BF16)
        nothing = jnp.zeros((HD, length), BF16)
        for h in range(2):
            query, key, value = [
                projected[(3 * h + k) * HD : (3 * h + k + 1) * HD] for k in range(3)
            ]
            m.q[h, :HD, :] = (rotate_rows(query, cosine, sine) * scale).astype(BF16)
            m.q[h, HD:, :] = nothing
            m.d[h, :HD, :] = nothing
            m.d[h, HD:, :] = grad_context[h * HD : (h + 1) * HD]
            both = jnp.concatenate([rotate_rows(key, cosine, sine), value], axis=0).astype(BF16)
            m.kvt[h] = both
            m.kv[h] = both.T

        items = [
            (block, h) for block in reversed(range(length // QUERY_BLOCK)) for h in range(2)
        ]

        def place(item):
            block = items[item][0]
            width = (block + 1) * QUERY_BLOCK
            return *items[item], width, slice(block * QUERY_BLOCK, width)

        def products(item):
            _, h, width, lanes = place(item)
            key_value = m.kv[h, :width, :]
            m.score[item % 2, :width, :] = dot_nn(key_value, m.q[h, :, lanes])
            m.gprob[item % 2, :width, :] = dot_nn(key_value, m.d[h, :, lanes])

        def softmax(item):
            block, _, width, _ = place(item)
            scores = m.score[item % 2, :width, :] + m.mask[block, :width, :]
            highest = jnp.max(scores, axis=0, keepdims=True)
            numerators = jnp.exp(scores - highest)
            weights = numerators * (1.0 / jnp.sum(numerators, axis=0, keepdims=True))
            grad_probs = m.gprob[item % 2, :width, :]
            centre = jnp.sum(grad_probs * weights, axis=0, keepdims=True)
            m.weight[item % 2, :width, :] = weights.astype(BF16)
            m.gprod[item % 2, :width, :] = (weights * (grad_probs - centre)).astype(BF16)

        def results(item):
            _, h, width, lanes = place(item)
            weights_low = m.weight[item % 2, :width, :]
            grad_products = m.gprod[item % 2, :width, :]
            context = dot_nn(m.kvt[h, HD:, :width], weights_low)
            m.ctxt[h * HD : (h + 1) * HD, lanes] = context.astype(BF16)
            grad_query = dot_nn(m.kvt[h, :HD, :width], grad_products)
            m.dq[h, :, lanes] = grad_query * scale
            grad_key = dot_nt(m.q[h, :HD, lanes], grad_products)
            grad_value = dot_nt(m.d[h, HD:, lanes], weights_low)
            if width == length:
                m.dk[h] = grad_key
                m.dv[h] = grad_value
            else:
                m.dk[h, :, :width] += grad_key
                m.dv[h, :, :width] += grad_value

        products(0)
        for item in range(len(items)):
            if item + 1 < len(items):
                products(item + 1)
            if item:
                results(item - 1)
            softmax(item)
        results(len(items) - 1)

        for h in range(2):
            parts = [
                rotate_rows(m.dq[h], cosine, -sine),
                rotate_rows(m.dk[h], cosine, -sine),
                m.dv[h],
            ]
            for k, part in enumerate(parts):
                rows = slice((3 * h + k) * HD, (3 * h + k + 1) * HD)
                low = part.astype(BF16)
                m.gmt[rows, :] = low
                bias_sums[rows, :] += fold_lanes(low.astype(F32))
        m.gm[...] = m.gmt[...].T
        m.ctx[...] = m.ctxt[...].T

    @staticmethod
    def accumulate(m, norm, cot, total):
        heads = 6 * HD
        total[0, :heads, :] += dot_nn(m.gmt[...], norm[...])
        total[0, heads:, :] += dot_nn(m.ctxt[...], cot[...])

    @staticmethod
    def forward_out(m, w, cols):
        return dot_nn(m.ctx[...], w[6 * HD :, cols])

    @staticmethod
    def backward_out(m, w, cols):
        return dot_nn(m.gm[...], w[: 6 * HD, cols])


class Mlp:
    picks = (0, 1)
    turns = False

    @staticmethod
    def scratch(length, features, width):
        return dict(
            hid=pltpu.VMEM((2, length, width), F32),
            act=pltpu.VMEM((length, width), BF16),
            dh=pltpu.VMEM((length, width), BF16),
        )

    @staticmethod
    def bias_shape(width):
        return (8, width)

    @staticmethod
    def cost(length, features, width):
        return 12 * length * features * width, 2 * length * width

    @staticmethod
    def compute(m, norm, cot, w, bias, bias_sums, table):
        m.hid[0] = dot_nn(norm[...], w[0]) + bias[...]
        m.hid[1] = dot_nn(cot[...], w[1])
        for rows in row_chunks(norm.shape[0]):
            hid = m.hid[0, rows, :]
            below = 0.5 + 0.5 * lax.erf(hid * np.float32(0.5**0.5))
            slope = below + hid * jnp.exp(-0.5 * (hid * hid)) * np.float32((2 * np.pi) ** -0.5)
            m.act[rows, :] = (hid * below).astype(BF16)
            grad_hid = (slope * m.hid[1, rows, :]).astype(BF16)
            m.dh[rows, :] = grad_hid
            bias_sums[...] += fold_rows(grad_hid.astype(F32))

    @staticmethod
    def accumulate(m, norm, cot, total):
        total[0] += dot_tn(m.dh[...], norm[...])
        total[1] += dot_tn(m.act[...], cot[...])

    @staticmethod
    def forward_out(m, w, cols):
        return dot_nt(m.act[...], w[1, cols, :])

    @staticmethod
    def backward_out(m, w, cols):
        return dot_nt(m.dh[...], w[0, cols, :])


def branch_body(kind, names, n_seq, count, is_first, is_last, places, *refs):
    refs = list(refs)
    take = lambda number: [refs.pop(0) for _ in range(number)]
    (meta, gain, shift, bias) = take(4)
    messages = [take(2) for _ in range(n_seq)]
    partials = [take(2) for _ in places or ()]
    reads_turned = kind.turns and not is_first
    blocks = take(1 if reads_turned else count)
    carried = [] if is_first else take(3)
    outs = take(2 * n_seq if places else 2)
    sums, bias_sums = take(2)
    if is_last:
        grads = take(count)
    else:
        (total_hbm,) = take(1)
        if kind.turns:
            (turned_hbm,) = take(1) if is_first else (None,)
    x_s, d_s, tab_s, w_s, total, norm_s, hat_s, out_st, grad_st = take(9)
    wt_s = take(1)[0] if kind.turns else None
    turned = take(1)[0] if is_last else None
    m = SimpleNamespace(**dict(zip(names, take(len(names)))))
    token_sem, table_sem, weight_sem, part_sem, out_sem, total_sem = take(6)

    length, features = x_s.shape[1:]
    half = length // 2
    mine = pl.multiple_of(meta[0] * half, half)
    other = pl.multiple_of((1 - meta[0]) * half, half)
    rows = features // (QUAD * count)

    weight_copies = []
    if reads_turned:
        weight_copies.append(pltpu.make_async_copy(blocks[0], wt_s, weight_sem.at[0, 0, 0]))
    else:
        for k in range(count):
            for j in range(QUAD):
                place = (meta[2] ^ k) * (QUAD * rows) + (meta[1] ^ j) * rows
                for number, pick in enumerate(kind.picks):
                    source = blocks[k].at[j] if pick is None else blocks[k].at[j, pick]
                    target = w_s.at[number, pl.ds(pl.multiple_of(place, rows), rows)]
                    weight_copies.append(
                        pltpu.make_async_copy(source, target, weight_sem.at[number, k, j])
                    )

    def start_message(i, target, first, which):
        for number, place in enumerate((mine, other)):
            pltpu.make_async_copy(
                messages[i][number].at[pl.ds(first, half)],
                target.at[i, pl.ds(place, half)],
                token_sem.at[i, which, number],
            ).start()

    def start_rest(i):
        start_message(i, d_s, half, 1)
        if kind.turns:
            pltpu.make_async_copy(
                messages[i][0].at[pl.ds(2 * half, TABLE_ROWS)], tab_s.at[i], table_sem.at[i]
            ).start()
        if i == 0:
            for copy in weight_copies:
                copy.start()

    def start_partials(i):
        if places:
            for number, stage in enumerate((out_st, grad_st)):
                pltpu.make_async_copy(
                    partials[i][number].at[places[i]], stage.at[i], part_sem.at[i, number]
                ).start()

    start_message(0, x_s, 0, 0)
    if is_first:
        total[...] = jnp.zeros_like(total)
        sums[...] = jnp.zeros_like(sums)
        bias_sums[...] = jnp.zeros_like(bias_sums)
    else:
        load = pltpu.make_async_copy(carried[0], total, total_sem.at[0])
        sums[...] = carried[1][...]
        bias_sums[...] = carried[2][...]
    saves = []
    if not is_last:
        saves.append(pltpu.make_async_copy(total, total_hbm, total_sem.at[1]))
        if kind.turns and is_first:
            keep = pltpu.make_async_copy(wt_s, turned_hbm, total_sem.at[2])

    def stores(stage, i, which):
        if not places:
            return [pltpu.make_async_copy(stage.at[i], outs[which].at[i], out_sem.at[i, which, 0])]
        return [
            pltpu.make_async_copy(
                stage.at[i, pl.ds(place, half)],
                outs[2 * i + number].at[which],
                out_sem.at[i, which, number],
            )
            for number, place in enumerate((mine, other))
        ]

    def start_stores(stage, i, which):
        if not places or n_seq == 1:
            for copy in stores(stage, i, which):
                copy.start()
            return
        for k in range(n_seq):

            @pl.when(i == k)
            def _(k=k):
                for copy in stores(stage, k, which):
                    copy.start()

    def one_sequence(i, carry):
        for number in range(2):
            wait_bytes(x_s.at[i, pl.ds(0, half)], token_sem.at[i, 0, number])

        @pl.when(i == 0)
        def _():
            start_rest(0)

        normalize(x_s.at[i], gain, shift, norm_s, hat_s)
        if kind.turns:
            wait_bytes(tab_s.at[i], table_sem.at[i])
        for number in range(2):
            wait_bytes(d_s.at[i, pl.ds(0, half)], token_sem.at[i, 1, number])

        @pl.when(i == 0)
        def _():
            for copy in weight_copies:
                copy.wait()
            if not is_first:
                load.start()
            for later in range(1, n_seq):
                start_message(later, x_s, 0, 0)
                start_rest(later)
            for later in range(n_seq):
                start_partials(later)
            if kind.turns and is_first:
                for cols in column_chunks(features):
                    wt_s[:, cols] = w_s[0, cols, :].T
                if not is_last:
                    keep.start()

        cot = d_s.at[i]
        w = wt_s if kind.turns else w_s
        kind.compute(m, norm_s, cot, w, bias, bias_sums, tab_s.at[i])
        if not is_first:

            @pl.when(i == 0)
            def _():
                load.wait()

        kind.accumulate(m, norm_s, cot, total)
        if not is_last:

            @pl.when(i == n_seq - 1)
            def _():
                for copy in saves:
                    copy.start()

        if places:
            wait_bytes(out_st.at[i], part_sem.at[i, 0])
            wait_bytes(grad_st.at[i], part_sem.at[i, 1])
        for cols in column_chunks(features):
            out = kind.forward_out(m, w, cols)
            if places:
                out = out + out_st[i, :, cols].astype(F32)
            out_st[i, :, cols] = out.astype(BF16)
        start_stores(out_st, i, 0)
        for cols in column_chunks(features):
            grad = kind.backward_out(m, w, cols)
            sums[0:8, cols] += fold_rows(grad * hat_s[:, cols])
            sums[8:16, cols] += fold_rows(grad)
            whole = grad * gain[:, cols]
            if places:
                whole = whole + grad_st[i, :, cols].astype(F32)
            grad_st[i, :, cols] = whole.astype(BF16)
        start_stores(grad_st, i, 1)
        return carry

    if n_seq == 1:
        one_sequence(0, 0)
    else:
        lax.fori_loop(0, n_seq, one_sequence, 0)
    if is_last:
        for number, pick in enumerate(kind.picks):
            for cols in column_chunks(features):
                turned[cols, :] = total[number, :, cols].T
            for k in range(count):
                for j in range(QUAD):
                    place = (meta[2] ^ k) * (QUAD * rows) + (meta[1] ^ j) * rows
                    piece = turned[pl.ds(pl.multiple_of(place, rows), rows), :]
                    at = (j,) if pick is None else (j, pick)
                    grads[k][at] = piece.astype(grads[k].dtype)
    for copy in saves:
        copy.wait()
    if kind.turns and is_first and not is_last:
        keep.wait()
    for i in range(n_seq):
        for copy in stores(out_st, i, 0) + stores(grad_st, i, 1):
            copy.wait()


def branch(kind, meta, gain, shift, bias, messages, partials, blocks, carried, is_last):
    n_seq, count, is_first = len(messages), len(blocks), carried is None
    half = (messages[0][0].shape[0] - TABLE_ROWS) // 2
    features = messages[0][0].shape[1]
    length = 2 * half
    width = blocks[0].shape[-1]
    n_pick = len(kind.picks)
    operands = [meta, gain, shift, bias]
    specs = [SMEM] + [VMEM] * 3
    for pair in messages:
        operands += list(pair)
        specs += [ANY] * 2
    for part in partials:
        operands += list(part[:2])
        specs += [HBM] * 2
    places = [part[2] for part in partials]
    if kind.turns and not is_first:
        operands += [carried[3]]
        specs += [HBM]
    else:
        operands += list(blocks)
        specs += [HBM] * count
    if not is_first:
        operands += list(carried[:3])
        specs += [HBM, VMEM, VMEM]
    if places:
        shapes = [jax.ShapeDtypeStruct((2, half, features), BF16)] * (2 * n_seq)
    else:
        shapes = [jax.ShapeDtypeStruct((n_seq, length, features), BF16)] * 2
    n_out = len(shapes)
    shapes += [
        jax.ShapeDtypeStruct((16, features), F32),
        jax.ShapeDtypeStruct(kind.bias_shape(width), F32),
    ]
    out_specs = [HBM] * n_out + [VMEM, VMEM]
    if is_last:
        shape = blocks[0].shape
        shapes += [jax.ShapeDtypeStruct(shape, BF16 if k else F32) for k in range(count)]
        out_specs += [VMEM] * count
    else:
        shapes += [jax.ShapeDtypeStruct((n_pick, width, features), F32)]
        out_specs += [HBM]
        if kind.turns and is_first:
            shapes += [jax.ShapeDtypeStruct((width, features), BF16)]
            out_specs += [HBM]
    scratch = [
        pltpu.VMEM((n_seq, length, features), BF16),
        pltpu.VMEM((n_seq, length, features), BF16),
        pltpu.VMEM((n_seq, TABLE_ROWS, features), BF16),
        pltpu.VMEM((n_pick, features, width), BF16),
        pltpu.VMEM((n_pick, width, features), F32),
        pltpu.VMEM((length, features), BF16),
        pltpu.VMEM((length, features), F32),
        pltpu.VMEM((n_seq, length, features), BF16),
        pltpu.VMEM((n_seq, length, features), BF16),
    ]
    if kind.turns:
        scratch += [pltpu.VMEM((width, features), BF16)]
    if is_last:
        scratch += [pltpu.VMEM((features, width), F32)]
    named = kind.scratch(length, features, width)
    scratch += list(named.values())
    scratch += [
        pltpu.SemaphoreType.DMA((n_seq, 2, 2)),
        pltpu.SemaphoreType.DMA((n_seq,)),
        pltpu.SemaphoreType.DMA((n_pick, count, QUAD)),
        pltpu.SemaphoreType.DMA((n_seq, 2)),
        pltpu.SemaphoreType.DMA((n_seq, 2, 2)),
        pltpu.SemaphoreType.DMA((3,)),
    ]
    flops, transcendentals = kind.cost(length, features, width)
    names = tuple(named)

    def body(*refs):
        branch_body(kind, names, n_seq, count, is_first, is_last, places, *refs)

    call = pl.pallas_call(
        body,
        in_specs=specs,
        out_specs=out_specs,
        out_shape=shapes,
        scratch_shapes=scratch,
        cost_estimate=pl.CostEstimate(
            flops=n_seq * flops,
            bytes_accessed=n_seq * 8 * length * features + 10 * n_pick * width * features,
            transcendentals=n_seq * transcendentals,
        ),
    )
    results = call(*operands)
    outs, sums, rest = results[:n_out], results[n_out : n_out + 2], results[n_out + 2 :]
    if is_last:
        return outs, sums, rest
    turned = () if not kind.turns else (rest[1] if is_first else carried[3],)
    return outs, sums, (rest[0], *sums, *turned)


def finish_body(first_bias, second_bias, x, d, mine, other, p1, p2, p3, out, grad):
    bias = first_bias[...] + second_bias[...]

    def some_rows(number, carry):
        rows = pl.ds(pl.multiple_of(number * ROW_CHUNK, ROW_CHUNK), ROW_CHUNK)

        def total(which):
            own = mine[which, rows, :].astype(F32) + other[which, rows, :].astype(F32)
            pair = p2[which, rows, :].astype(F32) + p3[which, rows, :].astype(F32)
            return own + p1[which, rows, :].astype(F32) + pair

        tokens = x[rows, :].astype(F32)
        out[rows, :] = (tokens + total(0) + bias).astype(BF16)
        back = total(1)
        share = np.float32(1.0 / tokens.shape[1])
        mean = lambda value: jnp.sum(fold_lanes(value), axis=-1, keepdims=True) * share
        centred = tokens - mean(tokens)
        inverse = lax.rsqrt(mean(centred * centred) + EPSILON)
        scaled = centred * inverse
        change = (back - mean(back) - scaled * mean(back * scaled)) * inverse
        grad[rows, :] = (d[rows, :].astype(F32) + change).astype(BF16)
        return carry

    lax.fori_loop(0, x.shape[0] // ROW_CHUNK, some_rows, 0, unroll=2)


def finish(x, d, own, parts, first_bias, second_bias):
    shapes = [jax.ShapeDtypeStruct(x.shape, BF16)] * 2
    arrays = [first_bias, second_bias, x, d, *own, *parts]
    return staged_call(finish_body, [], arrays, shapes)


def on_device(
    n_dp,
    inputs,
    segment_ids,
    positions,
    first_gain,
    first_shift,
    second_gain,
    second_shift,
    attend_weight,
    attend_bias,
    project_weight,
    project_bias,
    expand_weight,
    expand_bias,
    shrink_weight,
    shrink_bias,
    output_grad,
):
    count = n_dp // QUAD
    features = inputs.shape[1]
    attend_cols, hidden_cols = attend_weight.shape[1], expand_weight.shape[1]
    project_cols = project_weight.shape[0]
    core = lax.axis_index("tensor").astype(jnp.int32)
    dp_at = lax.axis_index("dp").astype(jnp.int32)
    quarter = dp_at % QUAD
    meta = jnp.stack([core, quarter, dp_at // QUAD])

    def to_quad(value, j):
        return lax.ppermute(value, "dp", xor_pairs(n_dp, j))

    def to_layer(value, bits):
        return lax.ppermute(value, "dp", xor_pairs(n_dp, bits * QUAD))

    def gather_layers(block):
        blocks = {0: block}
        bit = count // 2
        while bit:
            for k in sorted(blocks):
                blocks[k | bit] = to_layer(blocks[k], bit)
            bit //= 2
        return [blocks[k] for k in range(count)]

    def gather_direct(block):
        return [block] + [to_layer(block, k) for k in range(1, count)]

    halfway = ROT // 2
    frequency = 1.0 / 10000.0 ** (jnp.arange(halfway, dtype=F32) * (2.0 / ROT))
    angles = frequency[:, None] * positions.astype(F32)[None, :]
    earlier = segment_ids[None, :] < segment_ids[:, None]
    start = jnp.sum(earlier.astype(jnp.int32), axis=1)
    start = jnp.concatenate([start // 256, start % 256]).astype(BF16)
    turns = jnp.concatenate([jnp.cos(angles), jnp.sin(angles)], axis=1)
    message, cotangent_sum = join_message(
        inputs, output_grad, *low_parts(turns, 3), jnp.broadcast_to(start[None], turns.shape)
    )

    first_pack, second_pack = pack_weights(
        meta, attend_weight, project_weight.T, expand_weight, shrink_weight.T
    )
    second_parts = [second_pack[0]]
    second_parts += [to_quad(second_pack[j], j) for j in range(1, QUAD)]
    second_blocks = gather_direct(jnp.stack(second_parts))
    first_parts = [first_pack[0]] + [to_quad(first_pack[j], j) for j in range(1, QUAD)]
    first_blocks = gather_layers(jnp.stack(first_parts))

    whole = [message] + [to_quad(message, j) for j in range(1, QUAD)]
    messages = [(value, swap_cores(value)) for value in whole]

    one_row = lambda vector: vector[None, :]
    bias_part = lax.dynamic_index_in_dim(
        attend_bias.reshape(QUAD, attend_cols // QUAD), quarter, 0, False
    )
    bias_part = jnp.broadcast_to(bias_part[:, None], (attend_cols // QUAD, 128))
    hidden_part = lax.dynamic_index_in_dim(
        expand_bias.reshape(QUAD, hidden_cols // QUAD), quarter, 0, True
    )

    carried, partials = None, {}
    for group in ATTEND_GROUPS:
        results = branch(
            Attend,
            meta,
            one_row(first_gain),
            one_row(first_shift),
            bias_part,
            [messages[s] for s in group],
            [],
            first_blocks,
            carried,
            group is ATTEND_GROUPS[-1],
        )
        (out_part, grad_part), attend_sums, carried = results
        for place, s in enumerate(group):
            partials[s] = (out_part, grad_part, place)
    attend_grads = carried

    carried, sums_of = None, {}
    for group in MLP_GROUPS:
        results = branch(
            Mlp,
            meta,
            one_row(second_gain),
            one_row(second_shift),
            hidden_part,
            [messages[s] for s in group],
            [partials[s] for s in group],
            second_blocks,
            carried,
            group is MLP_GROUPS[-1],
        )
        outs, mlp_sums, carried = results
        for place, s in enumerate(group):
            mine, other = outs[2 * place], swap_cores(outs[2 * place + 1])
            if s == 0:
                own_halves = mine, other
                continue
            sums_of[s] = add_halves(mine, other)
    mlp_grads = carried

    parts = [to_quad(sums_of[j], j) for j in range(1, QUAD)]
    outputs, grad_inputs = finish(
        inputs, output_grad, own_halves, parts, one_row(project_bias), one_row(shrink_bias)
    )

    def reduce_layers(grads):
        received = [to_layer(grads[k], k) for k in range(1, count)]
        parts = sum_layers(grads[0], received)
        return parts[0], [to_quad(parts[j], j) for j in range(1, QUAD)]

    own, received = reduce_layers(attend_grads)
    grad_attend, grad_project = unpack_attend(meta, own, received, attend_cols, project_cols)
    own, received = reduce_layers(mlp_grads)
    grad_expand, grad_shrink = unpack_mlp(meta, own, received, hidden_cols)

    sizes = [features] * 4 + [features] * 2 + [2 * attend_cols, 2 * hidden_cols]
    vector = join_vector(meta, *attend_sums, *mlp_sums, cotangent_sum, sizes)
    vector = vector + swap_cores(vector)
    for bit in (1, 2):
        vector = vector + lax.ppermute(vector, "dp", xor_pairs(n_dp, bit))
    vectors = [vector] + [to_layer(vector, k) for k in range(1, count)]
    pieces = split_vector(vectors, sizes)
    return (
        outputs,
        grad_inputs,
        *pieces[:4],
        grad_attend,
        pieces[6],
        grad_project.T,
        pieces[4],
        grad_expand,
        pieces[7],
        grad_shrink.T,
        pieces[5],
    )


def solution(mesh):
    n_dp = mesh.shape["dp"]
    assert mesh.shape["tensor"] == 2 and n_dp % QUAD == 0 and n_dp & (n_dp - 1) == 0
    rows = P(("dp", "tensor"), None)
    in_specs = (
        rows,
        P("dp"),
        P("dp"),
        P(),
        P(),
        P(),
        P(),
        P("dp", "tensor"),
        P("tensor"),
        P("tensor", "dp"),
        P(),
        P("dp", "tensor"),
        P("tensor"),
        P("tensor", "dp"),
        P(),
        rows,
    )
    out_specs = (
        rows,
        rows,
        P(),
        P(),
        P(),
        P(),
        P("dp", "tensor"),
        P(),
        P("tensor", "dp"),
        P(),
        P("dp", "tensor"),
        P(),
        P("tensor", "dp"),
        P(),
    )

    def program(*args):
        return on_device(n_dp, *args)

    return jax.shard_map(
        program, mesh=mesh, in_specs=in_specs, out_specs=out_specs, check_vma=False
    )
```

```python
from types import SimpleNamespace

import jax
import jax.numpy as jnp
import numpy as np
from jax import lax
from jax.experimental import pallas as pl
from jax.experimental.pallas import tpu as pltpu
from jax.sharding import PartitionSpec as P


HD = 64
ROT = 16
QUAD = 4
TABLE_ROWS = 32
EPSILON = 1e-05
NEGATIVE = -1e30
QUERY_BLOCK = 256
SMALL_VMEM = 12 << 20
ROW_CHUNK = 32
ATTEND_GROUPS = ((0,), (1, 2), (3,))
MLP_GROUPS = ((3,), (1, 2, 0))
F32 = jnp.float32
BF16 = jnp.bfloat16


HBM = pl.BlockSpec(memory_space=pltpu.HBM)
ANY = pl.BlockSpec(memory_space=pl.ANY)
VMEM = pl.BlockSpec(memory_space=pltpu.VMEM)
SMEM = pl.BlockSpec(memory_space=pltpu.SMEM)


def dot_nn(left, right):
    return lax.dot_general(left, right, (((1,), (0,)), ((), ())), preferred_element_type=F32)


def dot_nt(left, right):
    return lax.dot_general(left, right, (((1,), (1,)), ((), ())), preferred_element_type=F32)


def dot_tn(left, right):
    return lax.dot_general(left, right, (((0,), (0,)), ((), ())), preferred_element_type=F32)


def xor_pairs(n_dp, bits):
    return [(index, index ^ bits) for index in range(n_dp)]


def swap_cores(value):
    return lax.ppermute(value, "tensor", [(0, 1), (1, 0)])


def low_parts(value, number):
    parts = []
    for _ in range(number):
        part = lax.reduce_precision(value, 8, 7)
        parts.append(part.astype(BF16))
        value = value - part
    return parts


def staged_call(body, scalars, arrays, shapes):
    count = len(arrays)

    def whole(*refs):
        at = len(scalars)
        given, sources = refs[:at], refs[at : at + count]
        outs = refs[at + count : at + count + len(shapes)]
        targets, sems = refs[at + count + len(shapes) : -1], refs[-1]
        copies = [
            pltpu.make_async_copy(source, target, sems.at[k])
            for k, (source, target) in enumerate(zip(sources, targets))
        ]
        for copy in copies:
            copy.start()
        for copy in copies:
            copy.wait()
        body(*given, *targets, *outs)

    return pl.pallas_call(
        whole,
        in_specs=[SMEM] * len(scalars) + [ANY] * count,
        out_specs=[VMEM] * len(shapes),
        out_shape=shapes,
        scratch_shapes=[pltpu.VMEM(array.shape, array.dtype) for array in arrays]
        + [pltpu.SemaphoreType.DMA((count,))],
        compiler_params=pltpu.CompilerParams(vmem_limit_bytes=SMALL_VMEM),
    )(*scalars, *arrays)


def pack_body(meta, attend, project, expand, shrink, *outs):
    first, second = outs[:QUAD], outs[QUAD:]
    quarter = meta[1]
    heads = attend.shape[1] // QUAD
    context = project.shape[1] // QUAD
    hidden = expand.shape[1] // QUAD
    for j in range(QUAD):
        at = quarter ^ j
        first[j][:, :heads] = attend[:, pl.ds(pl.multiple_of(at * heads, 128), heads)]
        first[j][:, heads:] = project[:, pl.ds(pl.multiple_of(at * context, 128), context)]
        second[j][0] = expand[:, pl.ds(pl.multiple_of(at * hidden, 128), hidden)]
        second[j][1] = shrink[:, pl.ds(pl.multiple_of(at * hidden, 128), hidden)]


def pack_weights(meta, attend, project, expand, shrink):
    rows = attend.shape[0]
    width = (attend.shape[1] + project.shape[1]) // QUAD
    hidden = expand.shape[1] // QUAD
    parts = pl.pallas_call(
        pack_body,
        in_specs=[SMEM] + [VMEM] * 4,
        out_specs=[VMEM] * (2 * QUAD),
        out_shape=[jax.ShapeDtypeStruct((rows, width), BF16)] * QUAD
        + [jax.ShapeDtypeStruct((2, rows, hidden), BF16)] * QUAD,
    )(meta, attend, project, expand, shrink)
    return parts[:QUAD], parts[QUAD:]


def join_body(*refs):
    parts, message, column_sums = refs[:-2], refs[-2], refs[-1]
    total = fold_rows(parts[1][...].astype(F32))
    column_sums[...] = jnp.sum(total, axis=0, keepdims=True)
    at = 0
    for part in parts:
        message[at : at + part.shape[0]] = part[...]
        at += part.shape[0]


def join_message(*parts):
    rows = sum(part.shape[0] for part in parts)
    return pl.pallas_call(
        join_body,
        in_specs=[VMEM] * len(parts),
        out_specs=[VMEM] * 2,
        out_shape=[
            jax.ShapeDtypeStruct((rows, parts[0].shape[1]), BF16),
            jax.ShapeDtypeStruct((1, parts[0].shape[1]), F32),
        ],
    )(*parts)


def sum_layers_body(keep, *refs):
    received, outs = refs[:-QUAD], refs[-QUAD:]
    for j in range(QUAD):
        total = keep[j]
        for part in received:
            total = total + part[j].astype(F32)
        outs[j][...] = total.astype(outs[j].dtype)


def sum_layers(keep, received):
    shape = keep.shape[1:]
    shapes = [jax.ShapeDtypeStruct(shape, BF16 if j else F32) for j in range(QUAD)]
    return staged_call(sum_layers_body, [], [keep, *received], shapes)


def add_body(mine, other, out, mine_s, other_s, out_s, sems):
    def copies(which):
        pairs = ((mine, mine_s), (other, other_s))
        return [
            pltpu.make_async_copy(source.at[which], target.at[which], sems.at[which, n])
            for n, (source, target) in enumerate(pairs)
        ]

    saves = [
        pltpu.make_async_copy(out_s.at[which], out.at[which], sems.at[which, 2]) for which in (0, 1)
    ]
    for which in (0, 1):
        for copy in copies(which):
            copy.start()
    for which in (0, 1):
        for copy in copies(which):
            copy.wait()
        out_s[which] = (mine_s[which].astype(F32) + other_s[which].astype(F32)).astype(BF16)
        saves[which].start()
    for save in saves:
        save.wait()


def add_halves(mine, other):
    shape = mine.shape
    return pl.pallas_call(
        add_body,
        in_specs=[ANY] * 2,
        out_specs=ANY,
        out_shape=jax.ShapeDtypeStruct(shape, BF16),
        scratch_shapes=[pltpu.VMEM(shape, BF16)] * 3 + [pltpu.SemaphoreType.DMA((2, 3))],
        compiler_params=pltpu.CompilerParams(vmem_limit_bytes=SMALL_VMEM),
    )(mine, other)


def join_vector_body(meta, first, first_bias, second, second_bias, cotangent, out):
    out[...] = jnp.zeros_like(out)
    tiles = first.shape[1] // 128

    def put(at, row):
        for k in range(row.shape[1] // 128):
            out[pl.ds(at + k, 1), :] = row[:, k * 128 : (k + 1) * 128]

    at = 0
    for sums in (first, second):
        for part in (sums[:8], sums[8:]):
            put(at, jnp.sum(part, axis=0, keepdims=True))
            at += tiles
    put(at, cotangent[...])
    at += tiles
    place = meta[0] * QUAD + meta[1]
    row = jnp.sum(first_bias[...].T, axis=0, keepdims=True)
    put(at + place * (row.shape[1] // 128), row)
    at += 2 * QUAD * (row.shape[1] // 128)
    row = jnp.sum(second_bias[...], axis=0, keepdims=True)
    put(at + place * (row.shape[1] // 128), row)


def join_vector(meta, first, first_bias, second, second_bias, cotangent, sizes):
    rows = (sum(sizes) - cotangent.shape[1]) // 128
    return pl.pallas_call(
        join_vector_body,
        in_specs=[SMEM] + [VMEM] * 5,
        out_specs=VMEM,
        out_shape=jax.ShapeDtypeStruct((rows, 128), F32),
    )(meta, first, first_bias, second, second_bias, cotangent)


def split_body(*refs):
    count = len(refs) - 8
    totals = [ref[...] for ref in refs[:count]]
    while len(totals) > 1:
        totals = [first + second for first, second in zip(totals[::2], totals[1::2])]
    at = 0
    for number, out in enumerate(refs[count:]):
        at -= out.shape[0] if number == 5 else 0
        out[...] = totals[0][at : at + out.shape[0]]
        at += out.shape[0]


def split_vector(vectors, sizes):
    shapes = [jax.ShapeDtypeStruct((size // 128, 128), F32) for size in sizes]
    pieces = staged_call(split_body, [], vectors, shapes)
    return [piece.reshape(-1) for piece in pieces]


def unpack_attend_body(meta, own, *refs):
    received, (attend, project) = refs[:3], refs[3:]
    quarter = meta[1]
    heads = attend.shape[1] // QUAD
    context = project.shape[1] // QUAD
    for j in range(QUAD):
        piece = own[...] if j == 0 else received[j - 1][...].astype(F32)
        at = quarter ^ j
        attend[:, pl.ds(pl.multiple_of(at * heads, 128), heads)] = piece[:, :heads]
        project[:, pl.ds(pl.multiple_of(at * context, 128), context)] = piece[:, heads:]


def unpack_attend(meta, own, received, attend_cols, project_cols):
    rows = own.shape[0]
    shapes = [jax.ShapeDtypeStruct((rows, cols), F32) for cols in (attend_cols, project_cols)]
    return staged_call(unpack_attend_body, [meta], [own, *received], shapes)


def unpack_mlp_body(meta, own, *refs):
    received, (expand, shrink) = refs[:3], refs[3:]
    quarter = meta[1]
    hidden = expand.shape[1] // QUAD
    for j in range(QUAD):
        piece = own if j == 0 else received[j - 1]
        lanes = pl.ds(pl.multiple_of((quarter ^ j) * hidden, 128), hidden)
        expand[:, lanes] = piece[0].astype(F32)
        shrink[:, lanes] = piece[1].astype(F32)


def unpack_mlp(meta, own, received, hidden_cols):
    rows = own.shape[1]
    shapes = [jax.ShapeDtypeStruct((rows, hidden_cols), F32)] * 2
    return staged_call(unpack_mlp_body, [meta], [own, *received], shapes)


def row_chunks(length):
    return [slice(c * ROW_CHUNK, (c + 1) * ROW_CHUNK) for c in range(length // ROW_CHUNK)]


def column_chunks(features):
    return [slice(c * 256, (c + 1) * 256) for c in range(features // 256)]


def wait_bytes(view, sem):
    pltpu.make_async_copy(view, view, sem).wait()


def widen(tile, features):
    return jnp.concatenate([tile] * (features // 128), axis=1)


def fold_rows(value):
    return jnp.sum(value.reshape(value.shape[0] // 8, 8, value.shape[1]), axis=0)


def fold_lanes(value):
    tiles = [value[:, k * 128 : (k + 1) * 128] for k in range(value.shape[1] // 128)]
    while len(tiles) > 1:
        tiles = [sum(tiles[k : k + 2]) for k in range(0, len(tiles), 2)]
    return tiles[0]


def normalize(x, gain, shift, norm_s, hat_s):
    length, features = x.shape
    share = np.float32(1.0 / features)

    def some_rows(number, carry):
        for part in range(4):
            at = pl.multiple_of((number * 4 + part) * ROW_CHUNK, ROW_CHUNK)
            rows = pl.ds(at, ROW_CHUNK)
            tokens = x[rows, :].astype(F32)
            centred = tokens - jnp.sum(fold_lanes(tokens), axis=-1, keepdims=True) * share
            variance = jnp.sum(fold_lanes(centred * centred), axis=-1, keepdims=True) * share
            scaled = centred * lax.rsqrt(variance + EPSILON)
            hat_s[rows, :] = scaled
            norm_s[rows, :] = (scaled * gain[...] + shift[...]).astype(BF16)
        return carry

    lax.fori_loop(0, length // (4 * ROW_CHUNK), some_rows, 0)


def rotate_rows(part, cosine, sine):
    half = ROT // 2
    lead, trail = part[:half], part[half:ROT]
    return jnp.concatenate(
        [lead * cosine - trail * sine, trail * cosine + lead * sine, part[ROT:]], axis=0
    )


class Attend:
    picks = (None,)
    turns = True

    @staticmethod
    def scratch(length, features, width):
        return dict(
            mask=pltpu.VMEM((length // QUERY_BLOCK, length, QUERY_BLOCK), F32),
            q=pltpu.VMEM((2, 2 * HD, length), BF16),
            d=pltpu.VMEM((2, 2 * HD, length), BF16),
            kv=pltpu.VMEM((2, length, 2 * HD), BF16),
            kvt=pltpu.VMEM((2, 2 * HD, length), BF16),
            score=pltpu.VMEM((2, length, QUERY_BLOCK), F32),
            gprob=pltpu.VMEM((2, length, QUERY_BLOCK), F32),
            weight=pltpu.VMEM((2, length, QUERY_BLOCK), BF16),
            gprod=pltpu.VMEM((2, length, QUERY_BLOCK), BF16),
            dq=pltpu.VMEM((2, HD, length), F32),
            dk=pltpu.VMEM((2, HD, length), F32),
            dv=pltpu.VMEM((2, HD, length), F32),
            ctxt=pltpu.VMEM((2 * HD, length), BF16),
            ctx=pltpu.VMEM((length, 2 * HD), BF16),
            gmt=pltpu.VMEM((6 * HD, length), BF16),
            gm=pltpu.VMEM((length, 6 * HD), BF16),
        )

    @staticmethod
    def bias_shape(width):
        return (6 * HD, 128)

    @staticmethod
    def cost(length, features, width):
        return 6 * length * features * width + 14 * length * length * 2 * HD, 2 * length**2

    @staticmethod
    def compute(m, norm, cot, w, bias, bias_sums, table):
        length = norm.shape[0]
        heads = 6 * HD
        scale = np.float32(HD ** (-0.5))
        values = sum(table[k * 8 : (k + 1) * 8, :].astype(F32) for k in range(3))
        cosine, sine = values[:, :length], values[:, length:]
        start = table[24:25, :length].astype(F32) * 256.0 + table[24:25, length:].astype(F32)
        for block in range(length // QUERY_BLOCK):
            width = (block + 1) * QUERY_BLOCK
            lanes = slice(block * QUERY_BLOCK, width)
            key_at = lax.broadcasted_iota(jnp.int32, (width, QUERY_BLOCK), 0)
            query_at = lax.broadcasted_iota(jnp.int32, (width, QUERY_BLOCK), 1)
            first = start[:, lanes].astype(jnp.int32)
            allowed = (key_at >= first) & (key_at <= query_at + block * QUERY_BLOCK)
            m.mask[block, :width, :] = jnp.where(allowed, 0.0, NEGATIVE)

        column = jnp.broadcast_to(bias[...], (128, heads)).T
        projected = dot_nt(w[:heads, :], norm[...]) + widen(column, length)
        grad_context = dot_nt(w[heads:, :], cot[...]).astype(BF16)
        nothing = jnp.zeros((HD, length), BF16)
        for h in range(2):
            query, key, value = [
                projected[(3 * h + k) * HD : (3 * h + k + 1) * HD] for k in range(3)
            ]
            m.q[h, :HD, :] = (rotate_rows(query, cosine, sine) * scale).astype(BF16)
            m.q[h, HD:, :] = nothing
            m.d[h, :HD, :] = nothing
            m.d[h, HD:, :] = grad_context[h * HD : (h + 1) * HD]
            both = jnp.concatenate([rotate_rows(key, cosine, sine), value], axis=0).astype(BF16)
            m.kvt[h] = both
            m.kv[h] = both.T

        items = [
            (block, h) for block in reversed(range(length // QUERY_BLOCK)) for h in range(2)
        ]

        def place(item):
            block = items[item][0]
            width = (block + 1) * QUERY_BLOCK
            return *items[item], width, slice(block * QUERY_BLOCK, width)

        def products(item):
            _, h, width, lanes = place(item)
            key_value = m.kv[h, :width, :]
            m.score[item % 2, :width, :] = dot_nn(key_value, m.q[h, :, lanes])
            m.gprob[item % 2, :width, :] = dot_nn(key_value, m.d[h, :, lanes])

        def softmax(item):
            block, _, width, _ = place(item)
            scores = m.score[item % 2, :width, :] + m.mask[block, :width, :]
            highest = jnp.max(scores, axis=0, keepdims=True)
            numerators = jnp.exp(scores - highest)
            weights = numerators * (1.0 / jnp.sum(numerators, axis=0, keepdims=True))
            grad_probs = m.gprob[item % 2, :width, :]
            centre = jnp.sum(grad_probs * weights, axis=0, keepdims=True)
            m.weight[item % 2, :width, :] = weights.astype(BF16)
            m.gprod[item % 2, :width, :] = (weights * (grad_probs - centre)).astype(BF16)

        def results(item):
            _, h, width, lanes = place(item)
            weights_low = m.weight[item % 2, :width, :]
            grad_products = m.gprod[item % 2, :width, :]
            context = dot_nn(m.kvt[h, HD:, :width], weights_low)
            m.ctxt[h * HD : (h + 1) * HD, lanes] = context.astype(BF16)
            grad_query = dot_nn(m.kvt[h, :HD, :width], grad_products)
            m.dq[h, :, lanes] = grad_query * scale
            grad_key = dot_nt(m.q[h, :HD, lanes], grad_products)
            grad_value = dot_nt(m.d[h, HD:, lanes], weights_low)
            if width == length:
                m.dk[h] = grad_key
                m.dv[h] = grad_value
            else:
                m.dk[h, :, :width] += grad_key
                m.dv[h, :, :width] += grad_value

        products(0)
        for item in range(len(items)):
            if item + 1 < len(items):
                products(item + 1)
            if item:
                results(item - 1)
            softmax(item)
        results(len(items) - 1)

        for h in range(2):
            parts = [
                rotate_rows(m.dq[h], cosine, -sine),
                rotate_rows(m.dk[h], cosine, -sine),
                m.dv[h],
            ]
            for k, part in enumerate(parts):
                rows = slice((3 * h + k) * HD, (3 * h + k + 1) * HD)
                low = part.astype(BF16)
                m.gmt[rows, :] = low
                bias_sums[rows, :] += fold_lanes(low.astype(F32))
        m.gm[...] = m.gmt[...].T
        m.ctx[...] = m.ctxt[...].T

    @staticmethod
    def accumulate(m, norm, cot, total):
        heads = 6 * HD
        total[0, :heads, :] += dot_nn(m.gmt[...], norm[...])
        total[0, heads:, :] += dot_nn(m.ctxt[...], cot[...])

    @staticmethod
    def forward_out(m, w, cols):
        return dot_nn(m.ctx[...], w[6 * HD :, cols])

    @staticmethod
    def backward_out(m, w, cols):
        return dot_nn(m.gm[...], w[: 6 * HD, cols])


class Mlp:
    picks = (0, 1)
    turns = False

    @staticmethod
    def scratch(length, features, width):
        return dict(
            hid=pltpu.VMEM((2, length, width), F32),
            act=pltpu.VMEM((length, width), BF16),
            dh=pltpu.VMEM((length, width), BF16),
        )

    @staticmethod
    def bias_shape(width):
        return (8, width)

    @staticmethod
    def cost(length, features, width):
        return 12 * length * features * width, 2 * length * width

    @staticmethod
    def compute(m, norm, cot, w, bias, bias_sums, table):
        m.hid[0] = dot_nn(norm[...], w[0]) + bias[...]
        m.hid[1] = dot_nn(cot[...], w[1])
        for rows in row_chunks(norm.shape[0]):
            hid = m.hid[0, rows, :]
            below = 0.5 + 0.5 * lax.erf(hid * np.float32(0.5**0.5))
            slope = below + hid * jnp.exp(-0.5 * (hid * hid)) * np.float32((2 * np.pi) ** -0.5)
            m.act[rows, :] = (hid * below).astype(BF16)
            grad_hid = (slope * m.hid[1, rows, :]).astype(BF16)
            m.dh[rows, :] = grad_hid
            bias_sums[...] += fold_rows(grad_hid.astype(F32))

    @staticmethod
    def accumulate(m, norm, cot, total):
        total[0] += dot_tn(m.dh[...], norm[...])
        total[1] += dot_tn(m.act[...], cot[...])

    @staticmethod
    def forward_out(m, w, cols):
        return dot_nt(m.act[...], w[1, cols, :])

    @staticmethod
    def backward_out(m, w, cols):
        return dot_nt(m.dh[...], w[0, cols, :])


def branch_body(kind, names, n_seq, count, is_first, is_last, places, *refs):
    refs = list(refs)
    take = lambda number: [refs.pop(0) for _ in range(number)]
    (meta, gain, shift, bias) = take(4)
    messages = [take(2) for _ in range(n_seq)]
    partials = [take(2) for _ in places or ()]
    reads_turned = kind.turns and not is_first
    blocks = take(1 if reads_turned else count)
    carried = [] if is_first else take(3)
    outs = take(2 * n_seq if places else 2)
    sums, bias_sums = take(2)
    if is_last:
        grads = take(count)
    else:
        (total_hbm,) = take(1)
        if kind.turns:
            (turned_hbm,) = take(1) if is_first else (None,)
    x_s, d_s, tab_s, w_s, total, norm_s, hat_s, out_st, grad_st = take(9)
    wt_s = take(1)[0] if kind.turns else None
    turned = take(1)[0] if is_last else None
    m = SimpleNamespace(**dict(zip(names, take(len(names)))))
    token_sem, table_sem, weight_sem, part_sem, out_sem, total_sem = take(6)

    length, features = x_s.shape[1:]
    half = length // 2
    mine = pl.multiple_of(meta[0] * half, half)
    other = pl.multiple_of((1 - meta[0]) * half, half)
    rows = features // (QUAD * count)

    weight_copies = []
    if reads_turned:
        weight_copies.append(pltpu.make_async_copy(blocks[0], wt_s, weight_sem.at[0, 0, 0]))
    else:
        for k in range(count):
            for j in range(QUAD):
                place = (meta[2] ^ k) * (QUAD * rows) + (meta[1] ^ j) * rows
                for number, pick in enumerate(kind.picks):
                    source = blocks[k].at[j] if pick is None else blocks[k].at[j, pick]
                    target = w_s.at[number, pl.ds(pl.multiple_of(place, rows), rows)]
                    weight_copies.append(
                        pltpu.make_async_copy(source, target, weight_sem.at[number, k, j])
                    )

    def start_message(i, target, first, which):
        for number, place in enumerate((mine, other)):
            pltpu.make_async_copy(
                messages[i][number].at[pl.ds(first, half)],
                target.at[i, pl.ds(place, half)],
                token_sem.at[i, which, number],
            ).start()

    def start_rest(i):
        start_message(i, d_s, half, 1)
        if kind.turns:
            pltpu.make_async_copy(
                messages[i][0].at[pl.ds(2 * half, TABLE_ROWS)], tab_s.at[i], table_sem.at[i]
            ).start()
        if i == 0:
            for copy in weight_copies:
                copy.start()

    def start_partials(i):
        if places:
            for number, stage in enumerate((out_st, grad_st)):
                pltpu.make_async_copy(
                    partials[i][number].at[places[i]], stage.at[i], part_sem.at[i, number]
                ).start()

    start_message(0, x_s, 0, 0)
    if is_first:
        total[...] = jnp.zeros_like(total)
        sums[...] = jnp.zeros_like(sums)
        bias_sums[...] = jnp.zeros_like(bias_sums)
    else:
        load = pltpu.make_async_copy(carried[0], total, total_sem.at[0])
        sums[...] = carried[1][...]
        bias_sums[...] = carried[2][...]
    saves = []
    if not is_last:
        saves.append(pltpu.make_async_copy(total, total_hbm, total_sem.at[1]))
        if kind.turns and is_first:
            keep = pltpu.make_async_copy(wt_s, turned_hbm, total_sem.at[2])

    def stores(stage, i, which):
        if not places:
            return [pltpu.make_async_copy(stage.at[i], outs[which].at[i], out_sem.at[i, which, 0])]
        return [
            pltpu.make_async_copy(
                stage.at[i, pl.ds(place, half)],
                outs[2 * i + number].at[which],
                out_sem.at[i, which, number],
            )
            for number, place in enumerate((mine, other))
        ]

    def start_stores(stage, i, which):
        if not places or n_seq == 1:
            for copy in stores(stage, i, which):
                copy.start()
            return
        for k in range(n_seq):

            @pl.when(i == k)
            def _(k=k):
                for copy in stores(stage, k, which):
                    copy.start()

    def one_sequence(i, carry):
        for number in range(2):
            wait_bytes(x_s.at[i, pl.ds(0, half)], token_sem.at[i, 0, number])

        @pl.when(i == 0)
        def _():
            start_rest(0)

        normalize(x_s.at[i], gain, shift, norm_s, hat_s)
        if kind.turns:
            wait_bytes(tab_s.at[i], table_sem.at[i])
        for number in range(2):
            wait_bytes(d_s.at[i, pl.ds(0, half)], token_sem.at[i, 1, number])

        @pl.when(i == 0)
        def _():
            for copy in weight_copies:
                copy.wait()
            if not is_first:
                load.start()
            for later in range(1, n_seq):
                start_message(later, x_s, 0, 0)
                start_rest(later)
            for later in range(n_seq):
                start_partials(later)
            if kind.turns and is_first:
                for cols in column_chunks(features):
                    wt_s[:, cols] = w_s[0, cols, :].T
                if not is_last:
                    keep.start()

        cot = d_s.at[i]
        w = wt_s if kind.turns else w_s
        kind.compute(m, norm_s, cot, w, bias, bias_sums, tab_s.at[i])
        if not is_first:

            @pl.when(i == 0)
            def _():
                load.wait()

        kind.accumulate(m, norm_s, cot, total)
        if not is_last:

            @pl.when(i == n_seq - 1)
            def _():
                for copy in saves:
                    copy.start()

        if places:
            wait_bytes(out_st.at[i], part_sem.at[i, 0])
            wait_bytes(grad_st.at[i], part_sem.at[i, 1])
        for cols in column_chunks(features):
            out = kind.forward_out(m, w, cols)
            if places:
                out = out + out_st[i, :, cols].astype(F32)
            out_st[i, :, cols] = out.astype(BF16)
        start_stores(out_st, i, 0)
        for cols in column_chunks(features):
            grad = kind.backward_out(m, w, cols)
            sums[0:8, cols] += fold_rows(grad * hat_s[:, cols])
            sums[8:16, cols] += fold_rows(grad)
            whole = grad * gain[:, cols]
            if places:
                whole = whole + grad_st[i, :, cols].astype(F32)
            grad_st[i, :, cols] = whole.astype(BF16)
        start_stores(grad_st, i, 1)
        return carry

    if n_seq == 1:
        one_sequence(0, 0)
    else:
        lax.fori_loop(0, n_seq, one_sequence, 0)
    if is_last:
        for number, pick in enumerate(kind.picks):
            for cols in column_chunks(features):
                turned[cols, :] = total[number, :, cols].T
            for k in range(count):
                for j in range(QUAD):
                    place = (meta[2] ^ k) * (QUAD * rows) + (meta[1] ^ j) * rows
                    piece = turned[pl.ds(pl.multiple_of(place, rows), rows), :]
                    at = (j,) if pick is None else (j, pick)
                    grads[k][at] = piece.astype(grads[k].dtype)
    for copy in saves:
        copy.wait()
    if kind.turns and is_first and not is_last:
        keep.wait()
    for i in range(n_seq):
        for copy in stores(out_st, i, 0) + stores(grad_st, i, 1):
            copy.wait()


def branch(kind, meta, gain, shift, bias, messages, partials, blocks, carried, is_last):
    n_seq, count, is_first = len(messages), len(blocks), carried is None
    half = (messages[0][0].shape[0] - TABLE_ROWS) // 2
    features = messages[0][0].shape[1]
    length = 2 * half
    width = blocks[0].shape[-1]
    n_pick = len(kind.picks)
    operands = [meta, gain, shift, bias]
    specs = [SMEM] + [VMEM] * 3
    for pair in messages:
        operands += list(pair)
        specs += [ANY] * 2
    for part in partials:
        operands += list(part[:2])
        specs += [HBM] * 2
    places = [part[2] for part in partials]
    if kind.turns and not is_first:
        operands += [carried[3]]
        specs += [HBM]
    else:
        operands += list(blocks)
        specs += [HBM] * count
    if not is_first:
        operands += list(carried[:3])
        specs += [HBM, VMEM, VMEM]
    if places:
        shapes = [jax.ShapeDtypeStruct((2, half, features), BF16)] * (2 * n_seq)
    else:
        shapes = [jax.ShapeDtypeStruct((n_seq, length, features), BF16)] * 2
    n_out = len(shapes)
    shapes += [
        jax.ShapeDtypeStruct((16, features), F32),
        jax.ShapeDtypeStruct(kind.bias_shape(width), F32),
    ]
    out_specs = [HBM] * n_out + [VMEM, VMEM]
    if is_last:
        shape = blocks[0].shape
        shapes += [jax.ShapeDtypeStruct(shape, BF16 if k else F32) for k in range(count)]
        out_specs += [VMEM] * count
    else:
        shapes += [jax.ShapeDtypeStruct((n_pick, width, features), F32)]
        out_specs += [HBM]
        if kind.turns and is_first:
            shapes += [jax.ShapeDtypeStruct((width, features), BF16)]
            out_specs += [HBM]
    scratch = [
        pltpu.VMEM((n_seq, length, features), BF16),
        pltpu.VMEM((n_seq, length, features), BF16),
        pltpu.VMEM((n_seq, TABLE_ROWS, features), BF16),
        pltpu.VMEM((n_pick, features, width), BF16),
        pltpu.VMEM((n_pick, width, features), F32),
        pltpu.VMEM((length, features), BF16),
        pltpu.VMEM((length, features), F32),
        pltpu.VMEM((n_seq, length, features), BF16),
        pltpu.VMEM((n_seq, length, features), BF16),
    ]
    if kind.turns:
        scratch += [pltpu.VMEM((width, features), BF16)]
    if is_last:
        scratch += [pltpu.VMEM((features, width), F32)]
    named = kind.scratch(length, features, width)
    scratch += list(named.values())
    scratch += [
        pltpu.SemaphoreType.DMA((n_seq, 2, 2)),
        pltpu.SemaphoreType.DMA((n_seq,)),
        pltpu.SemaphoreType.DMA((n_pick, count, QUAD)),
        pltpu.SemaphoreType.DMA((n_seq, 2)),
        pltpu.SemaphoreType.DMA((n_seq, 2, 2)),
        pltpu.SemaphoreType.DMA((3,)),
    ]
    flops, transcendentals = kind.cost(length, features, width)
    names = tuple(named)

    def body(*refs):
        branch_body(kind, names, n_seq, count, is_first, is_last, places, *refs)

    call = pl.pallas_call(
        body,
        in_specs=specs,
        out_specs=out_specs,
        out_shape=shapes,
        scratch_shapes=scratch,
        cost_estimate=pl.CostEstimate(
            flops=n_seq * flops,
            bytes_accessed=n_seq * 8 * length * features + 10 * n_pick * width * features,
            transcendentals=n_seq * transcendentals,
        ),
    )
    results = call(*operands)
    outs, sums, rest = results[:n_out], results[n_out : n_out + 2], results[n_out + 2 :]
    if is_last:
        return outs, sums, rest
    turned = () if not kind.turns else (rest[1] if is_first else carried[3],)
    return outs, sums, (rest[0], *sums, *turned)


def finish_body(first_bias, second_bias, x, d, mine, other, p1, p2, p3, out, grad):
    bias = first_bias[...] + second_bias[...]

    def some_rows(number, carry):
        rows = pl.ds(pl.multiple_of(number * ROW_CHUNK, ROW_CHUNK), ROW_CHUNK)

        def total(which):
            own = mine[which, rows, :].astype(F32) + other[which, rows, :].astype(F32)
            pair = p2[which, rows, :].astype(F32) + p3[which, rows, :].astype(F32)
            return own + p1[which, rows, :].astype(F32) + pair

        tokens = x[rows, :].astype(F32)
        out[rows, :] = (tokens + total(0) + bias).astype(BF16)
        back = total(1)
        share = np.float32(1.0 / tokens.shape[1])
        mean = lambda value: jnp.sum(fold_lanes(value), axis=-1, keepdims=True) * share
        centred = tokens - mean(tokens)
        inverse = lax.rsqrt(mean(centred * centred) + EPSILON)
        scaled = centred * inverse
        change = (back - mean(back) - scaled * mean(back * scaled)) * inverse
        grad[rows, :] = (d[rows, :].astype(F32) + change).astype(BF16)
        return carry

    lax.fori_loop(0, x.shape[0] // ROW_CHUNK, some_rows, 0, unroll=2)


def finish(x, d, own, parts, first_bias, second_bias):
    shapes = [jax.ShapeDtypeStruct(x.shape, BF16)] * 2
    arrays = [first_bias, second_bias, x, d, *own, *parts]
    return staged_call(finish_body, [], arrays, shapes)


def on_device(
    n_dp,
    inputs,
    segment_ids,
    positions,
    first_gain,
    first_shift,
    second_gain,
    second_shift,
    attend_weight,
    attend_bias,
    project_weight,
    project_bias,
    expand_weight,
    expand_bias,
    shrink_weight,
    shrink_bias,
    output_grad,
):
    count = n_dp // QUAD
    features = inputs.shape[1]
    attend_cols, hidden_cols = attend_weight.shape[1], expand_weight.shape[1]
    project_cols = project_weight.shape[0]
    core = lax.axis_index("tensor").astype(jnp.int32)
    dp_at = lax.axis_index("dp").astype(jnp.int32)
    quarter = dp_at % QUAD
    meta = jnp.stack([core, quarter, dp_at // QUAD])

    def to_quad(value, j):
        return lax.ppermute(value, "dp", xor_pairs(n_dp, j))

    def to_layer(value, bits):
        return lax.ppermute(value, "dp", xor_pairs(n_dp, bits * QUAD))

    def gather_layers(block):
        blocks = {0: block}
        bit = count // 2
        while bit:
            for k in sorted(blocks):
                blocks[k | bit] = to_layer(blocks[k], bit)
            bit //= 2
        return [blocks[k] for k in range(count)]

    def gather_direct(block):
        return [block] + [to_layer(block, k) for k in range(1, count)]

    halfway = ROT // 2
    frequency = 1.0 / 10000.0 ** (jnp.arange(halfway, dtype=F32) * (2.0 / ROT))
    angles = frequency[:, None] * positions.astype(F32)[None, :]
    earlier = segment_ids[None, :] < segment_ids[:, None]
    start = jnp.sum(earlier.astype(jnp.int32), axis=1)
    start = jnp.concatenate([start // 256, start % 256]).astype(BF16)
    turns = jnp.concatenate([jnp.cos(angles), jnp.sin(angles)], axis=1)
    message, cotangent_sum = join_message(
        inputs, output_grad, *low_parts(turns, 3), jnp.broadcast_to(start[None], turns.shape)
    )

    first_pack, second_pack = pack_weights(
        meta, attend_weight, project_weight.T, expand_weight, shrink_weight.T
    )
    second_parts = [second_pack[0]]
    second_parts += [to_quad(second_pack[j], j) for j in range(1, QUAD)]
    second_blocks = gather_direct(jnp.stack(second_parts))
    first_parts = [first_pack[0]] + [to_quad(first_pack[j], j) for j in range(1, QUAD)]
    first_blocks = gather_layers(jnp.stack(first_parts))

    whole = [message] + [to_quad(message, j) for j in range(1, QUAD)]
    messages = [(value, swap_cores(value)) for value in whole]

    one_row = lambda vector: vector[None, :]
    bias_part = lax.dynamic_index_in_dim(
        attend_bias.reshape(QUAD, attend_cols // QUAD), quarter, 0, True
    )
    hidden_part = lax.dynamic_index_in_dim(
        expand_bias.reshape(QUAD, hidden_cols // QUAD), quarter, 0, True
    )

    carried, partials = None, {}
    for group in ATTEND_GROUPS:
        results = branch(
            Attend,
            meta,
            one_row(first_gain),
            one_row(first_shift),
            bias_part,
            [messages[s] for s in group],
            [],
            first_blocks,
            carried,
            group is ATTEND_GROUPS[-1],
        )
        (out_part, grad_part), attend_sums, carried = results
        for place, s in enumerate(group):
            partials[s] = (out_part, grad_part, place)
    attend_grads = carried

    carried, sums_of = None, {}
    for group in MLP_GROUPS:
        results = branch(
            Mlp,
            meta,
            one_row(second_gain),
            one_row(second_shift),
            hidden_part,
            [messages[s] for s in group],
            [partials[s] for s in group],
            second_blocks,
            carried,
            group is MLP_GROUPS[-1],
        )
        outs, mlp_sums, carried = results
        for place, s in enumerate(group):
            mine, other = outs[2 * place], swap_cores(outs[2 * place + 1])
            if s == 0:
                own_halves = mine, other
                continue
            sums_of[s] = add_halves(mine, other)
    mlp_grads = carried

    parts = [to_quad(sums_of[j], j) for j in range(1, QUAD)]
    outputs, grad_inputs = finish(
        inputs, output_grad, own_halves, parts, one_row(project_bias), one_row(shrink_bias)
    )

    def reduce_layers(grads):
        received = [to_layer(grads[k], k) for k in range(1, count)]
        parts = sum_layers(grads[0], received)
        return parts[0], [to_quad(parts[j], j) for j in range(1, QUAD)]

    own, received = reduce_layers(attend_grads)
    grad_attend, grad_project = unpack_attend(meta, own, received, attend_cols, project_cols)
    own, received = reduce_layers(mlp_grads)
    grad_expand, grad_shrink = unpack_mlp(meta, own, received, hidden_cols)

    sizes = [features] * 4 + [features] * 2 + [2 * attend_cols, 2 * hidden_cols]
    vector = join_vector(meta, *attend_sums, *mlp_sums, cotangent_sum, sizes)
    vector = vector + swap_cores(vector)
    near = [to_quad(vector, j) for j in range(1, QUAD)]
    vector = (vector + near[0]) + (near[1] + near[2])
    vectors = [vector] + [to_layer(vector, k) for k in range(1, count)]
    pieces = split_vector(vectors, sizes)
    return (
        outputs,
        grad_inputs,
        *pieces[:4],
        grad_attend,
        pieces[6],
        grad_project.T,
        pieces[4],
        grad_expand,
        pieces[7],
        grad_shrink.T,
        pieces[5],
    )


def solution(mesh):
    n_dp = mesh.shape["dp"]
    assert mesh.shape["tensor"] == 2 and n_dp % QUAD == 0 and n_dp & (n_dp - 1) == 0
    rows = P(("dp", "tensor"), None)
    in_specs = (
        rows,
        P("dp"),
        P("dp"),
        P(),
        P(),
        P(),
        P(),
        P("dp", "tensor"),
        P("tensor"),
        P("tensor", "dp"),
        P(),
        P("dp", "tensor"),
        P("tensor"),
        P("tensor", "dp"),
        P(),
        rows,
    )
    out_specs = (
        rows,
        rows,
        P(),
        P(),
        P(),
        P(),
        P("dp", "tensor"),
        P(),
        P("tensor", "dp"),
        P(),
        P("dp", "tensor"),
        P(),
        P("tensor", "dp"),
        P(),
    )

    def program(*args):
        return on_device(n_dp, *args)

    return jax.shard_map(
        program, mesh=mesh, in_specs=in_specs, out_specs=out_specs, check_vma=False
    )
```

```python
from types import SimpleNamespace

import jax
import jax.numpy as jnp
import numpy as np
from jax import lax
from jax.experimental import pallas as pl
from jax.experimental.pallas import tpu as pltpu
from jax.sharding import PartitionSpec as P


HD = 64
ROT = 16
QUAD = 4
TABLE_ROWS = 32
EPSILON = 1e-05
NEGATIVE = -1e30
QUERY_BLOCK = 256
SMALL_VMEM = 12 << 20
ROW_CHUNK = 32
ATTEND_GROUPS = ((0,), (1, 2), (3,))
MLP_GROUPS = ((3,), (1, 2, 0))
F32 = jnp.float32
BF16 = jnp.bfloat16


HBM = pl.BlockSpec(memory_space=pltpu.HBM)
ANY = pl.BlockSpec(memory_space=pl.ANY)
VMEM = pl.BlockSpec(memory_space=pltpu.VMEM)
SMEM = pl.BlockSpec(memory_space=pltpu.SMEM)


def dot_nn(left, right):
    return lax.dot_general(left, right, (((1,), (0,)), ((), ())), preferred_element_type=F32)


def dot_nt(left, right):
    return lax.dot_general(left, right, (((1,), (1,)), ((), ())), preferred_element_type=F32)


def dot_tn(left, right):
    return lax.dot_general(left, right, (((0,), (0,)), ((), ())), preferred_element_type=F32)


def xor_pairs(n_dp, bits):
    return [(index, index ^ bits) for index in range(n_dp)]


def swap_cores(value):
    return lax.ppermute(value, "tensor", [(0, 1), (1, 0)])


def low_parts(value, number):
    parts = []
    for _ in range(number):
        part = lax.reduce_precision(value, 8, 7)
        parts.append(part.astype(BF16))
        value = value - part
    return parts


def staged_call(body, scalars, arrays, shapes):
    count = len(arrays)

    def whole(*refs):
        at = len(scalars)
        given, sources = refs[:at], refs[at : at + count]
        outs = refs[at + count : at + count + len(shapes)]
        targets, sems = refs[at + count + len(shapes) : -1], refs[-1]
        copies = [
            pltpu.make_async_copy(source, target, sems.at[k])
            for k, (source, target) in enumerate(zip(sources, targets))
        ]
        for copy in copies:
            copy.start()
        for copy in copies:
            copy.wait()
        body(*given, *targets, *outs)

    return pl.pallas_call(
        whole,
        in_specs=[SMEM] * len(scalars) + [ANY] * count,
        out_specs=[VMEM] * len(shapes),
        out_shape=shapes,
        scratch_shapes=[pltpu.VMEM(array.shape, array.dtype) for array in arrays]
        + [pltpu.SemaphoreType.DMA((count,))],
        compiler_params=pltpu.CompilerParams(vmem_limit_bytes=SMALL_VMEM),
    )(*scalars, *arrays)


def pack_body(meta, attend, project, expand, shrink, *outs):
    first, second = outs[:QUAD], outs[QUAD:]
    quarter = meta[1]
    heads = attend.shape[1] // QUAD
    context = project.shape[1] // QUAD
    hidden = expand.shape[1] // QUAD
    for j in range(QUAD):
        at = quarter ^ j
        first[j][:, :heads] = attend[:, pl.ds(pl.multiple_of(at * heads, 128), heads)]
        first[j][:, heads:] = project[:, pl.ds(pl.multiple_of(at * context, 128), context)]
        second[j][0] = expand[:, pl.ds(pl.multiple_of(at * hidden, 128), hidden)]
        second[j][1] = shrink[:, pl.ds(pl.multiple_of(at * hidden, 128), hidden)]


def pack_weights(meta, attend, project, expand, shrink):
    rows = attend.shape[0]
    width = (attend.shape[1] + project.shape[1]) // QUAD
    hidden = expand.shape[1] // QUAD
    parts = pl.pallas_call(
        pack_body,
        in_specs=[SMEM] + [VMEM] * 4,
        out_specs=[VMEM] * (2 * QUAD),
        out_shape=[jax.ShapeDtypeStruct((rows, width), BF16)] * QUAD
        + [jax.ShapeDtypeStruct((2, rows, hidden), BF16)] * QUAD,
    )(meta, attend, project, expand, shrink)
    return parts[:QUAD], parts[QUAD:]


def join_body(*refs):
    cotangents, parts, message, column_sums = refs[0], refs[1:-2], refs[-2], refs[-1]
    total = fold_rows(cotangents[...].astype(F32))
    column_sums[...] = jnp.sum(total, axis=0, keepdims=True)
    at = 0
    for part in parts:
        message[at : at + part.shape[0]] = part[...]
        at += part.shape[0]


def join_message(cotangents, *parts):
    rows = sum(part.shape[0] for part in parts)
    return pl.pallas_call(
        join_body,
        in_specs=[VMEM] * (1 + len(parts)),
        out_specs=[VMEM] * 2,
        out_shape=[
            jax.ShapeDtypeStruct((rows, parts[0].shape[1]), BF16),
            jax.ShapeDtypeStruct((1, parts[0].shape[1]), F32),
        ],
    )(cotangents, *parts)


def sum_layers_body(keep, *refs):
    received, outs = refs[:-QUAD], refs[-QUAD:]
    for j in range(QUAD):
        total = keep[j]
        for part in received:
            total = total + part[j].astype(F32)
        outs[j][...] = total.astype(outs[j].dtype)


def sum_layers(keep, received):
    shape = keep.shape[1:]
    shapes = [jax.ShapeDtypeStruct(shape, BF16 if j else F32) for j in range(QUAD)]
    return staged_call(sum_layers_body, [], [keep, *received], shapes)


def add_body(mine, other, out, mine_s, other_s, out_s, sems):
    def copies(which):
        pairs = ((mine, mine_s), (other, other_s))
        return [
            pltpu.make_async_copy(source.at[which], target.at[which], sems.at[which, n])
            for n, (source, target) in enumerate(pairs)
        ]

    saves = [
        pltpu.make_async_copy(out_s.at[which], out.at[which], sems.at[which, 2]) for which in (0, 1)
    ]
    for which in (0, 1):
        for copy in copies(which):
            copy.start()
    for which in (0, 1):
        for copy in copies(which):
            copy.wait()
        out_s[which] = (mine_s[which].astype(F32) + other_s[which].astype(F32)).astype(BF16)
        saves[which].start()
    for save in saves:
        save.wait()


def add_halves(mine, other):
    shape = mine.shape
    return pl.pallas_call(
        add_body,
        in_specs=[ANY] * 2,
        out_specs=ANY,
        out_shape=jax.ShapeDtypeStruct(shape, BF16),
        scratch_shapes=[pltpu.VMEM(shape, BF16)] * 3 + [pltpu.SemaphoreType.DMA((2, 3))],
        compiler_params=pltpu.CompilerParams(vmem_limit_bytes=SMALL_VMEM),
    )(mine, other)


def join_vector_body(meta, first, first_bias, second, second_bias, cotangent, out):
    out[...] = jnp.zeros_like(out)
    tiles = first.shape[1] // 128

    def put(at, row):
        for k in range(row.shape[1] // 128):
            out[pl.ds(at + k, 1), :] = row[:, k * 128 : (k + 1) * 128]

    at = 0
    for sums in (first, second):
        for part in (sums[:8], sums[8:]):
            put(at, jnp.sum(part, axis=0, keepdims=True))
            at += tiles
    put(at, cotangent[...])
    at += tiles
    place = meta[0] * QUAD + meta[1]
    row = jnp.sum(first_bias[...].T, axis=0, keepdims=True)
    put(at + place * (row.shape[1] // 128), row)
    at += 2 * QUAD * (row.shape[1] // 128)
    row = jnp.sum(second_bias[...], axis=0, keepdims=True)
    put(at + place * (row.shape[1] // 128), row)


def join_vector(meta, first, first_bias, second, second_bias, cotangent, sizes):
    rows = (sum(sizes) - cotangent.shape[1]) // 128
    return pl.pallas_call(
        join_vector_body,
        in_specs=[SMEM] + [VMEM] * 5,
        out_specs=VMEM,
        out_shape=jax.ShapeDtypeStruct((rows, 128), F32),
    )(meta, first, first_bias, second, second_bias, cotangent)


def split_body(*refs):
    count = len(refs) - 8
    totals = [ref[...] for ref in refs[:count]]
    while len(totals) > 1:
        totals = [first + second for first, second in zip(totals[::2], totals[1::2])]
    at = 0
    for number, out in enumerate(refs[count:]):
        at -= out.shape[0] if number == 5 else 0
        out[...] = totals[0][at : at + out.shape[0]]
        at += out.shape[0]


def split_vector(vectors, sizes):
    shapes = [jax.ShapeDtypeStruct((size // 128, 128), F32) for size in sizes]
    pieces = staged_call(split_body, [], vectors, shapes)
    return [piece.reshape(-1) for piece in pieces]


def unpack_attend_body(meta, own, *refs):
    received, (attend, project) = refs[:3], refs[3:]
    quarter = meta[1]
    heads = attend.shape[1] // QUAD
    context = project.shape[1] // QUAD
    for j in range(QUAD):
        piece = own[...] if j == 0 else received[j - 1][...].astype(F32)
        at = quarter ^ j
        attend[:, pl.ds(pl.multiple_of(at * heads, 128), heads)] = piece[:, :heads]
        project[:, pl.ds(pl.multiple_of(at * context, 128), context)] = piece[:, heads:]


def unpack_attend(meta, own, received, attend_cols, project_cols):
    rows = own.shape[0]
    shapes = [jax.ShapeDtypeStruct((rows, cols), F32) for cols in (attend_cols, project_cols)]
    return staged_call(unpack_attend_body, [meta], [own, *received], shapes)


def unpack_mlp_body(meta, own, *refs):
    received, (expand, shrink) = refs[:3], refs[3:]
    quarter = meta[1]
    hidden = expand.shape[1] // QUAD
    for j in range(QUAD):
        piece = own if j == 0 else received[j - 1]
        lanes = pl.ds(pl.multiple_of((quarter ^ j) * hidden, 128), hidden)
        expand[:, lanes] = piece[0].astype(F32)
        shrink[:, lanes] = piece[1].astype(F32)


def unpack_mlp(meta, own, received, hidden_cols):
    rows = own.shape[1]
    shapes = [jax.ShapeDtypeStruct((rows, hidden_cols), F32)] * 2
    return staged_call(unpack_mlp_body, [meta], [own, *received], shapes)


def row_chunks(length):
    return [slice(c * ROW_CHUNK, (c + 1) * ROW_CHUNK) for c in range(length // ROW_CHUNK)]


def column_chunks(features):
    return [slice(c * 256, (c + 1) * 256) for c in range(features // 256)]


def wait_bytes(view, sem):
    pltpu.make_async_copy(view, view, sem).wait()


def widen(tile, features):
    return jnp.concatenate([tile] * (features // 128), axis=1)


def fold_rows(value):
    return jnp.sum(value.reshape(value.shape[0] // 8, 8, value.shape[1]), axis=0)


def fold_lanes(value):
    tiles = [value[:, k * 128 : (k + 1) * 128] for k in range(value.shape[1] // 128)]
    while len(tiles) > 1:
        tiles = [sum(tiles[k : k + 2]) for k in range(0, len(tiles), 2)]
    return tiles[0]


def normalize(x, gain, shift, norm_s, hat_s):
    length, features = x.shape
    share = np.float32(1.0 / features)

    def some_rows(number, carry):
        for part in range(4):
            at = pl.multiple_of((number * 4 + part) * ROW_CHUNK, ROW_CHUNK)
            rows = pl.ds(at, ROW_CHUNK)
            tokens = x[rows, :].astype(F32)
            centred = tokens - jnp.sum(fold_lanes(tokens), axis=-1, keepdims=True) * share
            variance = jnp.sum(fold_lanes(centred * centred), axis=-1, keepdims=True) * share
            scaled = centred * lax.rsqrt(variance + EPSILON)
            hat_s[rows, :] = scaled
            norm_s[rows, :] = (scaled * gain[...] + shift[...]).astype(BF16)
        return carry

    lax.fori_loop(0, length // (4 * ROW_CHUNK), some_rows, 0)


def rotate_rows(part, cosine, sine):
    half = ROT // 2
    lead, trail = part[:half], part[half:ROT]
    return jnp.concatenate(
        [lead * cosine - trail * sine, trail * cosine + lead * sine, part[ROT:]], axis=0
    )


class Attend:
    picks = (None,)
    turns = True

    @staticmethod
    def scratch(length, features, width):
        return dict(
            mask=pltpu.VMEM((length // QUERY_BLOCK, length, QUERY_BLOCK), F32),
            q=pltpu.VMEM((2, 2 * HD, length), BF16),
            d=pltpu.VMEM((2, 2 * HD, length), BF16),
            kv=pltpu.VMEM((2, length, 2 * HD), BF16),
            kvt=pltpu.VMEM((2, 2 * HD, length), BF16),
            score=pltpu.VMEM((2, length, QUERY_BLOCK), F32),
            gprob=pltpu.VMEM((2, length, QUERY_BLOCK), F32),
            weight=pltpu.VMEM((2, length, QUERY_BLOCK), BF16),
            gprod=pltpu.VMEM((2, length, QUERY_BLOCK), BF16),
            dq=pltpu.VMEM((2, HD, length), F32),
            dk=pltpu.VMEM((2, HD, length), F32),
            dv=pltpu.VMEM((2, HD, length), F32),
            ctxt=pltpu.VMEM((2 * HD, length), BF16),
            ctx=pltpu.VMEM((length, 2 * HD), BF16),
            gmt=pltpu.VMEM((6 * HD, length), BF16),
            gm=pltpu.VMEM((length, 6 * HD), BF16),
        )

    @staticmethod
    def bias_shape(width):
        return (6 * HD, 128)

    @staticmethod
    def cost(length, features, width):
        return 6 * length * features * width + 14 * length * length * 2 * HD, 2 * length**2

    @staticmethod
    def compute(m, norm, cot, w, bias, bias_sums, table):
        length = norm.shape[0]
        heads = 6 * HD
        scale = np.float32(HD ** (-0.5))
        values = sum(table[k * 8 : (k + 1) * 8, :].astype(F32) for k in range(3))
        cosine, sine = values[:, :length], values[:, length:]
        start = table[24:25, :length].astype(F32) * 256.0 + table[24:25, length:].astype(F32)
        for block in range(length // QUERY_BLOCK):
            width = (block + 1) * QUERY_BLOCK
            lanes = slice(block * QUERY_BLOCK, width)
            key_at = lax.broadcasted_iota(jnp.int32, (width, QUERY_BLOCK), 0)
            query_at = lax.broadcasted_iota(jnp.int32, (width, QUERY_BLOCK), 1)
            first = start[:, lanes].astype(jnp.int32)
            allowed = (key_at >= first) & (key_at <= query_at + block * QUERY_BLOCK)
            m.mask[block, :width, :] = jnp.where(allowed, 0.0, NEGATIVE)

        column = jnp.broadcast_to(bias[...], (128, heads)).T
        projected = dot_nt(w[:heads, :], norm[...]) + widen(column, length)
        grad_context = dot_nt(w[heads:, :], cot[...]).astype(BF16)
        nothing = jnp.zeros((HD, length), BF16)
        for h in range(2):
            query, key, value = [
                projected[(3 * h + k) * HD : (3 * h + k + 1) * HD] for k in range(3)
            ]
            m.q[h, :HD, :] = (rotate_rows(query, cosine, sine) * scale).astype(BF16)
            m.q[h, HD:, :] = nothing
            m.d[h, :HD, :] = nothing
            m.d[h, HD:, :] = grad_context[h * HD : (h + 1) * HD]
            both = jnp.concatenate([rotate_rows(key, cosine, sine), value], axis=0).astype(BF16)
            m.kvt[h] = both
            m.kv[h] = both.T

        items = [
            (block, h) for block in reversed(range(length // QUERY_BLOCK)) for h in range(2)
        ]

        def place(item):
            block = items[item][0]
            width = (block + 1) * QUERY_BLOCK
            return *items[item], width, slice(block * QUERY_BLOCK, width)

        def products(item):
            _, h, width, lanes = place(item)
            key_value = m.kv[h, :width, :]
            m.score[item % 2, :width, :] = dot_nn(key_value, m.q[h, :, lanes])
            m.gprob[item % 2, :width, :] = dot_nn(key_value, m.d[h, :, lanes])

        def softmax(item):
            block, _, width, _ = place(item)
            scores = m.score[item % 2, :width, :] + m.mask[block, :width, :]
            highest = jnp.max(scores, axis=0, keepdims=True)
            numerators = jnp.exp(scores - highest)
            weights = numerators * (1.0 / jnp.sum(numerators, axis=0, keepdims=True))
            grad_probs = m.gprob[item % 2, :width, :]
            centre = jnp.sum(grad_probs * weights, axis=0, keepdims=True)
            m.weight[item % 2, :width, :] = weights.astype(BF16)
            m.gprod[item % 2, :width, :] = (weights * (grad_probs - centre)).astype(BF16)

        def results(item):
            _, h, width, lanes = place(item)
            weights_low = m.weight[item % 2, :width, :]
            grad_products = m.gprod[item % 2, :width, :]
            context = dot_nn(m.kvt[h, HD:, :width], weights_low)
            m.ctxt[h * HD : (h + 1) * HD, lanes] = context.astype(BF16)
            grad_query = dot_nn(m.kvt[h, :HD, :width], grad_products)
            m.dq[h, :, lanes] = grad_query * scale
            grad_key = dot_nt(m.q[h, :HD, lanes], grad_products)
            grad_value = dot_nt(m.d[h, HD:, lanes], weights_low)
            if width == length:
                m.dk[h] = grad_key
                m.dv[h] = grad_value
            else:
                m.dk[h, :, :width] += grad_key
                m.dv[h, :, :width] += grad_value

        products(0)
        for item in range(len(items)):
            if item + 1 < len(items):
                products(item + 1)
            if item:
                results(item - 1)
            softmax(item)
        results(len(items) - 1)

        for h in range(2):
            parts = [
                rotate_rows(m.dq[h], cosine, -sine),
                rotate_rows(m.dk[h], cosine, -sine),
                m.dv[h],
            ]
            for k, part in enumerate(parts):
                rows = slice((3 * h + k) * HD, (3 * h + k + 1) * HD)
                low = part.astype(BF16)
                m.gmt[rows, :] = low
                bias_sums[rows, :] += fold_lanes(low.astype(F32))
        m.gm[...] = m.gmt[...].T
        m.ctx[...] = m.ctxt[...].T

    @staticmethod
    def accumulate(m, norm, cot, total):
        heads = 6 * HD
        total[0, :heads, :] += dot_nn(m.gmt[...], norm[...])
        total[0, heads:, :] += dot_nn(m.ctxt[...], cot[...])

    @staticmethod
    def forward_out(m, w, cols):
        return dot_nn(m.ctx[...], w[6 * HD :, cols])

    @staticmethod
    def backward_out(m, w, cols):
        return dot_nn(m.gm[...], w[: 6 * HD, cols])


class Mlp:
    picks = (0, 1)
    turns = False

    @staticmethod
    def scratch(length, features, width):
        return dict(
            hid=pltpu.VMEM((2, length, width), F32),
            act=pltpu.VMEM((length, width), BF16),
            dh=pltpu.VMEM((length, width), BF16),
        )

    @staticmethod
    def bias_shape(width):
        return (8, width)

    @staticmethod
    def cost(length, features, width):
        return 12 * length * features * width, 2 * length * width

    @staticmethod
    def compute(m, norm, cot, w, bias, bias_sums, table):
        m.hid[0] = dot_nn(norm[...], w[0]) + bias[...]
        m.hid[1] = dot_nn(cot[...], w[1])
        for rows in row_chunks(norm.shape[0]):
            hid = m.hid[0, rows, :]
            below = 0.5 + 0.5 * lax.erf(hid * np.float32(0.5**0.5))
            slope = below + hid * jnp.exp(-0.5 * (hid * hid)) * np.float32((2 * np.pi) ** -0.5)
            m.act[rows, :] = (hid * below).astype(BF16)
            grad_hid = (slope * m.hid[1, rows, :]).astype(BF16)
            m.dh[rows, :] = grad_hid
            bias_sums[...] += fold_rows(grad_hid.astype(F32))

    @staticmethod
    def accumulate(m, norm, cot, total):
        total[0] += dot_tn(m.dh[...], norm[...])
        total[1] += dot_tn(m.act[...], cot[...])

    @staticmethod
    def forward_out(m, w, cols):
        return dot_nt(m.act[...], w[1, cols, :])

    @staticmethod
    def backward_out(m, w, cols):
        return dot_nt(m.dh[...], w[0, cols, :])


def branch_body(kind, names, n_seq, count, is_first, is_last, places, *refs):
    refs = list(refs)
    take = lambda number: [refs.pop(0) for _ in range(number)]
    (meta, gain, shift, bias) = take(4)
    messages = [take(4) for _ in range(n_seq)]
    partials = [take(2) for _ in places or ()]
    reads_turned = kind.turns and not is_first
    blocks = take(1 if reads_turned else count)
    carried = [] if is_first else take(3)
    outs = take(2 * n_seq if places else 2)
    sums, bias_sums = take(2)
    if is_last:
        grads = take(count)
    else:
        (total_hbm,) = take(1)
        if kind.turns:
            (turned_hbm,) = take(1) if is_first else (None,)
    x_s, d_s, tab_s, w_s, total, norm_s, hat_s, out_st, grad_st = take(9)
    wt_s = take(1)[0] if kind.turns else None
    turned = take(1)[0] if is_last else None
    m = SimpleNamespace(**dict(zip(names, take(len(names)))))
    token_sem, table_sem, weight_sem, part_sem, out_sem, total_sem = take(6)

    length, features = x_s.shape[1:]
    half = length // 2
    mine = pl.multiple_of(meta[0] * half, half)
    other = pl.multiple_of((1 - meta[0]) * half, half)
    rows = features // (QUAD * count)

    weight_copies = []
    if reads_turned:
        weight_copies.append(pltpu.make_async_copy(blocks[0], wt_s, weight_sem.at[0, 0, 0]))
    else:
        for k in range(count):
            for j in range(QUAD):
                place = (meta[2] ^ k) * (QUAD * rows) + (meta[1] ^ j) * rows
                for number, pick in enumerate(kind.picks):
                    source = blocks[k].at[j] if pick is None else blocks[k].at[j, pick]
                    target = w_s.at[number, pl.ds(pl.multiple_of(place, rows), rows)]
                    weight_copies.append(
                        pltpu.make_async_copy(source, target, weight_sem.at[number, k, j])
                    )

    def start_message(i, target, first, which):
        for number, place in enumerate((mine, other)):
            pltpu.make_async_copy(
                messages[i][first + number].at[pl.ds(0, half)],
                target.at[i, pl.ds(place, half)],
                token_sem.at[i, which, number],
            ).start()

    def start_rest(i):
        start_message(i, d_s, 2, 1)
        if kind.turns:
            pltpu.make_async_copy(
                messages[i][0].at[pl.ds(half, TABLE_ROWS)], tab_s.at[i], table_sem.at[i]
            ).start()
        if i == 0:
            for copy in weight_copies:
                copy.start()

    def start_partials(i):
        if places:
            for number, stage in enumerate((out_st, grad_st)):
                pltpu.make_async_copy(
                    partials[i][number].at[places[i]], stage.at[i], part_sem.at[i, number]
                ).start()

    start_message(0, x_s, 0, 0)
    if is_first:
        total[...] = jnp.zeros_like(total)
        sums[...] = jnp.zeros_like(sums)
        bias_sums[...] = jnp.zeros_like(bias_sums)
    else:
        load = pltpu.make_async_copy(carried[0], total, total_sem.at[0])
        sums[...] = carried[1][...]
        bias_sums[...] = carried[2][...]
    saves = []
    if not is_last:
        saves.append(pltpu.make_async_copy(total, total_hbm, total_sem.at[1]))
        if kind.turns and is_first:
            keep = pltpu.make_async_copy(wt_s, turned_hbm, total_sem.at[2])

    def stores(stage, i, which):
        if not places:
            return [pltpu.make_async_copy(stage.at[i], outs[which].at[i], out_sem.at[i, which, 0])]
        return [
            pltpu.make_async_copy(
                stage.at[i, pl.ds(place, half)],
                outs[2 * i + number].at[which],
                out_sem.at[i, which, number],
            )
            for number, place in enumerate((mine, other))
        ]

    def start_stores(stage, i, which):
        if not places or n_seq == 1:
            for copy in stores(stage, i, which):
                copy.start()
            return
        for k in range(n_seq):

            @pl.when(i == k)
            def _(k=k):
                for copy in stores(stage, k, which):
                    copy.start()

    def one_sequence(i, carry):
        for number in range(2):
            wait_bytes(x_s.at[i, pl.ds(0, half)], token_sem.at[i, 0, number])

        @pl.when(i == 0)
        def _():
            start_rest(0)

        normalize(x_s.at[i], gain, shift, norm_s, hat_s)
        if kind.turns:
            wait_bytes(tab_s.at[i], table_sem.at[i])
        for number in range(2):
            wait_bytes(d_s.at[i, pl.ds(0, half)], token_sem.at[i, 1, number])

        @pl.when(i == 0)
        def _():
            for copy in weight_copies:
                copy.wait()
            if not is_first:
                load.start()
            for later in range(1, n_seq):
                start_message(later, x_s, 0, 0)
                start_rest(later)
            for later in range(n_seq):
                start_partials(later)
            if kind.turns and is_first:
                for cols in column_chunks(features):
                    wt_s[:, cols] = w_s[0, cols, :].T
                if not is_last:
                    keep.start()

        cot = d_s.at[i]
        w = wt_s if kind.turns else w_s
        kind.compute(m, norm_s, cot, w, bias, bias_sums, tab_s.at[i])
        if not is_first:

            @pl.when(i == 0)
            def _():
                load.wait()

        kind.accumulate(m, norm_s, cot, total)
        if not is_last:

            @pl.when(i == n_seq - 1)
            def _():
                for copy in saves:
                    copy.start()

        if places:
            wait_bytes(out_st.at[i], part_sem.at[i, 0])
            wait_bytes(grad_st.at[i], part_sem.at[i, 1])
        for cols in column_chunks(features):
            out = kind.forward_out(m, w, cols)
            if places:
                out = out + out_st[i, :, cols].astype(F32)
            out_st[i, :, cols] = out.astype(BF16)
        start_stores(out_st, i, 0)
        for cols in column_chunks(features):
            grad = kind.backward_out(m, w, cols)
            sums[0:8, cols] += fold_rows(grad * hat_s[:, cols])
            sums[8:16, cols] += fold_rows(grad)
            whole = grad * gain[:, cols]
            if places:
                whole = whole + grad_st[i, :, cols].astype(F32)
            grad_st[i, :, cols] = whole.astype(BF16)
        start_stores(grad_st, i, 1)
        return carry

    if n_seq == 1:
        one_sequence(0, 0)
    else:
        lax.fori_loop(0, n_seq, one_sequence, 0)
    if is_last:
        for number, pick in enumerate(kind.picks):
            for cols in column_chunks(features):
                turned[cols, :] = total[number, :, cols].T
            for k in range(count):
                for j in range(QUAD):
                    place = (meta[2] ^ k) * (QUAD * rows) + (meta[1] ^ j) * rows
                    piece = turned[pl.ds(pl.multiple_of(place, rows), rows), :]
                    at = (j,) if pick is None else (j, pick)
                    grads[k][at] = piece.astype(grads[k].dtype)
    for copy in saves:
        copy.wait()
    if kind.turns and is_first and not is_last:
        keep.wait()
    for i in range(n_seq):
        for copy in stores(out_st, i, 0) + stores(grad_st, i, 1):
            copy.wait()


def branch(kind, meta, gain, shift, bias, messages, partials, blocks, carried, is_last):
    n_seq, count, is_first = len(messages), len(blocks), carried is None
    half = messages[0][2].shape[0]
    features = messages[0][0].shape[1]
    length = 2 * half
    width = blocks[0].shape[-1]
    n_pick = len(kind.picks)
    operands = [meta, gain, shift, bias]
    specs = [SMEM] + [VMEM] * 3
    for pair in messages:
        operands += list(pair)
        specs += [ANY] * 4
    for part in partials:
        operands += list(part[:2])
        specs += [HBM] * 2
    places = [part[2] for part in partials]
    if kind.turns and not is_first:
        operands += [carried[3]]
        specs += [HBM]
    else:
        operands += list(blocks)
        specs += [HBM] * count
    if not is_first:
        operands += list(carried[:3])
        specs += [HBM, VMEM, VMEM]
    if places:
        shapes = [jax.ShapeDtypeStruct((2, half, features), BF16)] * (2 * n_seq)
    else:
        shapes = [jax.ShapeDtypeStruct((n_seq, length, features), BF16)] * 2
    n_out = len(shapes)
    shapes += [
        jax.ShapeDtypeStruct((16, features), F32),
        jax.ShapeDtypeStruct(kind.bias_shape(width), F32),
    ]
    out_specs = [HBM] * n_out + [VMEM, VMEM]
    if is_last:
        shape = blocks[0].shape
        shapes += [jax.ShapeDtypeStruct(shape, BF16 if k else F32) for k in range(count)]
        out_specs += [VMEM] * count
    else:
        shapes += [jax.ShapeDtypeStruct((n_pick, width, features), F32)]
        out_specs += [HBM]
        if kind.turns and is_first:
            shapes += [jax.ShapeDtypeStruct((width, features), BF16)]
            out_specs += [HBM]
    scratch = [
        pltpu.VMEM((n_seq, length, features), BF16),
        pltpu.VMEM((n_seq, length, features), BF16),
        pltpu.VMEM((n_seq, TABLE_ROWS, features), BF16),
        pltpu.VMEM((n_pick, features, width), BF16),
        pltpu.VMEM((n_pick, width, features), F32),
        pltpu.VMEM((length, features), BF16),
        pltpu.VMEM((length, features), F32),
        pltpu.VMEM((n_seq, length, features), BF16),
        pltpu.VMEM((n_seq, length, features), BF16),
    ]
    if kind.turns:
        scratch += [pltpu.VMEM((width, features), BF16)]
    if is_last:
        scratch += [pltpu.VMEM((features, width), F32)]
    named = kind.scratch(length, features, width)
    scratch += list(named.values())
    scratch += [
        pltpu.SemaphoreType.DMA((n_seq, 2, 2)),
        pltpu.SemaphoreType.DMA((n_seq,)),
        pltpu.SemaphoreType.DMA((n_pick, count, QUAD)),
        pltpu.SemaphoreType.DMA((n_seq, 2)),
        pltpu.SemaphoreType.DMA((n_seq, 2, 2)),
        pltpu.SemaphoreType.DMA((3,)),
    ]
    flops, transcendentals = kind.cost(length, features, width)
    names = tuple(named)

    def body(*refs):
        branch_body(kind, names, n_seq, count, is_first, is_last, places, *refs)

    call = pl.pallas_call(
        body,
        in_specs=specs,
        out_specs=out_specs,
        out_shape=shapes,
        scratch_shapes=scratch,
        cost_estimate=pl.CostEstimate(
            flops=n_seq * flops,
            bytes_accessed=n_seq * 8 * length * features + 10 * n_pick * width * features,
            transcendentals=n_seq * transcendentals,
        ),
    )
    results = call(*operands)
    outs, sums, rest = results[:n_out], results[n_out : n_out + 2], results[n_out + 2 :]
    if is_last:
        return outs, sums, rest
    turned = () if not kind.turns else (rest[1] if is_first else carried[3],)
    return outs, sums, (rest[0], *sums, *turned)


def finish_body(first_bias, second_bias, x, d, mine, other, p1, p2, p3, out, grad):
    bias = first_bias[...] + second_bias[...]

    def some_rows(number, carry):
        rows = pl.ds(pl.multiple_of(number * ROW_CHUNK, ROW_CHUNK), ROW_CHUNK)

        def total(which):
            own = mine[which, rows, :].astype(F32) + other[which, rows, :].astype(F32)
            pair = p2[which, rows, :].astype(F32) + p3[which, rows, :].astype(F32)
            return own + p1[which, rows, :].astype(F32) + pair

        tokens = x[rows, :].astype(F32)
        out[rows, :] = (tokens + total(0) + bias).astype(BF16)
        back = total(1)
        share = np.float32(1.0 / tokens.shape[1])
        mean = lambda value: jnp.sum(fold_lanes(value), axis=-1, keepdims=True) * share
        centred = tokens - mean(tokens)
        inverse = lax.rsqrt(mean(centred * centred) + EPSILON)
        scaled = centred * inverse
        change = (back - mean(back) - scaled * mean(back * scaled)) * inverse
        grad[rows, :] = (d[rows, :].astype(F32) + change).astype(BF16)
        return carry

    lax.fori_loop(0, x.shape[0] // ROW_CHUNK, some_rows, 0, unroll=2)


def finish(x, d, own, parts, first_bias, second_bias):
    shapes = [jax.ShapeDtypeStruct(x.shape, BF16)] * 2
    arrays = [first_bias, second_bias, x, d, *own, *parts]
    return staged_call(finish_body, [], arrays, shapes)


def on_device(
    n_dp,
    inputs,
    segment_ids,
    positions,
    first_gain,
    first_shift,
    second_gain,
    second_shift,
    attend_weight,
    attend_bias,
    project_weight,
    project_bias,
    expand_weight,
    expand_bias,
    shrink_weight,
    shrink_bias,
    output_grad,
):
    count = n_dp // QUAD
    features = inputs.shape[1]
    attend_cols, hidden_cols = attend_weight.shape[1], expand_weight.shape[1]
    project_cols = project_weight.shape[0]
    core = lax.axis_index("tensor").astype(jnp.int32)
    dp_at = lax.axis_index("dp").astype(jnp.int32)
    quarter = dp_at % QUAD
    meta = jnp.stack([core, quarter, dp_at // QUAD])

    def to_quad(value, j):
        return lax.ppermute(value, "dp", xor_pairs(n_dp, j))

    def to_layer(value, bits):
        return lax.ppermute(value, "dp", xor_pairs(n_dp, bits * QUAD))

    def gather_layers(block):
        blocks = {0: block}
        bit = count // 2
        while bit:
            for k in sorted(blocks):
                blocks[k | bit] = to_layer(blocks[k], bit)
            bit //= 2
        return [blocks[k] for k in range(count)]

    def gather_direct(block):
        return [block] + [to_layer(block, k) for k in range(1, count)]

    halfway = ROT // 2
    frequency = 1.0 / 10000.0 ** (jnp.arange(halfway, dtype=F32) * (2.0 / ROT))
    angles = frequency[:, None] * positions.astype(F32)[None, :]
    earlier = segment_ids[None, :] < segment_ids[:, None]
    start = jnp.sum(earlier.astype(jnp.int32), axis=1)
    start = jnp.concatenate([start // 256, start % 256]).astype(BF16)
    turns = jnp.concatenate([jnp.cos(angles), jnp.sin(angles)], axis=1)
    message, cotangent_sum = join_message(
        output_grad, inputs, *low_parts(turns, 3), jnp.broadcast_to(start[None], turns.shape)
    )

    first_pack, second_pack = pack_weights(
        meta, attend_weight, project_weight.T, expand_weight, shrink_weight.T
    )
    second_parts = [second_pack[0]]
    second_parts += [to_quad(second_pack[j], j) for j in range(1, QUAD)]
    second_blocks = gather_direct(jnp.stack(second_parts))
    first_parts = [first_pack[0]] + [to_quad(first_pack[j], j) for j in range(1, QUAD)]
    first_blocks = gather_layers(jnp.stack(first_parts))

    rows_a = [message] + [to_quad(message, j) for j in (1, 2)]
    rows_b = [output_grad] + [to_quad(output_grad, j) for j in (1, 2)]
    rows_a.append(to_quad(rows_a[2], 1))
    rows_b.append(to_quad(rows_b[1], 2))
    messages = [(a, swap_cores(a), b, swap_cores(b)) for a, b in zip(rows_a, rows_b)]

    one_row = lambda vector: vector[None, :]
    bias_part = lax.dynamic_index_in_dim(
        attend_bias.reshape(QUAD, attend_cols // QUAD), quarter, 0, True
    )
    hidden_part = lax.dynamic_index_in_dim(
        expand_bias.reshape(QUAD, hidden_cols // QUAD), quarter, 0, True
    )

    carried, partials = None, {}
    for group in ATTEND_GROUPS:
        results = branch(
            Attend,
            meta,
            one_row(first_gain),
            one_row(first_shift),
            bias_part,
            [messages[s] for s in group],
            [],
            first_blocks,
            carried,
            group is ATTEND_GROUPS[-1],
        )
        (out_part, grad_part), attend_sums, carried = results
        for place, s in enumerate(group):
            partials[s] = (out_part, grad_part, place)
    attend_grads = carried

    carried, sums_of = None, {}
    for group in MLP_GROUPS:
        results = branch(
            Mlp,
            meta,
            one_row(second_gain),
            one_row(second_shift),
            hidden_part,
            [messages[s] for s in group],
            [partials[s] for s in group],
            second_blocks,
            carried,
            group is MLP_GROUPS[-1],
        )
        outs, mlp_sums, carried = results
        for place, s in enumerate(group):
            mine, other = outs[2 * place], swap_cores(outs[2 * place + 1])
            if s == 0:
                own_halves = mine, other
                continue
            sums_of[s] = add_halves(mine, other)
    mlp_grads = carried

    parts = [to_quad(sums_of[j], j) for j in range(1, QUAD)]
    outputs, grad_inputs = finish(
        inputs, output_grad, own_halves, parts, one_row(project_bias), one_row(shrink_bias)
    )

    def reduce_layers(grads):
        received = [to_layer(grads[k], k) for k in range(1, count)]
        parts = sum_layers(grads[0], received)
        return parts[0], [to_quad(parts[j], j) for j in range(1, QUAD)]

    own, received = reduce_layers(attend_grads)
    grad_attend, grad_project = unpack_attend(meta, own, received, attend_cols, project_cols)
    own, received = reduce_layers(mlp_grads)
    grad_expand, grad_shrink = unpack_mlp(meta, own, received, hidden_cols)

    sizes = [features] * 4 + [features] * 2 + [2 * attend_cols, 2 * hidden_cols]
    vector = join_vector(meta, *attend_sums, *mlp_sums, cotangent_sum, sizes)
    vector = vector + swap_cores(vector)
    near = [to_quad(vector, j) for j in range(1, QUAD)]
    vector = (vector + near[0]) + (near[1] + near[2])
    vectors = [vector] + [to_layer(vector, k) for k in range(1, count)]
    pieces = split_vector(vectors, sizes)
    return (
        outputs,
        grad_inputs,
        *pieces[:4],
        grad_attend,
        pieces[6],
        grad_project.T,
        pieces[4],
        grad_expand,
        pieces[7],
        grad_shrink.T,
        pieces[5],
    )


def solution(mesh):
    n_dp = mesh.shape["dp"]
    assert mesh.shape["tensor"] == 2 and n_dp % QUAD == 0 and n_dp & (n_dp - 1) == 0
    rows = P(("dp", "tensor"), None)
    in_specs = (
        rows,
        P("dp"),
        P("dp"),
        P(),
        P(),
        P(),
        P(),
        P("dp", "tensor"),
        P("tensor"),
        P("tensor", "dp"),
        P(),
        P("dp", "tensor"),
        P("tensor"),
        P("tensor", "dp"),
        P(),
        rows,
    )
    out_specs = (
        rows,
        rows,
        P(),
        P(),
        P(),
        P(),
        P("dp", "tensor"),
        P(),
        P("tensor", "dp"),
        P(),
        P("dp", "tensor"),
        P(),
        P("tensor", "dp"),
        P(),
    )

    def program(*args):
        return on_device(n_dp, *args)

    return jax.shard_map(
        program, mesh=mesh, in_specs=in_specs, out_specs=out_specs, check_vma=False
    )
```

```python
from types import SimpleNamespace

import jax
import jax.numpy as jnp
import numpy as np
from jax import lax
from jax.experimental import pallas as pl
from jax.experimental.pallas import tpu as pltpu
from jax.sharding import PartitionSpec as P


HD = 64
ROT = 16
QUAD = 4
TABLE_ROWS = 32
EPSILON = 1e-05
NEGATIVE = -1e30
QUERY_BLOCK = 256
SMALL_VMEM = 12 << 20
ROW_CHUNK = 32
ATTEND_GROUPS = ((0,), (1, 2), (3,))
MLP_GROUPS = ((3,), (1, 2, 0))
F32 = jnp.float32
BF16 = jnp.bfloat16


HBM = pl.BlockSpec(memory_space=pltpu.HBM)
ANY = pl.BlockSpec(memory_space=pl.ANY)
VMEM = pl.BlockSpec(memory_space=pltpu.VMEM)
SMEM = pl.BlockSpec(memory_space=pltpu.SMEM)


def dot_nn(left, right):
    return lax.dot_general(left, right, (((1,), (0,)), ((), ())), preferred_element_type=F32)


def dot_nt(left, right):
    return lax.dot_general(left, right, (((1,), (1,)), ((), ())), preferred_element_type=F32)


def dot_tn(left, right):
    return lax.dot_general(left, right, (((0,), (0,)), ((), ())), preferred_element_type=F32)


def xor_pairs(n_dp, bits):
    return [(index, index ^ bits) for index in range(n_dp)]


def swap_cores(value):
    return lax.ppermute(value, "tensor", [(0, 1), (1, 0)])


def low_parts(value, number):
    parts = []
    for _ in range(number):
        part = lax.reduce_precision(value, 8, 7)
        parts.append(part.astype(BF16))
        value = value - part
    return parts


def staged_call(body, scalars, arrays, shapes):
    count = len(arrays)

    def whole(*refs):
        at = len(scalars)
        given, sources = refs[:at], refs[at : at + count]
        outs = refs[at + count : at + count + len(shapes)]
        targets, sems = refs[at + count + len(shapes) : -1], refs[-1]
        copies = [
            pltpu.make_async_copy(source, target, sems.at[k])
            for k, (source, target) in enumerate(zip(sources, targets))
        ]
        for copy in copies:
            copy.start()
        for copy in copies:
            copy.wait()
        body(*given, *targets, *outs)

    return pl.pallas_call(
        whole,
        in_specs=[SMEM] * len(scalars) + [ANY] * count,
        out_specs=[VMEM] * len(shapes),
        out_shape=shapes,
        scratch_shapes=[pltpu.VMEM(array.shape, array.dtype) for array in arrays]
        + [pltpu.SemaphoreType.DMA((count,))],
        compiler_params=pltpu.CompilerParams(vmem_limit_bytes=SMALL_VMEM),
    )(*scalars, *arrays)


def pack_body(meta, attend, project, expand, shrink, *outs):
    first, second = outs[:QUAD], outs[QUAD:]
    quarter = meta[1]
    heads = attend.shape[1] // QUAD
    context = project.shape[1] // QUAD
    hidden = expand.shape[1] // QUAD
    for j in range(QUAD):
        at = quarter ^ j
        first[j][:, :heads] = attend[:, pl.ds(pl.multiple_of(at * heads, 128), heads)]
        first[j][:, heads:] = project[:, pl.ds(pl.multiple_of(at * context, 128), context)]
        second[j][0] = expand[:, pl.ds(pl.multiple_of(at * hidden, 128), hidden)]
        second[j][1] = shrink[:, pl.ds(pl.multiple_of(at * hidden, 128), hidden)]


def pack_weights(meta, attend, project, expand, shrink):
    rows = attend.shape[0]
    width = (attend.shape[1] + project.shape[1]) // QUAD
    hidden = expand.shape[1] // QUAD
    parts = pl.pallas_call(
        pack_body,
        in_specs=[SMEM] + [VMEM] * 4,
        out_specs=[VMEM] * (2 * QUAD),
        out_shape=[jax.ShapeDtypeStruct((rows, width), BF16)] * QUAD
        + [jax.ShapeDtypeStruct((2, rows, hidden), BF16)] * QUAD,
    )(meta, attend, project, expand, shrink)
    return parts[:QUAD], parts[QUAD:]


def join_body(*refs):
    cotangents, parts, message, column_sums = refs[0], refs[1:-2], refs[-2], refs[-1]
    total = fold_rows(cotangents[...].astype(F32))
    column_sums[...] = jnp.sum(total, axis=0, keepdims=True)
    at = 0
    for part in parts:
        message[at : at + part.shape[0]] = part[...]
        at += part.shape[0]


def join_message(cotangents, *parts):
    rows = sum(part.shape[0] for part in parts)
    return pl.pallas_call(
        join_body,
        in_specs=[VMEM] * (1 + len(parts)),
        out_specs=[VMEM] * 2,
        out_shape=[
            jax.ShapeDtypeStruct((rows, parts[0].shape[1]), BF16),
            jax.ShapeDtypeStruct((1, parts[0].shape[1]), F32),
        ],
    )(cotangents, *parts)


def sum_layers_body(keep, *refs):
    received, outs = refs[:-QUAD], refs[-QUAD:]
    for j in range(QUAD):
        total = keep[j]
        for part in received:
            total = total + part[j].astype(F32)
        outs[j][...] = total.astype(outs[j].dtype)


def sum_layers(keep, received):
    shape = keep.shape[1:]
    shapes = [jax.ShapeDtypeStruct(shape, BF16 if j else F32) for j in range(QUAD)]
    return staged_call(sum_layers_body, [], [keep, *received], shapes)


def add_body(mine, other, out, mine_s, other_s, out_s, sems):
    def copies(which):
        pairs = ((mine, mine_s), (other, other_s))
        return [
            pltpu.make_async_copy(source.at[which], target.at[which], sems.at[which, n])
            for n, (source, target) in enumerate(pairs)
        ]

    saves = [
        pltpu.make_async_copy(out_s.at[which], out.at[which], sems.at[which, 2]) for which in (0, 1)
    ]
    for which in (0, 1):
        for copy in copies(which):
            copy.start()
    for which in (0, 1):
        for copy in copies(which):
            copy.wait()
        out_s[which] = (mine_s[which].astype(F32) + other_s[which].astype(F32)).astype(BF16)
        saves[which].start()
    for save in saves:
        save.wait()


def add_halves(mine, other):
    shape = mine.shape
    return pl.pallas_call(
        add_body,
        in_specs=[ANY] * 2,
        out_specs=ANY,
        out_shape=jax.ShapeDtypeStruct(shape, BF16),
        scratch_shapes=[pltpu.VMEM(shape, BF16)] * 3 + [pltpu.SemaphoreType.DMA((2, 3))],
        compiler_params=pltpu.CompilerParams(vmem_limit_bytes=SMALL_VMEM),
    )(mine, other)


def join_vector_body(meta, first, first_bias, second, second_bias, cotangent, out):
    out[...] = jnp.zeros_like(out)
    tiles = first.shape[1] // 128

    def put(at, row):
        for k in range(row.shape[1] // 128):
            out[pl.ds(at + k, 1), :] = row[:, k * 128 : (k + 1) * 128]

    at = 0
    for sums in (first, second):
        for part in (sums[:8], sums[8:]):
            put(at, jnp.sum(part, axis=0, keepdims=True))
            at += tiles
    put(at, cotangent[...])
    at += tiles
    place = meta[0] * QUAD + meta[1]
    row = jnp.sum(first_bias[...].T, axis=0, keepdims=True)
    put(at + place * (row.shape[1] // 128), row)
    at += 2 * QUAD * (row.shape[1] // 128)
    row = jnp.sum(second_bias[...], axis=0, keepdims=True)
    put(at + place * (row.shape[1] // 128), row)


def join_vector(meta, first, first_bias, second, second_bias, cotangent, sizes):
    rows = (sum(sizes) - cotangent.shape[1]) // 128
    return pl.pallas_call(
        join_vector_body,
        in_specs=[SMEM] + [VMEM] * 5,
        out_specs=VMEM,
        out_shape=jax.ShapeDtypeStruct((rows, 128), F32),
    )(meta, first, first_bias, second, second_bias, cotangent)


def split_body(*refs):
    count = len(refs) - 8
    totals = [ref[...] for ref in refs[:count]]
    while len(totals) > 1:
        totals = [first + second for first, second in zip(totals[::2], totals[1::2])]
    at = 0
    for number, out in enumerate(refs[count:]):
        at -= out.shape[0] if number == 5 else 0
        out[...] = totals[0][at : at + out.shape[0]]
        at += out.shape[0]


def split_vector(vectors, sizes):
    shapes = [jax.ShapeDtypeStruct((size // 128, 128), F32) for size in sizes]
    pieces = staged_call(split_body, [], vectors, shapes)
    return [piece.reshape(-1) for piece in pieces]


def unpack_attend_body(meta, own, *refs):
    received, (attend, project) = refs[:3], refs[3:]
    quarter = meta[1]
    heads = attend.shape[1] // QUAD
    context = project.shape[1] // QUAD
    for j in range(QUAD):
        piece = own[...] if j == 0 else received[j - 1][...].astype(F32)
        at = quarter ^ j
        attend[:, pl.ds(pl.multiple_of(at * heads, 128), heads)] = piece[:, :heads]
        project[:, pl.ds(pl.multiple_of(at * context, 128), context)] = piece[:, heads:]


def unpack_attend(meta, own, received, attend_cols, project_cols):
    rows = own.shape[0]
    shapes = [jax.ShapeDtypeStruct((rows, cols), F32) for cols in (attend_cols, project_cols)]
    return staged_call(unpack_attend_body, [meta], [own, *received], shapes)


def unpack_mlp_body(meta, own, *refs):
    received, (expand, shrink) = refs[:3], refs[3:]
    quarter = meta[1]
    hidden = expand.shape[1] // QUAD
    for j in range(QUAD):
        piece = own if j == 0 else received[j - 1]
        lanes = pl.ds(pl.multiple_of((quarter ^ j) * hidden, 128), hidden)
        expand[:, lanes] = piece[0].astype(F32)
        shrink[:, lanes] = piece[1].astype(F32)


def unpack_mlp(meta, own, received, hidden_cols):
    rows = own.shape[1]
    shapes = [jax.ShapeDtypeStruct((rows, hidden_cols), F32)] * 2
    return staged_call(unpack_mlp_body, [meta], [own, *received], shapes)


def row_chunks(length):
    return [slice(c * ROW_CHUNK, (c + 1) * ROW_CHUNK) for c in range(length // ROW_CHUNK)]


def column_chunks(features):
    return [slice(c * 256, (c + 1) * 256) for c in range(features // 256)]


def wait_bytes(view, sem):
    pltpu.make_async_copy(view, view, sem).wait()


def widen(tile, features):
    return jnp.concatenate([tile] * (features // 128), axis=1)


def fold_rows(value):
    return jnp.sum(value.reshape(value.shape[0] // 8, 8, value.shape[1]), axis=0)


def fold_lanes(value):
    tiles = [value[:, k * 128 : (k + 1) * 128] for k in range(value.shape[1] // 128)]
    while len(tiles) > 1:
        tiles = [sum(tiles[k : k + 2]) for k in range(0, len(tiles), 2)]
    return tiles[0]


def normalize(x, gain, shift, norm_s, hat_s):
    length, features = x.shape
    share = np.float32(1.0 / features)

    def some_rows(number, carry):
        for part in range(4):
            at = pl.multiple_of((number * 4 + part) * ROW_CHUNK, ROW_CHUNK)
            rows = pl.ds(at, ROW_CHUNK)
            tokens = x[rows, :].astype(F32)
            centred = tokens - jnp.sum(fold_lanes(tokens), axis=-1, keepdims=True) * share
            variance = jnp.sum(fold_lanes(centred * centred), axis=-1, keepdims=True) * share
            scaled = centred * lax.rsqrt(variance + EPSILON)
            hat_s[rows, :] = scaled
            norm_s[rows, :] = (scaled * gain[...] + shift[...]).astype(BF16)
        return carry

    lax.fori_loop(0, length // (4 * ROW_CHUNK), some_rows, 0)


def rotate_rows(part, cosine, sine):
    half = ROT // 2
    lead, trail = part[:half], part[half:ROT]
    return jnp.concatenate(
        [lead * cosine - trail * sine, trail * cosine + lead * sine, part[ROT:]], axis=0
    )


class Attend:
    picks = (None,)
    turns = True

    @staticmethod
    def scratch(length, features, width):
        return dict(
            mask=pltpu.VMEM((length // QUERY_BLOCK, length, QUERY_BLOCK), F32),
            q=pltpu.VMEM((2, 2 * HD, length), BF16),
            d=pltpu.VMEM((2, 2 * HD, length), BF16),
            kv=pltpu.VMEM((2, length, 2 * HD), BF16),
            kvt=pltpu.VMEM((2, 2 * HD, length), BF16),
            score=pltpu.VMEM((2, length, QUERY_BLOCK), F32),
            gprob=pltpu.VMEM((2, length, QUERY_BLOCK), F32),
            weight=pltpu.VMEM((2, length, QUERY_BLOCK), BF16),
            gprod=pltpu.VMEM((2, length, QUERY_BLOCK), BF16),
            dq=pltpu.VMEM((2, HD, length), F32),
            dk=pltpu.VMEM((2, HD, length), F32),
            dv=pltpu.VMEM((2, HD, length), F32),
            ctxt=pltpu.VMEM((2 * HD, length), BF16),
            ctx=pltpu.VMEM((length, 2 * HD), BF16),
            gmt=pltpu.VMEM((6 * HD, length), BF16),
            gm=pltpu.VMEM((length, 6 * HD), BF16),
        )

    @staticmethod
    def bias_shape(width):
        return (6 * HD, 128)

    @staticmethod
    def cost(length, features, width):
        return 6 * length * features * width + 14 * length * length * 2 * HD, 2 * length**2

    @staticmethod
    def compute(m, norm, cot, w, bias, bias_sums, table):
        length = norm.shape[0]
        heads = 6 * HD
        scale = np.float32(HD ** (-0.5))
        values = sum(table[k * 8 : (k + 1) * 8, :].astype(F32) for k in range(3))
        cosine, sine = values[:, :length], values[:, length:]
        start = table[24:25, :length].astype(F32) * 256.0 + table[24:25, length:].astype(F32)
        for block in range(length // QUERY_BLOCK):
            width = (block + 1) * QUERY_BLOCK
            lanes = slice(block * QUERY_BLOCK, width)
            key_at = lax.broadcasted_iota(jnp.int32, (width, QUERY_BLOCK), 0)
            query_at = lax.broadcasted_iota(jnp.int32, (width, QUERY_BLOCK), 1)
            first = start[:, lanes].astype(jnp.int32)
            allowed = (key_at >= first) & (key_at <= query_at + block * QUERY_BLOCK)
            m.mask[block, :width, :] = jnp.where(allowed, 0.0, NEGATIVE)

        column = jnp.broadcast_to(bias[...], (128, heads)).T
        projected = dot_nt(w[:heads, :], norm[...]) + widen(column, length)
        grad_context = dot_nt(w[heads:, :], cot[...]).astype(BF16)
        nothing = jnp.zeros((HD, length), BF16)
        for h in range(2):
            query, key, value = [
                projected[(3 * h + k) * HD : (3 * h + k + 1) * HD] for k in range(3)
            ]
            m.q[h, :HD, :] = (rotate_rows(query, cosine, sine) * scale).astype(BF16)
            m.q[h, HD:, :] = nothing
            m.d[h, :HD, :] = nothing
            m.d[h, HD:, :] = grad_context[h * HD : (h + 1) * HD]
            both = jnp.concatenate([rotate_rows(key, cosine, sine), value], axis=0).astype(BF16)
            m.kvt[h] = both
            m.kv[h] = both.T

        items = [
            (block, h) for block in reversed(range(length // QUERY_BLOCK)) for h in range(2)
        ]

        def place(item):
            block = items[item][0]
            width = (block + 1) * QUERY_BLOCK
            return *items[item], width, slice(block * QUERY_BLOCK, width)

        def products(item):
            _, h, width, lanes = place(item)
            key_value = m.kv[h, :width, :]
            m.score[item % 2, :width, :] = dot_nn(key_value, m.q[h, :, lanes])
            m.gprob[item % 2, :width, :] = dot_nn(key_value, m.d[h, :, lanes])

        def softmax(item):
            block, _, width, _ = place(item)
            scores = m.score[item % 2, :width, :] + m.mask[block, :width, :]
            highest = jnp.max(scores, axis=0, keepdims=True)
            numerators = jnp.exp(scores - highest)
            weights = numerators * (1.0 / jnp.sum(numerators, axis=0, keepdims=True))
            grad_probs = m.gprob[item % 2, :width, :]
            centre = jnp.sum(grad_probs * weights, axis=0, keepdims=True)
            m.weight[item % 2, :width, :] = weights.astype(BF16)
            m.gprod[item % 2, :width, :] = (weights * (grad_probs - centre)).astype(BF16)

        def results(item):
            _, h, width, lanes = place(item)
            weights_low = m.weight[item % 2, :width, :]
            grad_products = m.gprod[item % 2, :width, :]
            context = dot_nn(m.kvt[h, HD:, :width], weights_low)
            m.ctxt[h * HD : (h + 1) * HD, lanes] = context.astype(BF16)
            grad_query = dot_nn(m.kvt[h, :HD, :width], grad_products)
            m.dq[h, :, lanes] = grad_query * scale
            grad_key = dot_nt(m.q[h, :HD, lanes], grad_products)
            grad_value = dot_nt(m.d[h, HD:, lanes], weights_low)
            if width == length:
                m.dk[h] = grad_key
                m.dv[h] = grad_value
            else:
                m.dk[h, :, :width] += grad_key
                m.dv[h, :, :width] += grad_value

        products(0)
        for item in range(len(items)):
            if item + 1 < len(items):
                products(item + 1)
            if item:
                results(item - 1)
            softmax(item)
        results(len(items) - 1)

        for h in range(2):
            parts = [
                rotate_rows(m.dq[h], cosine, -sine),
                rotate_rows(m.dk[h], cosine, -sine),
                m.dv[h],
            ]
            for k, part in enumerate(parts):
                rows = slice((3 * h + k) * HD, (3 * h + k + 1) * HD)
                low = part.astype(BF16)
                m.gmt[rows, :] = low
                bias_sums[rows, :] += fold_lanes(low.astype(F32))
        m.gm[...] = m.gmt[...].T
        m.ctx[...] = m.ctxt[...].T

    @staticmethod
    def accumulate(m, norm, cot, total):
        heads = 6 * HD
        total[0, :heads, :] += dot_nn(m.gmt[...], norm[...])
        total[0, heads:, :] += dot_nn(m.ctxt[...], cot[...])

    @staticmethod
    def forward_out(m, w, cols):
        return dot_nn(m.ctx[...], w[6 * HD :, cols])

    @staticmethod
    def backward_out(m, w, cols):
        return dot_nn(m.gm[...], w[: 6 * HD, cols])


class Mlp:
    picks = (0, 1)
    turns = False

    @staticmethod
    def scratch(length, features, width):
        return dict(
            hid=pltpu.VMEM((2, length, width), F32),
            act=pltpu.VMEM((length, width), BF16),
            dh=pltpu.VMEM((length, width), BF16),
        )

    @staticmethod
    def bias_shape(width):
        return (8, width)

    @staticmethod
    def cost(length, features, width):
        return 12 * length * features * width, 2 * length * width

    @staticmethod
    def compute(m, norm, cot, w, bias, bias_sums, table):
        m.hid[0] = dot_nn(norm[...], w[0]) + bias[...]
        m.hid[1] = dot_nn(cot[...], w[1])
        for rows in row_chunks(norm.shape[0]):
            hid = m.hid[0, rows, :]
            below = 0.5 + 0.5 * lax.erf(hid * np.float32(0.5**0.5))
            slope = below + hid * jnp.exp(-0.5 * (hid * hid)) * np.float32((2 * np.pi) ** -0.5)
            m.act[rows, :] = (hid * below).astype(BF16)
            grad_hid = (slope * m.hid[1, rows, :]).astype(BF16)
            m.dh[rows, :] = grad_hid
            bias_sums[...] += fold_rows(grad_hid.astype(F32))

    @staticmethod
    def accumulate(m, norm, cot, total):
        total[0] += dot_tn(m.dh[...], norm[...])
        total[1] += dot_tn(m.act[...], cot[...])

    @staticmethod
    def forward_out(m, w, cols):
        return dot_nt(m.act[...], w[1, cols, :])

    @staticmethod
    def backward_out(m, w, cols):
        return dot_nt(m.dh[...], w[0, cols, :])


def branch_body(kind, names, n_seq, count, is_first, is_last, places, *refs):
    refs = list(refs)
    take = lambda number: [refs.pop(0) for _ in range(number)]
    (meta, gain, shift, bias) = take(4)
    messages = [take(4) for _ in range(n_seq)]
    partials = [take(2) for _ in places or ()]
    reads_turned = kind.turns and not is_first
    blocks = take(1 if reads_turned else count)
    carried = [] if is_first else take(3)
    outs = take(2 * n_seq if places else 2)
    sums, bias_sums = take(2)
    if is_last:
        grads = take(count)
    else:
        (total_hbm,) = take(1)
        if kind.turns:
            (turned_hbm,) = take(1) if is_first else (None,)
    x_s, d_s, tab_s, w_s, total, norm_s, hat_s, out_st, grad_st = take(9)
    wt_s = take(1)[0] if kind.turns else None
    turned = take(1)[0] if is_last else None
    m = SimpleNamespace(**dict(zip(names, take(len(names)))))
    token_sem, table_sem, weight_sem, part_sem, out_sem, total_sem = take(6)

    length, features = x_s.shape[1:]
    half = length // 2
    mine = pl.multiple_of(meta[0] * half, half)
    other = pl.multiple_of((1 - meta[0]) * half, half)
    rows = features // (QUAD * count)

    weight_copies = []
    if reads_turned:
        weight_copies.append(pltpu.make_async_copy(blocks[0], wt_s, weight_sem.at[0, 0, 0]))
    else:
        for k in range(count):
            for j in range(QUAD):
                place = (meta[2] ^ k) * (QUAD * rows) + (meta[1] ^ j) * rows
                for number, pick in enumerate(kind.picks):
                    source = blocks[k].at[j] if pick is None else blocks[k].at[j, pick]
                    target = w_s.at[number, pl.ds(pl.multiple_of(place, rows), rows)]
                    weight_copies.append(
                        pltpu.make_async_copy(source, target, weight_sem.at[number, k, j])
                    )

    def start_message(i, target, first, which):
        for number, place in enumerate((mine, other)):
            pltpu.make_async_copy(
                messages[i][first + number].at[pl.ds(0, half)],
                target.at[i, pl.ds(place, half)],
                token_sem.at[i, which, number],
            ).start()

    def start_rest(i):
        start_message(i, d_s, 2, 1)
        if kind.turns:
            pltpu.make_async_copy(
                messages[i][0].at[pl.ds(half, TABLE_ROWS)], tab_s.at[i], table_sem.at[i]
            ).start()
        if i == 0:
            for copy in weight_copies:
                copy.start()

    def start_partials(i):
        if places:
            for number, stage in enumerate((out_st, grad_st)):
                pltpu.make_async_copy(
                    partials[i][number].at[places[i]], stage.at[i], part_sem.at[i, number]
                ).start()

    start_message(0, x_s, 0, 0)
    if is_first:
        total[...] = jnp.zeros_like(total)
        sums[...] = jnp.zeros_like(sums)
        bias_sums[...] = jnp.zeros_like(bias_sums)
    else:
        load = pltpu.make_async_copy(carried[0], total, total_sem.at[0])
        sums[...] = carried[1][...]
        bias_sums[...] = carried[2][...]
    saves = []
    if not is_last:
        saves.append(pltpu.make_async_copy(total, total_hbm, total_sem.at[1]))
        if kind.turns and is_first:
            keep = pltpu.make_async_copy(wt_s, turned_hbm, total_sem.at[2])

    def stores(stage, i, which):
        if not places:
            return [pltpu.make_async_copy(stage.at[i], outs[which].at[i], out_sem.at[i, which, 0])]
        return [
            pltpu.make_async_copy(
                stage.at[i, pl.ds(place, half)],
                outs[2 * i + number].at[which],
                out_sem.at[i, which, number],
            )
            for number, place in enumerate((mine, other))
        ]

    def start_stores(stage, i, which):
        if not places or n_seq == 1:
            for copy in stores(stage, i, which):
                copy.start()
            return
        for k in range(n_seq):

            @pl.when(i == k)
            def _(k=k):
                for copy in stores(stage, k, which):
                    copy.start()

    def one_sequence(i, carry):
        for number in range(2):
            wait_bytes(x_s.at[i, pl.ds(0, half)], token_sem.at[i, 0, number])

        @pl.when(i == 0)
        def _():
            start_rest(0)

        normalize(x_s.at[i], gain, shift, norm_s, hat_s)
        if kind.turns:
            wait_bytes(tab_s.at[i], table_sem.at[i])
        for number in range(2):
            wait_bytes(d_s.at[i, pl.ds(0, half)], token_sem.at[i, 1, number])

        @pl.when(i == 0)
        def _():
            for copy in weight_copies:
                copy.wait()
            if not is_first:
                load.start()
            for later in range(1, n_seq):
                start_message(later, x_s, 0, 0)
                start_rest(later)
            for later in range(n_seq):
                start_partials(later)
            if kind.turns and is_first:
                for cols in column_chunks(features):
                    wt_s[:, cols] = w_s[0, cols, :].T
                if not is_last:
                    keep.start()

        cot = d_s.at[i]
        w = wt_s if kind.turns else w_s
        kind.compute(m, norm_s, cot, w, bias, bias_sums, tab_s.at[i])
        if not is_first:

            @pl.when(i == 0)
            def _():
                load.wait()

        kind.accumulate(m, norm_s, cot, total)
        if not is_last:

            @pl.when(i == n_seq - 1)
            def _():
                for copy in saves:
                    copy.start()

        if places:
            wait_bytes(out_st.at[i], part_sem.at[i, 0])
            wait_bytes(grad_st.at[i], part_sem.at[i, 1])
        for cols in column_chunks(features):
            out = kind.forward_out(m, w, cols)
            if places:
                out = out + out_st[i, :, cols].astype(F32)
            out_st[i, :, cols] = out.astype(BF16)
        start_stores(out_st, i, 0)
        for cols in column_chunks(features):
            grad = kind.backward_out(m, w, cols)
            sums[0:8, cols] += fold_rows(grad * hat_s[:, cols])
            sums[8:16, cols] += fold_rows(grad)
            whole = grad * gain[:, cols]
            if places:
                whole = whole + grad_st[i, :, cols].astype(F32)
            grad_st[i, :, cols] = whole.astype(BF16)
        start_stores(grad_st, i, 1)
        return carry

    if n_seq == 1:
        one_sequence(0, 0)
    else:
        lax.fori_loop(0, n_seq, one_sequence, 0)
    if is_last:
        for number, pick in enumerate(kind.picks):
            for cols in column_chunks(features):
                turned[cols, :] = total[number, :, cols].T
            for k in range(count):
                for j in range(QUAD):
                    place = (meta[2] ^ k) * (QUAD * rows) + (meta[1] ^ j) * rows
                    piece = turned[pl.ds(pl.multiple_of(place, rows), rows), :]
                    at = (j,) if pick is None else (j, pick)
                    grads[k][at] = piece.astype(grads[k].dtype)
    for copy in saves:
        copy.wait()
    if kind.turns and is_first and not is_last:
        keep.wait()
    for i in range(n_seq):
        for copy in stores(out_st, i, 0) + stores(grad_st, i, 1):
            copy.wait()


def branch(kind, meta, gain, shift, bias, messages, partials, blocks, carried, is_last):
    n_seq, count, is_first = len(messages), len(blocks), carried is None
    half = messages[0][2].shape[0]
    features = messages[0][0].shape[1]
    length = 2 * half
    width = blocks[0].shape[-1]
    n_pick = len(kind.picks)
    operands = [meta, gain, shift, bias]
    specs = [SMEM] + [VMEM] * 3
    for pair in messages:
        operands += list(pair)
        specs += [ANY] * 4
    for part in partials:
        operands += list(part[:2])
        specs += [HBM] * 2
    places = [part[2] for part in partials]
    if kind.turns and not is_first:
        operands += [carried[3]]
        specs += [HBM]
    else:
        operands += list(blocks)
        specs += [HBM] * count
    if not is_first:
        operands += list(carried[:3])
        specs += [HBM, VMEM, VMEM]
    if places:
        shapes = [jax.ShapeDtypeStruct((2, half, features), BF16)] * (2 * n_seq)
    else:
        shapes = [jax.ShapeDtypeStruct((n_seq, length, features), BF16)] * 2
    n_out = len(shapes)
    shapes += [
        jax.ShapeDtypeStruct((16, features), F32),
        jax.ShapeDtypeStruct(kind.bias_shape(width), F32),
    ]
    out_specs = [HBM] * n_out + [VMEM, VMEM]
    if is_last:
        shape = blocks[0].shape
        shapes += [jax.ShapeDtypeStruct(shape, BF16 if k else F32) for k in range(count)]
        out_specs += [VMEM] * count
    else:
        shapes += [jax.ShapeDtypeStruct((n_pick, width, features), F32)]
        out_specs += [HBM]
        if kind.turns and is_first:
            shapes += [jax.ShapeDtypeStruct((width, features), BF16)]
            out_specs += [HBM]
    scratch = [
        pltpu.VMEM((n_seq, length, features), BF16),
        pltpu.VMEM((n_seq, length, features), BF16),
        pltpu.VMEM((n_seq, TABLE_ROWS, features), BF16),
        pltpu.VMEM((n_pick, features, width), BF16),
        pltpu.VMEM((n_pick, width, features), F32),
        pltpu.VMEM((length, features), BF16),
        pltpu.VMEM((length, features), F32),
        pltpu.VMEM((n_seq, length, features), BF16),
        pltpu.VMEM((n_seq, length, features), BF16),
    ]
    if kind.turns:
        scratch += [pltpu.VMEM((width, features), BF16)]
    if is_last:
        scratch += [pltpu.VMEM((features, width), F32)]
    named = kind.scratch(length, features, width)
    scratch += list(named.values())
    scratch += [
        pltpu.SemaphoreType.DMA((n_seq, 2, 2)),
        pltpu.SemaphoreType.DMA((n_seq,)),
        pltpu.SemaphoreType.DMA((n_pick, count, QUAD)),
        pltpu.SemaphoreType.DMA((n_seq, 2)),
        pltpu.SemaphoreType.DMA((n_seq, 2, 2)),
        pltpu.SemaphoreType.DMA((3,)),
    ]
    flops, transcendentals = kind.cost(length, features, width)
    names = tuple(named)

    def body(*refs):
        branch_body(kind, names, n_seq, count, is_first, is_last, places, *refs)

    call = pl.pallas_call(
        body,
        in_specs=specs,
        out_specs=out_specs,
        out_shape=shapes,
        scratch_shapes=scratch,
        cost_estimate=pl.CostEstimate(
            flops=n_seq * flops,
            bytes_accessed=n_seq * 8 * length * features + 10 * n_pick * width * features,
            transcendentals=n_seq * transcendentals,
        ),
    )
    results = call(*operands)
    outs, sums, rest = results[:n_out], results[n_out : n_out + 2], results[n_out + 2 :]
    if is_last:
        return outs, sums, rest
    turned = () if not kind.turns else (rest[1] if is_first else carried[3],)
    return outs, sums, (rest[0], *sums, *turned)


def finish_body(first_bias, second_bias, x, d, mine, other, p1, p2, p3, out, grad):
    bias = first_bias[...] + second_bias[...]

    def some_rows(number, carry):
        rows = pl.ds(pl.multiple_of(number * ROW_CHUNK, ROW_CHUNK), ROW_CHUNK)

        def total(which):
            own = mine[which, rows, :].astype(F32) + other[which, rows, :].astype(F32)
            pair = p2[which, rows, :].astype(F32) + p3[which, rows, :].astype(F32)
            return own + p1[which, rows, :].astype(F32) + pair

        tokens = x[rows, :].astype(F32)
        out[rows, :] = (tokens + total(0) + bias).astype(BF16)
        back = total(1)
        share = np.float32(1.0 / tokens.shape[1])
        mean = lambda value: jnp.sum(fold_lanes(value), axis=-1, keepdims=True) * share
        centred = tokens - mean(tokens)
        inverse = lax.rsqrt(mean(centred * centred) + EPSILON)
        scaled = centred * inverse
        change = (back - mean(back) - scaled * mean(back * scaled)) * inverse
        grad[rows, :] = (d[rows, :].astype(F32) + change).astype(BF16)
        return carry

    lax.fori_loop(0, x.shape[0] // ROW_CHUNK, some_rows, 0, unroll=2)


def finish(x, d, own, parts, first_bias, second_bias):
    shapes = [jax.ShapeDtypeStruct(x.shape, BF16)] * 2
    arrays = [first_bias, second_bias, x, d, *own, *parts]
    return staged_call(finish_body, [], arrays, shapes)


def on_device(
    n_dp,
    inputs,
    segment_ids,
    positions,
    first_gain,
    first_shift,
    second_gain,
    second_shift,
    attend_weight,
    attend_bias,
    project_weight,
    project_bias,
    expand_weight,
    expand_bias,
    shrink_weight,
    shrink_bias,
    output_grad,
):
    count = n_dp // QUAD
    features = inputs.shape[1]
    attend_cols, hidden_cols = attend_weight.shape[1], expand_weight.shape[1]
    project_cols = project_weight.shape[0]
    core = lax.axis_index("tensor").astype(jnp.int32)
    dp_at = lax.axis_index("dp").astype(jnp.int32)
    quarter = dp_at % QUAD
    meta = jnp.stack([core, quarter, dp_at // QUAD])

    def to_quad(value, j):
        return lax.ppermute(value, "dp", xor_pairs(n_dp, j))

    def to_layer(value, bits):
        return lax.ppermute(value, "dp", xor_pairs(n_dp, bits * QUAD))

    def gather_layers(block):
        blocks = {0: block}
        bit = count // 2
        while bit:
            for k in sorted(blocks):
                blocks[k | bit] = to_layer(blocks[k], bit)
            bit //= 2
        return [blocks[k] for k in range(count)]

    def gather_direct(block):
        return [block] + [to_layer(block, k) for k in range(1, count)]

    halfway = ROT // 2
    frequency = 1.0 / 10000.0 ** (jnp.arange(halfway, dtype=F32) * (2.0 / ROT))
    angles = frequency[:, None] * positions.astype(F32)[None, :]
    earlier = segment_ids[None, :] < segment_ids[:, None]
    start = jnp.sum(earlier.astype(jnp.int32), axis=1)
    start = jnp.concatenate([start // 256, start % 256]).astype(BF16)
    turns = jnp.concatenate([jnp.cos(angles), jnp.sin(angles)], axis=1)
    message, cotangent_sum = join_message(
        output_grad, inputs, *low_parts(turns, 3), jnp.broadcast_to(start[None], turns.shape)
    )

    first_pack, second_pack = pack_weights(
        meta, attend_weight, project_weight.T, expand_weight, shrink_weight.T
    )
    second_parts = [second_pack[0]]
    second_parts += [to_quad(second_pack[j], j) for j in range(1, QUAD)]
    second_blocks = gather_direct(jnp.stack(second_parts))
    first_parts = [first_pack[0]] + [to_quad(first_pack[j], j) for j in range(1, QUAD)]
    first_blocks = gather_layers(jnp.stack(first_parts))

    rows_a = [message] + [to_quad(message, j) for j in (1, 2)]
    rows_b = [output_grad] + [to_quad(output_grad, j) for j in (1, 2)]
    rows_a.append(to_quad(rows_a[2], 1))
    rows_b.append(to_quad(rows_b[1], 2))
    messages = [(a, swap_cores(a), b, swap_cores(b)) for a, b in zip(rows_a, rows_b)]

    one_row = lambda vector: vector[None, :]
    bias_part = lax.dynamic_index_in_dim(
        attend_bias.reshape(QUAD, attend_cols // QUAD), quarter, 0, True
    )
    hidden_part = lax.dynamic_index_in_dim(
        expand_bias.reshape(QUAD, hidden_cols // QUAD), quarter, 0, True
    )

    carried, partials = None, {}
    for group in ATTEND_GROUPS:
        results = branch(
            Attend,
            meta,
            one_row(first_gain),
            one_row(first_shift),
            bias_part,
            [messages[s] for s in group],
            [],
            first_blocks,
            carried,
            group is ATTEND_GROUPS[-1],
        )
        (out_part, grad_part), attend_sums, carried = results
        for place, s in enumerate(group):
            partials[s] = (out_part, grad_part, place)
    attend_grads = carried

    carried, sums_of = None, {}
    for group in MLP_GROUPS:
        results = branch(
            Mlp,
            meta,
            one_row(second_gain),
            one_row(second_shift),
            hidden_part,
            [messages[s] for s in group],
            [partials[s] for s in group],
            second_blocks,
            carried,
            group is MLP_GROUPS[-1],
        )
        outs, mlp_sums, carried = results
        for place, s in enumerate(group):
            mine, other = outs[2 * place], swap_cores(outs[2 * place + 1])
            if s == 0:
                own_halves = mine, other
                continue
            sums_of[s] = add_halves(mine, other)
    mlp_grads = carried

    parts = [to_quad(sums_of[j], j) for j in range(1, QUAD)]
    outputs, grad_inputs = finish(
        inputs, output_grad, own_halves, parts, one_row(project_bias), one_row(shrink_bias)
    )

    def reduce_layers(grads, relayed):
        if relayed:
            far = to_layer(grads[3], 1)
            near = to_layer(grads[1], 1)
            middle = (far.astype(F32) + grads[2].astype(F32)).astype(BF16)
            received = [near, to_layer(middle, 2)]
        else:
            received = [to_layer(grads[k], k) for k in range(1, count)]
        parts = sum_layers(grads[0], received)
        return parts[0], [to_quad(parts[j], j) for j in range(1, QUAD)]

    own, received = reduce_layers(attend_grads, False)
    grad_attend, grad_project = unpack_attend(meta, own, received, attend_cols, project_cols)
    own, received = reduce_layers(mlp_grads, count == 4)
    grad_expand, grad_shrink = unpack_mlp(meta, own, received, hidden_cols)

    sizes = [features] * 4 + [features] * 2 + [2 * attend_cols, 2 * hidden_cols]
    vector = join_vector(meta, *attend_sums, *mlp_sums, cotangent_sum, sizes)
    vector = vector + swap_cores(vector)
    near = [to_quad(vector, j) for j in range(1, QUAD)]
    vector = (vector + near[0]) + (near[1] + near[2])
    vectors = [vector] + [to_layer(vector, k) for k in range(1, count)]
    pieces = split_vector(vectors, sizes)
    return (
        outputs,
        grad_inputs,
        *pieces[:4],
        grad_attend,
        pieces[6],
        grad_project.T,
        pieces[4],
        grad_expand,
        pieces[7],
        grad_shrink.T,
        pieces[5],
    )


def solution(mesh):
    n_dp = mesh.shape["dp"]
    assert mesh.shape["tensor"] == 2 and n_dp % QUAD == 0 and n_dp & (n_dp - 1) == 0
    rows = P(("dp", "tensor"), None)
    in_specs = (
        rows,
        P("dp"),
        P("dp"),
        P(),
        P(),
        P(),
        P(),
        P("dp", "tensor"),
        P("tensor"),
        P("tensor", "dp"),
        P(),
        P("dp", "tensor"),
        P("tensor"),
        P("tensor", "dp"),
        P(),
        rows,
    )
    out_specs = (
        rows,
        rows,
        P(),
        P(),
        P(),
        P(),
        P("dp", "tensor"),
        P(),
        P("tensor", "dp"),
        P(),
        P("dp", "tensor"),
        P(),
        P("tensor", "dp"),
        P(),
    )

    def program(*args):
        return on_device(n_dp, *args)

    return jax.shard_map(
        program, mesh=mesh, in_specs=in_specs, out_specs=out_specs, check_vma=False
    )
```
